32 devices in a mesh: grp: 2 (over core), cores: 16 (over z, y, x).
Axes of the slice: x: 2, y: 2, z: 4, core: 2. Of those that a mesh axis runs over, the one named last changes fastest.
Arguments:
- rhs_core: float32 [4, 8192], P(None, 'cores'), may hold values from -6 to 6
- rhs_noncore: float32 [4, 8192], P(None, ('grp', 'cores')), may hold values from -6 to 6
- records_core: float32 [4, 8192], P(None, 'cores'), may hold values from 0.2 to 2
- records_noncore: float32 [4, 8192], P(None, ('grp', 'cores')), may hold values from 0.2 to 2
- core_inverse: bfloat16 [8192, 8192], P('cores'), as said below
- genomic_block: bfloat16 [8192, 8192], P(('grp', 'cores')), may hold values from -0.125 to 0.125
- m_inverse: float32 [8192], P(('grp', 'cores')), may hold values from 0.5 to 4
- trait_inverse: float32 [4, 4], replicated, as said below
Outputs:
- sol_core: float32 [4, 8192], P(None, 'cores')
- sol_noncore: float32 [4, 8192], P(None, ('grp', 'cores'))
- res_core: float32 [4, 8192], P(None, 'cores')
- res_noncore: float32 [4, 8192], P(None, ('grp', 'cores'))
The draws below stay inside these ranges and needn't reach their ends.
Inputs may be any that keep to these rules, and one draw needn't show every extreme that they name: core_inverse is symmetric and positive definite. trait_inverse is symmetric and positive definite.
All inputs are finite; a program needn't handle non-finite values.
Results may differ from the reference program's by a relative error of at most 0.028.
Values may be sent and summed in bfloat16 or wider, within the bound.
No kernel may reach another device: no remote copies, remote signals or barrier semaphores. Data moves between devices by JAX's collectives and lax.ppermute only.
A program may use at most 64 MiB of HBM per device.

```python
import math
import jax
import jax.numpy as jnp
from jax import lax

TRAITS = 4
CORE = 8192
ITERS = 2
NONCORE = 8192


def draw_core_inverse(key, part):
    base = jax.random.normal(jax.random.fold_in(key, 11), (CORE, CORE), jnp.float32)
    diag_vals = 1.2 + 1.3 * jax.random.uniform(jax.random.fold_in(key, 12), (CORE,), jnp.float32)
    offdiag = (base + base.T) * (0.45 / jnp.sqrt(2.0 * CORE))
    eye_mask = jnp.eye(CORE, dtype=jnp.float32)
    full = offdiag * (1.0 - eye_mask) + eye_mask * diag_vals[None, :]
    return full.astype(jnp.bfloat16)


def draw_trait_inverse(key, part):
    base = 0.5 * jax.random.normal(jax.random.fold_in(key, 21), (TRAITS, TRAITS), jnp.float32)
    return jnp.dot(base, base.T) + 0.5 * jnp.eye(TRAITS, dtype=jnp.float32)


def with_spikes(array, rng, source, target, blocks, factor):
    def block_of(axis_at):
        return (jnp.arange(array.shape[axis_at]) // (array.shape[axis_at] // blocks)).reshape((-1,) + (1,) * (array.ndim - 1 - axis_at))

    one_side = jax.random.permutation(rng, blocks)[block_of(target)]
    far = (block_of(target) + blocks // 2) % blocks
    return jnp.where((block_of(source) == one_side) | (block_of(source) == far), factor * array, array)


def block_scale(stream_key, shape, split, least, high):
    def one(dim, blocks):
        heights = jax.random.uniform(jax.random.fold_in(jax.random.fold_in(stream_key, 6), dim), (blocks,), jnp.float32, least / len(split), high / len(split))
        return jnp.repeat(jnp.exp(heights), shape[dim] // blocks).reshape((-1,) + (1,) * (len(shape) - dim - 1))

    factor_of = one(*split[0])
    for cut in split[1:]:
        factor_of = factor_of * one(*cut)
    return factor_of


def centred(own_key, shape, width, limit, pieces=(), held_as=jnp.bfloat16):
    values = width * jax.random.normal(own_key, shape, jnp.float32)
    if pieces:
        values = values * block_scale(own_key, shape, pieces, -0.22, 0.18)
    return jnp.clip(values, -limit, limit).astype(held_as)


def heavy_noise(stream_key, dims, width, limit, pieces, heavy, kind=jnp.bfloat16):
    values = width * jax.random.normal(stream_key, dims, jnp.float32)
    if pieces:
        values = values * block_scale(stream_key, dims, pieces, -0.22, 0.18)
    return jnp.clip(with_spikes(values, jax.random.fold_in(stream_key, 3), *heavy), -limit, limit).astype(kind)


def setup_inputs(seed: int = 0) -> dict:
    keys = jax.random.split(jax.random.key(seed), 9)
    return {
        "rhs_core": centred(keys[0], (TRAITS, CORE), 1.0, 6.0, ((1, 16),), jnp.float32),
        "rhs_noncore": centred(keys[1], (TRAITS, NONCORE), 1.0, 6.0, ((1, 32),), jnp.float32),
        "records_core": jnp.clip(jnp.exp(math.log(2.0) - 2.3025851 * jax.random.uniform(keys[2], (TRAITS, CORE), jnp.float32) ** block_scale(keys[2], (TRAITS, CORE), ((1, 16),), -0.2, 0.2)), 0.2, 2.0),
        "records_noncore": jnp.clip(jnp.exp(math.log(2.0) - 2.3025851 * jax.random.uniform(keys[3], (TRAITS, NONCORE), jnp.float32) ** block_scale(keys[3], (TRAITS, NONCORE), ((1, 32),), -0.2, 0.2)), 0.2, 2.0),
        "core_inverse": draw_core_inverse(jax.random.fold_in(keys[8], 71), 0),
        "genomic_block": heavy_noise(keys[5], (NONCORE, CORE), NONCORE ** -0.5, 0.125, ((0, 32),), (0, 1, 32, 2.75)),
        "m_inverse": jnp.clip(jnp.exp(math.log(4.0) - 2.0794415 * jax.random.uniform(keys[6], (NONCORE,), jnp.float32) ** block_scale(keys[6], (NONCORE,), ((0, 32),), -0.2, 0.2)), 0.5, 4.0),
        "trait_inverse": draw_trait_inverse(jax.random.fold_in(keys[8], 71), 0),
    }


def genomic_map(core_vec, non_vec, core_inverse, genomic_block, m_inverse):
    mapped = jnp.dot(core_vec.astype(jnp.bfloat16), core_inverse, preferred_element_type=jnp.float32)
    mapped_in = mapped.astype(jnp.bfloat16)
    pulled = lax.dot_general(mapped_in, genomic_block, (((1,), (1,)), ((), ())), preferred_element_type=jnp.float32)
    scaled = m_inverse[None, :] * (non_vec - pulled)
    pushed = jnp.dot(scaled.astype(jnp.bfloat16), genomic_block, preferred_element_type=jnp.float32)
    core_out = jnp.dot((core_vec - pushed).astype(jnp.bfloat16), core_inverse, preferred_element_type=jnp.float32)
    return core_out, scaled


def reference(rhs_core, rhs_noncore, records_core, records_noncore, core_inverse, genomic_block, m_inverse, trait_inverse):
    hp = lax.Precision.HIGHEST
    trait_diag = jnp.diagonal(trait_inverse)[:, None]
    prec_core = 1.0 / (records_core + trait_diag)
    prec_non = 1.0 / (records_noncore + trait_diag * m_inverse[None, :])
    sol_core = jnp.zeros_like(rhs_core)
    sol_non = jnp.zeros_like(rhs_noncore)
    res_core, res_non = rhs_core, rhs_noncore
    z_core, z_non = prec_core * res_core, prec_non * res_non
    dir_core, dir_non = z_core, z_non
    rz_now = jnp.sum(res_core * z_core) + jnp.sum(res_non * z_non)
    for iteration in range(ITERS):
        core_out, non_out = genomic_map(dir_core, dir_non, core_inverse, genomic_block, m_inverse)
        image_core = records_core * dir_core + jnp.dot(trait_inverse, core_out, precision=hp)
        image_non = records_noncore * dir_non + jnp.dot(trait_inverse, non_out, precision=hp)
        step_size = rz_now / (jnp.sum(dir_core * image_core) + jnp.sum(dir_non * image_non))
        sol_core = sol_core + step_size * dir_core
        sol_non = sol_non + step_size * dir_non
        res_core = res_core - step_size * image_core
        res_non = res_non - step_size * image_non
        z_core, z_non = prec_core * res_core, prec_non * res_non
        rz_next = jnp.sum(res_core * z_core) + jnp.sum(res_non * z_non)
        factor = rz_next / rz_now
        dir_core = z_core + factor * dir_core
        dir_non = z_non + factor * dir_non
        rz_now = rz_next
    return sol_core, sol_non, res_core, res_non
```

```python
import jax
import jax.numpy as jnp
from jax import lax
from jax.sharding import PartitionSpec as P

ITERS = 2
AXES = ("cores", "grp")


def split3(value):
    hi = lax.reduce_precision(value, 8, 7)
    mid = lax.reduce_precision(value - hi, 8, 7)
    low = value - hi - mid
    return jnp.stack([hi, mid, low]).astype(jnp.bfloat16)


def mix(trait_inverse, x):
    return sum(trait_inverse[:, s : s + 1] * x[s : s + 1, :] for s in range(x.shape[0]))


def make_body(groups, cores):
    parts = groups * cores

    def exchange(blocks):
        return lax.all_to_all(blocks, AXES, 0, 0, tiled=False)

    def gather(own, scalars=()):
        traits, width = own.shape
        sent = own.astype(jnp.bfloat16)
        if scalars:
            row = jnp.concatenate([split3(s) for s in scalars])
            row = jnp.pad(row, (0, 128 - row.shape[0]))[None]
            sent = jnp.concatenate([sent, jnp.pad(row, ((0, traits - 1), (0, 0)))], axis=1)
        got = exchange(jnp.broadcast_to(sent[None], (parts,) + sent.shape))
        full = got[:, :, :width].transpose(1, 0, 2).reshape(traits, parts * width)
        if not scalars:
            return full
        tail = got[:, 0, width : width + 3 * len(scalars)].astype(jnp.float32)
        sums = tail.reshape(parts, len(scalars), 3).sum((0, 2))
        return full, sums

    def scatter(partial, width):
        traits = partial.shape[0]
        blocks = partial.astype(jnp.bfloat16).reshape(traits, parts, width).transpose(1, 0, 2)
        return exchange(blocks).astype(jnp.float32).sum(0)

    def times_rows(full, rows):
        return lax.dot_general(full, rows, (((1,), (1,)), ((), ())), preferred_element_type=jnp.float32)

    def body(rhs_core, rhs_non, rec_core, rec_non, core_inverse, block, m_inverse, trait_inverse):
        traits, held = rhs_core.shape
        width = held // groups
        at = lax.axis_index("grp") * width

        def mine(x):
            return lax.dynamic_slice_in_dim(x, at, width, axis=1)

        rows_mine = lax.dynamic_slice_in_dim(core_inverse, at, width, axis=0)
        m_row = m_inverse[None, :]
        trait_diag = jnp.diagonal(trait_inverse)[:, None]
        prec_core = 1.0 / (rec_core + trait_diag)
        prec_non = 1.0 / (rec_non + trait_diag * m_row)
        sol_core, sol_non = jnp.zeros_like(rhs_core), jnp.zeros_like(rhs_non)
        res_core, res_non = rhs_core, rhs_non
        z_core, z_non = prec_core * res_core, prec_non * res_non
        dir_core, dir_non = jnp.zeros_like(z_core), jnp.zeros_like(z_non)
        mapped = jnp.zeros((traits, width), jnp.float32)
        rz_old = None
        for iteration in range(ITERS):
            rz_part = jnp.sum(res_non * z_non) + jnp.sum(mine(res_core * z_core))
            z_full, (rz,) = gather(mine(z_core), (rz_part,))
            z_mapped = times_rows(z_full, rows_mine)
            if iteration:
                factor = rz / rz_old
                mapped = z_mapped + factor * mapped
                dir_core = z_core + factor * dir_core
                dir_non = z_non + factor * dir_non
            else:
                mapped, dir_core, dir_non = z_mapped, z_core, z_non
            rz_old = rz
            mapped_full = gather(mapped)
            scaled = m_row * (dir_non - times_rows(mapped_full, block))
            pushed = scatter(
                jnp.dot(scaled.astype(jnp.bfloat16), block, preferred_element_type=jnp.float32), width
            )
            remainder = mine(dir_core) - pushed
            image_non = rec_non * dir_non + mix(trait_inverse, scaled)
            curve_part = (
                jnp.sum(dir_non * image_non)
                + jnp.sum(mine(rec_core * dir_core * dir_core))
                + jnp.sum(mapped * mix(trait_inverse, remainder))
            )
            rem_full, (curve,) = gather(remainder, (curve_part,))
            core_out = times_rows(rem_full, core_inverse)
            image_core = rec_core * dir_core + mix(trait_inverse, core_out)
            step = rz / curve
            sol_core = sol_core + step * dir_core
            sol_non = sol_non + step * dir_non
            res_core = res_core - step * image_core
            res_non = res_non - step * image_non
            z_core, z_non = prec_core * res_core, prec_non * res_non
        return sol_core, sol_non, res_core, res_non

    return body


def solution(mesh):
    in_specs = (
        P(None, "cores"),
        P(None, ("grp", "cores")),
        P(None, "cores"),
        P(None, ("grp", "cores")),
        P("cores", None),
        P(("grp", "cores"), None),
        P(("grp", "cores")),
        P(),
    )
    out_specs = (
        P(None, "cores"),
        P(None, ("grp", "cores")),
        P(None, "cores"),
        P(None, ("grp", "cores")),
    )
    body = make_body(mesh.shape["grp"], mesh.shape["cores"])
    return jax.shard_map(body, mesh=mesh, in_specs=in_specs, out_specs=out_specs, check_vma=False)
```

```python
import functools

import jax
import jax.numpy as jnp
from jax import lax
from jax.experimental import pallas as pl
from jax.experimental.pallas import tpu as pltpu
from jax.sharding import PartitionSpec as P

ITERS = 2
AXES = ("cores", "grp")


def split3(value):
    hi = lax.reduce_precision(value, 8, 7)
    mid = lax.reduce_precision(value - hi, 8, 7)
    low = value - hi - mid
    return jnp.stack([hi, mid, low]).astype(jnp.bfloat16)


def mix(trait_inverse, x):
    return sum(trait_inverse[:, s : s + 1] * x[s : s + 1, :] for s in range(x.shape[0]))


def make_plain_body(groups, cores):
    parts = groups * cores

    def exchange(blocks):
        return lax.all_to_all(blocks, AXES, 0, 0, tiled=False)

    def gather(own, scalars=()):
        traits, width = own.shape
        sent = own.astype(jnp.bfloat16)
        if scalars:
            row = jnp.concatenate([split3(s) for s in scalars])
            row = jnp.pad(row, (0, 128 - row.shape[0]))[None]
            sent = jnp.concatenate([sent, jnp.pad(row, ((0, traits - 1), (0, 0)))], axis=1)
        got = exchange(jnp.broadcast_to(sent[None], (parts,) + sent.shape))
        full = got[:, :, :width].transpose(1, 0, 2).reshape(traits, parts * width)
        if not scalars:
            return full
        tail = got[:, 0, width : width + 3 * len(scalars)].astype(jnp.float32)
        sums = tail.reshape(parts, len(scalars), 3).sum((0, 2))
        return full, sums

    def scatter(partial, width):
        traits = partial.shape[0]
        blocks = partial.astype(jnp.bfloat16).reshape(traits, parts, width).transpose(1, 0, 2)
        return exchange(blocks).astype(jnp.float32).sum(0)

    def times_rows(full, rows):
        return lax.dot_general(full, rows, (((1,), (1,)), ((), ())), preferred_element_type=jnp.float32)

    def body(rhs_core, rhs_non, rec_core, rec_non, core_inverse, block, m_inverse, trait_inverse):
        traits, held = rhs_core.shape
        width = held // groups
        at = lax.axis_index("grp") * width

        def mine(x):
            return lax.dynamic_slice_in_dim(x, at, width, axis=1)

        rows_mine = lax.dynamic_slice_in_dim(core_inverse, at, width, axis=0)
        m_row = m_inverse[None, :]
        trait_diag = jnp.diagonal(trait_inverse)[:, None]
        prec_core = 1.0 / (rec_core + trait_diag)
        prec_non = 1.0 / (rec_non + trait_diag * m_row)
        sol_core, sol_non = jnp.zeros_like(rhs_core), jnp.zeros_like(rhs_non)
        res_core, res_non = rhs_core, rhs_non
        z_core, z_non = prec_core * res_core, prec_non * res_non
        dir_core, dir_non = jnp.zeros_like(z_core), jnp.zeros_like(z_non)
        mapped = jnp.zeros((traits, width), jnp.float32)
        rz_old = None
        for iteration in range(ITERS):
            rz_part = jnp.sum(res_non * z_non) + jnp.sum(mine(res_core * z_core))
            z_full, (rz,) = gather(mine(z_core), (rz_part,))
            z_mapped = times_rows(z_full, rows_mine)
            if iteration:
                factor = rz / rz_old
                mapped = z_mapped + factor * mapped
                dir_core = z_core + factor * dir_core
                dir_non = z_non + factor * dir_non
            else:
                mapped, dir_core, dir_non = z_mapped, z_core, z_non
            rz_old = rz
            mapped_full = gather(mapped)
            scaled = m_row * (dir_non - times_rows(mapped_full, block))
            pushed = scatter(
                jnp.dot(scaled.astype(jnp.bfloat16), block, preferred_element_type=jnp.float32), width
            )
            remainder = mine(dir_core) - pushed
            image_non = rec_non * dir_non + mix(trait_inverse, scaled)
            curve_part = (
                jnp.sum(dir_non * image_non)
                + jnp.sum(mine(rec_core * dir_core * dir_core))
                + jnp.sum(mapped * mix(trait_inverse, remainder))
            )
            rem_full, (curve,) = gather(remainder, (curve_part,))
            core_out = times_rows(rem_full, core_inverse)
            image_core = rec_core * dir_core + mix(trait_inverse, core_out)
            step = rz / curve
            sol_core = sol_core + step * dir_core
            sol_non = sol_non + step * dir_non
            res_core = res_core - step * image_core
            res_non = res_non - step * image_non
            z_core, z_non = prec_core * res_core, prec_non * res_non
        return sol_core, sol_non, res_core, res_non

    return body

LANES = 128
F32 = jnp.float32
BF16 = jnp.bfloat16


def total(x):
    return jnp.sum(jnp.sum(x, axis=1, keepdims=True), axis=0, keepdims=True)


def trait_mix(t_ref, x):
    out = t_ref[:, 0:1] * x[0:1, :]
    for s in range(1, x.shape[0]):
        out = out + t_ref[:, s : s + 1] * x[s : s + 1, :]
    return out


def trait_diag(t_ref):
    shape = t_ref.shape
    row = lax.broadcasted_iota(jnp.int32, shape, 0)
    col = lax.broadcasted_iota(jnp.int32, shape, 1)
    return jnp.sum(jnp.where(row == col, t_ref[...], 0.0), axis=1, keepdims=True)


def rows_times(full_ref, got_ref, rows, width):
    for r in range(got_ref.shape[0]):
        full_ref[:, r * width : (r + 1) * width] = got_ref[r, :, :width]
    return lax.dot_general(
        full_ref[...], rows, (((1,), (1,)), ((), ())), preferred_element_type=F32
    )


def put_all(sent_ref, own, width):
    value = own.astype(BF16)
    sent_ref[:, :, :width] = jnp.broadcast_to(value[None], (sent_ref.shape[0],) + value.shape)


def put_sums(sent_ref, sums, width):
    shape = (sent_ref.shape[1], LANES)
    row = lax.broadcasted_iota(jnp.int32, shape, 0)
    lane = lax.broadcasted_iota(jnp.int32, shape, 1)
    tail = jnp.zeros(shape, F32)
    for k, value in enumerate(sums):
        rest = jnp.broadcast_to(value, shape)
        for j in range(3):
            term = rest.astype(BF16).astype(F32)
            rest = rest - term
            tail = jnp.where((row == 0) & (lane == 3 * k + j), term, tail)
    tail = tail.astype(BF16)
    sent_ref[:, :, width:] = jnp.broadcast_to(tail[None], (sent_ref.shape[0],) + shape)


def get_sums(got_ref, count, width):
    tail = jnp.sum(got_ref[:, :, width:].astype(F32), axis=0)
    lane = lax.broadcasted_iota(jnp.int32, tail.shape, 1)
    return [total(jnp.where(lane // 3 == k, tail, 0.0)) for k in range(count)]


def mine(x, groups, width):
    part = x[:, :width]
    for k in range(1, groups):
        part = jnp.where(lax.axis_index("grp") == k, x[:, k * width : (k + 1) * width], part)
    return part


def begin_kernel(groups, width, rhs_c, rhs_n, rec_c, rec_n, m_ref, t_ref, sent, dir_c, dir_n, rz):
    diag = trait_diag(t_ref)
    z_c = rhs_c[...] / (rec_c[...] + diag)
    z_n = rhs_n[...] / (rec_n[...] + diag * m_ref[...])
    dir_c[...] = z_c
    dir_n[...] = z_n
    put_all(sent, mine(z_c, groups, width), width)
    rz[...] = total(rhs_n[...] * z_n) + total(mine(rhs_c[...] * z_c, groups, width))


def map_first_kernel(width, got, c_ref, sent, mapped, full):
    at = pl.multiple_of(lax.axis_index("grp") * width, LANES)
    out = rows_times(full, got, c_ref[pl.ds(at, width), :], width)
    mapped[...] = out
    put_all(sent, out, width)


def map_next_kernel(
    width, got, c_ref, old_mapped, old_c, old_n, z_c, z_n, rz_old, sent, mapped, dir_c, dir_n, rz, full
):
    at = pl.multiple_of(lax.axis_index("grp") * width, LANES)
    out = rows_times(full, got, c_ref[pl.ds(at, width), :], width)
    (rz_now,) = get_sums(got, 1, width)
    factor = rz_now / rz_old[...]
    out = out + factor * old_mapped[...]
    mapped[...] = out
    put_all(sent, out, width)
    dir_c[...] = z_c[...] + factor * old_c[...]
    dir_n[...] = z_n[...] + factor * old_n[...]
    rz[...] = rz_now


def genomic_kernel(width, got, g_ref, m_ref, dir_n, sent, scaled, full):
    pulled = rows_times(full, got, g_ref[...], width)
    value = m_ref[...] * (dir_n[...] - pulled)
    scaled[...] = value
    out = jnp.dot(value.astype(BF16), g_ref[...], preferred_element_type=F32).astype(BF16)
    for r in range(sent.shape[0]):
        sent[r] = out[:, r * width : (r + 1) * width]


def remainder_kernel(groups, width, got, dir_c, dir_n, rec_c, rec_n, scaled, mapped, rz, t_ref, sent):
    pushed = jnp.sum(got[...].astype(F32), axis=0)
    rest = mine(dir_c[...], groups, width) - pushed
    put_all(sent, rest, width)
    image_n = rec_n[...] * dir_n[...] + trait_mix(t_ref, scaled[...])
    curve = (
        total(dir_n[...] * image_n)
        + total(mine(rec_c[...] * dir_c[...] * dir_c[...], groups, width))
        + total(mapped[...] * trait_mix(t_ref, rest))
    )
    put_sums(sent, (curve, rz[...]), width)


def step_kernel(
    groups, width, got, c_ref, dir_c, dir_n, rec_c, rec_n, rhs_c, rhs_n, scaled, m_ref, t_ref,
    sent, step_out, rz_out, res_c_out, res_n_out, z_c_out, z_n_out, full,
):
    core_out = rows_times(full, got, c_ref[...], width)
    curve, rz = get_sums(got, 2, width)
    step = rz / curve
    res_c = rhs_c[...] - step * (rec_c[...] * dir_c[...] + trait_mix(t_ref, core_out))
    res_n = rhs_n[...] - step * (rec_n[...] * dir_n[...] + trait_mix(t_ref, scaled[...]))
    diag = trait_diag(t_ref)
    z_c = res_c / (rec_c[...] + diag)
    z_n = res_n / (rec_n[...] + diag * m_ref[...])
    put_all(sent, mine(z_c, groups, width), width)
    put_sums(sent, (total(res_n * z_n) + total(mine(res_c * z_c, groups, width)),), width)
    step_out[...] = step
    rz_out[...] = rz
    res_c_out[...] = res_c
    res_n_out[...] = res_n
    z_c_out[...] = z_c
    z_n_out[...] = z_n


def final_kernel(
    width, got, c_ref, dir_c, dir_n, rec_c, rec_n, res_c, res_n, scaled, old_c, old_n, old_step, rz, t_ref,
    sol_c, sol_n, res_c_out, res_n_out, full,
):
    core_out = rows_times(full, got, c_ref[...], width)
    (curve,) = get_sums(got, 1, width)
    step = rz[...] / curve
    sol_c[...] = old_step[...] * old_c[...] + step * dir_c[...]
    sol_n[...] = old_step[...] * old_n[...] + step * dir_n[...]
    res_c_out[...] = res_c[...] - step * (rec_c[...] * dir_c[...] + trait_mix(t_ref, core_out))
    res_n_out[...] = res_n[...] - step * (rec_n[...] * dir_n[...] + trait_mix(t_ref, scaled[...]))


def call(kernel, outs, scratch=()):
    spec = pl.BlockSpec(memory_space=pltpu.VMEM)

    def run(*args):
        return pl.pallas_call(
            kernel,
            out_shape=[jax.ShapeDtypeStruct(shape, dtype) for shape, dtype in outs],
            in_specs=[spec] * len(args),
            out_specs=[spec] * len(outs),
            scratch_shapes=[pltpu.VMEM(shape, dtype) for shape, dtype in scratch],
        )(*args)

    return run


def make_kernel_body(groups, cores):
    parts = groups * cores

    def exchange(blocks):
        return lax.all_to_all(blocks, AXES, 0, 0, tiled=False)

    def body(rhs_c, rhs_n, rec_c, rec_n, core_inverse, block, m_inverse, t):
        traits, held = rhs_c.shape
        width = held // groups
        many = rhs_n.shape[1]
        m_row = m_inverse[None, :]
        core, non, own, one = ((traits, held), F32), ((traits, many), F32), ((traits, width), F32), ((1, 1), F32)
        plain = ((parts, traits, width), BF16)
        tailed = ((parts, traits, width + LANES), BF16)
        full = [((traits, parts * width), BF16)]
        part = functools.partial

        sent, dir_c, dir_n, rz = call(part(begin_kernel, groups, width), [plain, core, non, one])(
            rhs_c, rhs_n, rec_c, rec_n, m_row, t
        )
        sent, mapped = call(part(map_first_kernel, width), [plain, own], full)(exchange(sent), core_inverse)
        sent, scaled = call(part(genomic_kernel, width), [plain, non], full)(
            exchange(sent), block, m_row, dir_n
        )
        (sent,) = call(part(remainder_kernel, groups, width), [tailed])(
            exchange(sent), dir_c, dir_n, rec_c, rec_n, scaled, mapped, rz, t
        )
        sent, step, rz, res_c, res_n, z_c, z_n = call(
            part(step_kernel, groups, width), [tailed, one, one, core, non, core, non], full
        )(exchange(sent), core_inverse, dir_c, dir_n, rec_c, rec_n, rhs_c, rhs_n, scaled, m_row, t)
        old_c, old_n = dir_c, dir_n
        sent, mapped, dir_c, dir_n, rz = call(
            part(map_next_kernel, width), [plain, own, core, non, one], full
        )(exchange(sent), core_inverse, mapped, old_c, old_n, z_c, z_n, rz)
        sent, scaled = call(part(genomic_kernel, width), [plain, non], full)(
            exchange(sent), block, m_row, dir_n
        )
        (sent,) = call(part(remainder_kernel, groups, width), [tailed])(
            exchange(sent), dir_c, dir_n, rec_c, rec_n, scaled, mapped, rz, t
        )
        return tuple(
            call(part(final_kernel, width), [core, non, core, non], full)(
                exchange(sent), core_inverse, dir_c, dir_n, rec_c, rec_n, res_c, res_n, scaled,
                old_c, old_n, step, rz, t,
            )
        )

    return body


def solution(mesh):
    in_specs = (
        P(None, "cores"),
        P(None, ("grp", "cores")),
        P(None, "cores"),
        P(None, ("grp", "cores")),
        P("cores", None),
        P(("grp", "cores"), None),
        P(("grp", "cores")),
        P(),
    )
    out_specs = (
        P(None, "cores"),
        P(None, ("grp", "cores")),
        P(None, "cores"),
        P(None, ("grp", "cores")),
    )
    groups, cores = mesh.shape["grp"], mesh.shape["cores"]

    def body(rhs_core, *rest):
        fits = rhs_core.shape[1] % (groups * LANES) == 0
        make = make_kernel_body if fits else make_plain_body
        return make(groups, cores)(rhs_core, *rest)

    return jax.shard_map(body, mesh=mesh, in_specs=in_specs, out_specs=out_specs, check_vma=False)
```

```python
import functools

import jax
import jax.numpy as jnp
from jax import lax
from jax.experimental import pallas as pl
from jax.experimental.pallas import tpu as pltpu
from jax.sharding import PartitionSpec as P

ITERS = 2
AXES = ("cores", "grp")


def split3(value):
    hi = lax.reduce_precision(value, 8, 7)
    mid = lax.reduce_precision(value - hi, 8, 7)
    low = value - hi - mid
    return jnp.stack([hi, mid, low]).astype(jnp.bfloat16)


def mix(trait_inverse, x):
    return sum(trait_inverse[:, s : s + 1] * x[s : s + 1, :] for s in range(x.shape[0]))


def make_plain_body(groups, cores):
    parts = groups * cores

    def exchange(blocks):
        return lax.all_to_all(blocks, AXES, 0, 0, tiled=False)

    def gather(own, scalars=()):
        traits, width = own.shape
        sent = own.astype(jnp.bfloat16)
        if scalars:
            row = jnp.concatenate([split3(s) for s in scalars])
            row = jnp.pad(row, (0, 128 - row.shape[0]))[None]
            sent = jnp.concatenate([sent, jnp.pad(row, ((0, traits - 1), (0, 0)))], axis=1)
        got = exchange(jnp.broadcast_to(sent[None], (parts,) + sent.shape))
        full = got[:, :, :width].transpose(1, 0, 2).reshape(traits, parts * width)
        if not scalars:
            return full
        tail = got[:, 0, width : width + 3 * len(scalars)].astype(jnp.float32)
        sums = tail.reshape(parts, len(scalars), 3).sum((0, 2))
        return full, sums

    def scatter(partial, width):
        traits = partial.shape[0]
        blocks = partial.astype(jnp.bfloat16).reshape(traits, parts, width).transpose(1, 0, 2)
        return exchange(blocks).astype(jnp.float32).sum(0)

    def times_rows(full, rows):
        return lax.dot_general(full, rows, (((1,), (1,)), ((), ())), preferred_element_type=jnp.float32)

    def body(rhs_core, rhs_non, rec_core, rec_non, core_inverse, block, m_inverse, trait_inverse):
        traits, held = rhs_core.shape
        width = held // groups
        at = lax.axis_index("grp") * width

        def mine(x):
            return lax.dynamic_slice_in_dim(x, at, width, axis=1)

        rows_mine = lax.dynamic_slice_in_dim(core_inverse, at, width, axis=0)
        m_row = m_inverse[None, :]
        trait_diag = jnp.diagonal(trait_inverse)[:, None]
        prec_core = 1.0 / (rec_core + trait_diag)
        prec_non = 1.0 / (rec_non + trait_diag * m_row)
        sol_core, sol_non = jnp.zeros_like(rhs_core), jnp.zeros_like(rhs_non)
        res_core, res_non = rhs_core, rhs_non
        z_core, z_non = prec_core * res_core, prec_non * res_non
        dir_core, dir_non = jnp.zeros_like(z_core), jnp.zeros_like(z_non)
        mapped = jnp.zeros((traits, width), jnp.float32)
        rz_old = None
        for iteration in range(ITERS):
            rz_part = jnp.sum(res_non * z_non) + jnp.sum(mine(res_core * z_core))
            z_full, (rz,) = gather(mine(z_core), (rz_part,))
            z_mapped = times_rows(z_full, rows_mine)
            if iteration:
                factor = rz / rz_old
                mapped = z_mapped + factor * mapped
                dir_core = z_core + factor * dir_core
                dir_non = z_non + factor * dir_non
            else:
                mapped, dir_core, dir_non = z_mapped, z_core, z_non
            rz_old = rz
            mapped_full = gather(mapped)
            scaled = m_row * (dir_non - times_rows(mapped_full, block))
            pushed = scatter(
                jnp.dot(scaled.astype(jnp.bfloat16), block, preferred_element_type=jnp.float32), width
            )
            remainder = mine(dir_core) - pushed
            image_non = rec_non * dir_non + mix(trait_inverse, scaled)
            curve_part = (
                jnp.sum(dir_non * image_non)
                + jnp.sum(mine(rec_core * dir_core * dir_core))
                + jnp.sum(mapped * mix(trait_inverse, remainder))
            )
            rem_full, (curve,) = gather(remainder, (curve_part,))
            core_out = times_rows(rem_full, core_inverse)
            image_core = rec_core * dir_core + mix(trait_inverse, core_out)
            step = rz / curve
            sol_core = sol_core + step * dir_core
            sol_non = sol_non + step * dir_non
            res_core = res_core - step * image_core
            res_non = res_non - step * image_non
            z_core, z_non = prec_core * res_core, prec_non * res_non
        return sol_core, sol_non, res_core, res_non

    return body

LANES = 128
F32 = jnp.float32
BF16 = jnp.bfloat16
VMEM_SPEC = pl.BlockSpec(memory_space=pltpu.VMEM)
FAR_SPEC = pl.BlockSpec(memory_space=pltpu.HBM)
WORK = 10**8
GRANT = 20 * 2**20


def lane_sum(x):
    row = jnp.sum(x, axis=0, keepdims=True)
    out = row[:, :LANES]
    for k in range(LANES, row.shape[1], LANES):
        out = out + row[:, k : k + LANES]
    return out


def trait_mix(t_ref, x):
    out = t_ref[:, 0:1] * x[0:1, :]
    for s in range(1, x.shape[0]):
        out = out + t_ref[:, s : s + 1] * x[s : s + 1, :]
    return out


def trait_diag(t_ref):
    shape = t_ref.shape
    row = lax.broadcasted_iota(jnp.int32, shape, 0)
    col = lax.broadcasted_iota(jnp.int32, shape, 1)
    return jnp.sum(jnp.where(row == col, t_ref[...], 0.0), axis=1, keepdims=True)


def rows_times(full_ref, got_ref, rows, width):
    for r in range(got_ref.shape[0]):
        full_ref[:, r * width : (r + 1) * width] = got_ref[r, :, :width]
    return lax.dot_general(
        full_ref[...], rows, (((1,), (1,)), ((), ())), preferred_element_type=F32
    )


def put_all(sent_ref, own, width):
    value = own.astype(BF16)
    sent_ref[:, :, :width] = jnp.broadcast_to(value[None], (sent_ref.shape[0],) + value.shape)


def put_sums(sent_ref, sums, width):
    shape = (sent_ref.shape[1], LANES)
    row = lax.broadcasted_iota(jnp.int32, shape, 0)
    tail = jnp.zeros(shape, F32)
    for k, value in enumerate(sums):
        high = value.astype(BF16).astype(F32)
        tail = jnp.where(row == 2 * k, high, tail)
        tail = jnp.where(row == 2 * k + 1, value - high, tail)
    tail = tail.astype(BF16)
    sent_ref[:, :, width:] = jnp.broadcast_to(tail[None], (sent_ref.shape[0],) + shape)


def get_sums(got_ref, count, width):
    tail = jnp.sum(got_ref[:, :, width:].astype(F32), axis=0)
    rows = jnp.sum(tail, axis=1, keepdims=True)
    return [rows[2 * k : 2 * k + 1] + rows[2 * k + 1 : 2 * k + 2] for k in range(count)]


def own_part(x, groups, width):
    part = x[:, :width]
    for k in range(1, groups):
        part = jnp.where(lax.axis_index("grp") == k, x[:, k * width : (k + 1) * width], part)
    return part


def begin_kernel(groups, width, *refs):
    far, (sent, dir_c, dir_n, rz), held, sems = refs[:6], refs[6:10], refs[10:16], refs[16]
    copies = [pltpu.make_async_copy(far[k], held[k], sems.at[k]) for k in range(6)]
    for copy in copies:
        copy.start()
    for copy in copies:
        copy.wait()
    rhs_c, rhs_n, rec_c, rec_n, m_ref, t_ref = held
    diag = trait_diag(t_ref)
    z_c = rhs_c[...] / (rec_c[...] + diag)
    z_n = rhs_n[...] / (rec_n[...] + diag * m_ref[...])
    put_all(sent, own_part(z_c, groups, width), width)
    dir_c[...] = z_c
    dir_n[...] = z_n
    rz[...] = lane_sum(rhs_n[...] * z_n) + lane_sum(own_part(rhs_c[...] * z_c, groups, width))


def map_first_kernel(width, got, c_ref, sent, mapped, full):
    at = pl.multiple_of(lax.axis_index("grp") * width, LANES)
    out = rows_times(full, got, c_ref[pl.ds(at, width), :], width)
    mapped[...] = out
    put_all(sent, out, width)


def map_next_kernel(
    width, got, c_ref, old_mapped, old_c, old_n, z_c, z_n, rz_old, sent, mapped, dir_c, dir_n, rz, full
):
    at = pl.multiple_of(lax.axis_index("grp") * width, LANES)
    out = rows_times(full, got, c_ref[pl.ds(at, width), :], width)
    (rz_now,) = get_sums(got, 1, width)
    factor = rz_now / rz_old[...]
    out = out + factor * old_mapped[...]
    mapped[...] = out
    put_all(sent, out, width)
    dir_c[...] = z_c[...] + factor * old_c[...]
    dir_n[...] = z_n[...] + factor * old_n[...]
    rz[...] = rz_now


def genomic_kernel(width, got, g_ref, m_ref, dir_n, sent, scaled, full):
    pulled = rows_times(full, got, g_ref[...], width)
    value = m_ref[...] * (dir_n[...] - pulled)
    scaled[...] = value
    out = jnp.dot(value.astype(BF16), g_ref[...], preferred_element_type=F32).astype(BF16)
    for r in range(sent.shape[0]):
        sent[r] = out[:, r * width : (r + 1) * width]


def remainder_kernel(groups, width, got, dir_c, dir_n, rec_c, rec_n, scaled, mapped, t_ref, *others):
    sent, sums = others[-1], others[:-1]
    pushed = jnp.sum(got[...].astype(F32), axis=0)
    rest = own_part(dir_c[...], groups, width) - pushed
    put_all(sent, rest, width)
    image_n = rec_n[...] * dir_n[...] + trait_mix(t_ref, scaled[...])
    curve = (
        lane_sum(dir_n[...] * image_n)
        + lane_sum(own_part(rec_c[...] * dir_c[...] * dir_c[...], groups, width))
        + lane_sum(mapped[...] * trait_mix(t_ref, rest))
    )
    put_sums(sent, [curve] + [one[...] for one in sums], width)


def step_kernel(
    groups, width, got, c_ref, dir_c, dir_n, rec_c, rec_n, rhs_c, rhs_n, scaled, m_ref, t_ref,
    sent, step_out, rz_out, res_c_out, res_n_out, z_c_out, z_n_out, full,
):
    core_out = rows_times(full, got, c_ref[...], width)
    curve, rz = get_sums(got, 2, width)
    step = rz / curve
    res_c = rhs_c[...] - step * (rec_c[...] * dir_c[...] + trait_mix(t_ref, core_out))
    res_n = rhs_n[...] - step * (rec_n[...] * dir_n[...] + trait_mix(t_ref, scaled[...]))
    diag = trait_diag(t_ref)
    z_c = res_c / (rec_c[...] + diag)
    z_n = res_n / (rec_n[...] + diag * m_ref[...])
    put_all(sent, own_part(z_c, groups, width), width)
    put_sums(sent, [lane_sum(res_n * z_n) + lane_sum(own_part(res_c * z_c, groups, width))], width)
    step_out[...] = step
    rz_out[...] = rz
    res_c_out[...] = res_c
    res_n_out[...] = res_n
    z_c_out[...] = z_c
    z_n_out[...] = z_n


def final_kernel(
    width, got, c_ref, dir_c, dir_n, rec_c, rec_n, res_c, res_n, scaled, old_c, old_n, old_step, rz, t_ref,
    sol_c, sol_n, res_c_out, res_n_out, full,
):
    core_out = rows_times(full, got, c_ref[...], width)
    (curve,) = get_sums(got, 1, width)
    step = rz[...] / curve
    sol_c[...] = old_step[...] * old_c[...] + step * dir_c[...]
    sol_n[...] = old_step[...] * old_n[...] + step * dir_n[...]
    res_c_out[...] = res_c[...] - step * (rec_c[...] * dir_c[...] + trait_mix(t_ref, core_out))
    res_n_out[...] = res_n[...] - step * (rec_n[...] * dir_n[...] + trait_mix(t_ref, scaled[...]))


def call(kernel, outs, scratch=(), far=0, cost=None):
    def run(*args):
        return pl.pallas_call(
            kernel,
            out_shape=[jax.ShapeDtypeStruct(shape, dtype) for shape, dtype in outs],
            in_specs=[FAR_SPEC] * far + [VMEM_SPEC] * (len(args) - far),
            out_specs=[VMEM_SPEC] * len(outs),
            scratch_shapes=list(scratch),
            compiler_params=pltpu.CompilerParams(vmem_limit_bytes=GRANT),
            cost_estimate=pl.CostEstimate(flops=WORK, transcendentals=WORK, bytes_accessed=2**20),
        )(*args)

    return run


def make_kernel_body(groups, cores):
    parts = groups * cores

    def exchange(blocks):
        return lax.all_to_all(blocks, AXES, 0, 0, tiled=False)

    def body(rhs_c, rhs_n, rec_c, rec_n, core_inverse, block, m_inverse, t):
        traits, held = rhs_c.shape
        width = held // groups
        many = rhs_n.shape[1]
        m_row = m_inverse[None, :]
        core, non, own = ((traits, held), F32), ((traits, many), F32), ((traits, width), F32)
        one, lanes = ((1, 1), F32), ((1, LANES), F32)
        plain = ((parts, traits, width), BF16)
        tailed = ((parts, traits, width + LANES), BF16)
        full = [pltpu.VMEM((traits, parts * width), BF16)]
        part = functools.partial

        starts = (rhs_c, rhs_n, rec_c, rec_n, m_row, t)
        scratch = [pltpu.VMEM(x.shape, F32) for x in starts] + [pltpu.SemaphoreType.DMA((len(starts),))]
        sent, dir_c, dir_n, rz = call(
            part(begin_kernel, groups, width), [plain, core, non, lanes], scratch, len(starts)
        )(*starts)
        sent, mapped = call(part(map_first_kernel, width), [plain, own], full)(exchange(sent), core_inverse)
        sent, scaled = call(part(genomic_kernel, width), [plain, non], full)(
            exchange(sent), block, m_row, dir_n
        )
        (sent,) = call(part(remainder_kernel, groups, width), [tailed])(
            exchange(sent), dir_c, dir_n, rec_c, rec_n, scaled, mapped, t, rz
        )
        sent, step, rz, res_c, res_n, z_c, z_n = call(
            part(step_kernel, groups, width), [tailed, one, one, core, non, core, non], full
        )(exchange(sent), core_inverse, dir_c, dir_n, rec_c, rec_n, rhs_c, rhs_n, scaled, m_row, t)
        old_c, old_n = dir_c, dir_n
        sent, mapped, dir_c, dir_n, rz = call(
            part(map_next_kernel, width), [plain, own, core, non, one], full
        )(exchange(sent), core_inverse, mapped, old_c, old_n, z_c, z_n, rz)
        sent, scaled = call(part(genomic_kernel, width), [plain, non], full)(
            exchange(sent), block, m_row, dir_n
        )
        (sent,) = call(part(remainder_kernel, groups, width), [tailed])(
            exchange(sent), dir_c, dir_n, rec_c, rec_n, scaled, mapped, t
        )
        return tuple(
            call(part(final_kernel, width), [core, non, core, non], full)(
                exchange(sent), core_inverse, dir_c, dir_n, rec_c, rec_n, res_c, res_n, scaled,
                old_c, old_n, step, rz, t,
            )
        )

    return body


def solution(mesh):
    in_specs = (
        P(None, "cores"),
        P(None, ("grp", "cores")),
        P(None, "cores"),
        P(None, ("grp", "cores")),
        P("cores", None),
        P(("grp", "cores"), None),
        P(("grp", "cores")),
        P(),
    )
    out_specs = (
        P(None, "cores"),
        P(None, ("grp", "cores")),
        P(None, "cores"),
        P(None, ("grp", "cores")),
    )
    groups, cores = mesh.shape["grp"], mesh.shape["cores"]

    def body(rhs_core, *rest):
        fits = rhs_core.shape[1] % (groups * LANES) == 0
        make = make_kernel_body if fits else make_plain_body
        return make(groups, cores)(rhs_core, *rest)

    return jax.shard_map(body, mesh=mesh, in_specs=in_specs, out_specs=out_specs, check_vma=False)
```

```python
import functools

import jax
import jax.numpy as jnp
from jax import lax
from jax.experimental import pallas as pl
from jax.experimental.pallas import tpu as pltpu
from jax.sharding import PartitionSpec as P

ITERS = 2
AXES = ("cores", "grp")


def split3(value):
    hi = lax.reduce_precision(value, 8, 7)
    mid = lax.reduce_precision(value - hi, 8, 7)
    low = value - hi - mid
    return jnp.stack([hi, mid, low]).astype(jnp.bfloat16)


def mix(trait_inverse, x):
    return sum(trait_inverse[:, s : s + 1] * x[s : s + 1, :] for s in range(x.shape[0]))


def make_plain_body(groups, cores):
    parts = groups * cores

    def exchange(blocks):
        return lax.all_to_all(blocks, AXES, 0, 0, tiled=False)

    def gather(own, scalars=()):
        traits, width = own.shape
        sent = own.astype(jnp.bfloat16)
        if scalars:
            row = jnp.concatenate([split3(s) for s in scalars])
            row = jnp.pad(row, (0, 128 - row.shape[0]))[None]
            sent = jnp.concatenate([sent, jnp.pad(row, ((0, traits - 1), (0, 0)))], axis=1)
        got = exchange(jnp.broadcast_to(sent[None], (parts,) + sent.shape))
        full = got[:, :, :width].transpose(1, 0, 2).reshape(traits, parts * width)
        if not scalars:
            return full
        tail = got[:, 0, width : width + 3 * len(scalars)].astype(jnp.float32)
        sums = tail.reshape(parts, len(scalars), 3).sum((0, 2))
        return full, sums

    def scatter(partial, width):
        traits = partial.shape[0]
        blocks = partial.astype(jnp.bfloat16).reshape(traits, parts, width).transpose(1, 0, 2)
        return exchange(blocks).astype(jnp.float32).sum(0)

    def times_rows(full, rows):
        return lax.dot_general(full, rows, (((1,), (1,)), ((), ())), preferred_element_type=jnp.float32)

    def body(rhs_core, rhs_non, rec_core, rec_non, core_inverse, block, m_inverse, trait_inverse):
        traits, held = rhs_core.shape
        width = held // groups
        at = lax.axis_index("grp") * width

        def mine(x):
            return lax.dynamic_slice_in_dim(x, at, width, axis=1)

        rows_mine = lax.dynamic_slice_in_dim(core_inverse, at, width, axis=0)
        m_row = m_inverse[None, :]
        trait_diag = jnp.diagonal(trait_inverse)[:, None]
        prec_core = 1.0 / (rec_core + trait_diag)
        prec_non = 1.0 / (rec_non + trait_diag * m_row)
        sol_core, sol_non = jnp.zeros_like(rhs_core), jnp.zeros_like(rhs_non)
        res_core, res_non = rhs_core, rhs_non
        z_core, z_non = prec_core * res_core, prec_non * res_non
        dir_core, dir_non = jnp.zeros_like(z_core), jnp.zeros_like(z_non)
        mapped = jnp.zeros((traits, width), jnp.float32)
        rz_old = None
        for iteration in range(ITERS):
            rz_part = jnp.sum(res_non * z_non) + jnp.sum(mine(res_core * z_core))
            z_full, (rz,) = gather(mine(z_core), (rz_part,))
            z_mapped = times_rows(z_full, rows_mine)
            if iteration:
                factor = rz / rz_old
                mapped = z_mapped + factor * mapped
                dir_core = z_core + factor * dir_core
                dir_non = z_non + factor * dir_non
            else:
                mapped, dir_core, dir_non = z_mapped, z_core, z_non
            rz_old = rz
            mapped_full = gather(mapped)
            scaled = m_row * (dir_non - times_rows(mapped_full, block))
            pushed = scatter(
                jnp.dot(scaled.astype(jnp.bfloat16), block, preferred_element_type=jnp.float32), width
            )
            remainder = mine(dir_core) - pushed
            image_non = rec_non * dir_non + mix(trait_inverse, scaled)
            curve_part = (
                jnp.sum(dir_non * image_non)
                + jnp.sum(mine(rec_core * dir_core * dir_core))
                + jnp.sum(mapped * mix(trait_inverse, remainder))
            )
            rem_full, (curve,) = gather(remainder, (curve_part,))
            core_out = times_rows(rem_full, core_inverse)
            image_core = rec_core * dir_core + mix(trait_inverse, core_out)
            step = rz / curve
            sol_core = sol_core + step * dir_core
            sol_non = sol_non + step * dir_non
            res_core = res_core - step * image_core
            res_non = res_non - step * image_non
            z_core, z_non = prec_core * res_core, prec_non * res_non
        return sol_core, sol_non, res_core, res_non

    return body

LANES = 128
F32 = jnp.float32
BF16 = jnp.bfloat16
VMEM_SPEC = pl.BlockSpec(memory_space=pltpu.VMEM)
FAR_SPEC = pl.BlockSpec(memory_space=pltpu.HBM)
GRANT = 20 * 2**20
WORK = 10**8


def lane_sum(x):
    row = jnp.sum(x, axis=0, keepdims=True)
    out = row[:, :LANES]
    for k in range(LANES, row.shape[1], LANES):
        out = out + row[:, k : k + LANES]
    return out


def all_lanes(x):
    shift = LANES // 2
    while shift:
        x = x + pltpu.roll(x, shift, 1)
        shift //= 2
    return x


def wide(x, lanes):
    return jnp.concatenate([x] * (lanes // LANES), axis=1) if lanes > LANES else x


def trait_mix(tb_ref, x):
    out = None
    for s in range(x.shape[0]):
        term = wide(tb_ref[:, s * LANES : (s + 1) * LANES], x.shape[1]) * x[s : s + 1, :]
        out = term if out is None else out + term
    return out


def rows_times(full_ref, got_ref, rows, width):
    for r in range(got_ref.shape[0]):
        full_ref[:, r * width : (r + 1) * width] = got_ref[r, :, :width]
    return lax.dot_general(
        full_ref[...], rows, (((1,), (1,)), ((), ())), preferred_element_type=F32
    )


def put_all(sent_ref, own, width):
    value = own.astype(BF16)
    sent_ref[:, :, :width] = jnp.broadcast_to(value[None], (sent_ref.shape[0],) + value.shape)


def put_sums(sent_ref, sums, width):
    shape = (sent_ref.shape[1], LANES)
    row = lax.broadcasted_iota(jnp.int32, shape, 0)
    tail = jnp.zeros(shape, F32)
    for k, value in enumerate(sums):
        high = value.astype(BF16).astype(F32)
        tail = jnp.where(row == 2 * k, high, tail)
        tail = jnp.where(row == 2 * k + 1, value - high, tail)
    tail = tail.astype(BF16)
    sent_ref[:, :, width:] = jnp.broadcast_to(tail[None], (sent_ref.shape[0],) + shape)


def get_sums(got_ref, count, width):
    rows = all_lanes(jnp.sum(got_ref[:, :, width:].astype(F32), axis=0))
    return [rows[2 * k : 2 * k + 1] + rows[2 * k + 1 : 2 * k + 2] for k in range(count)]


def own_part(x, groups, width):
    part = x[:, :width]
    for k in range(1, groups):
        part = jnp.where(lax.axis_index("grp") == k, x[:, k * width : (k + 1) * width], part)
    return part


def early_kernel(out):
    out[...] = jnp.zeros_like(out)


def begin_kernel(
    groups, width, rhs_c, rhs_n, rec_c, rec_n, m_ref, t_ref, early, sent, dir_c, dir_n, rz, prec_c, prec_n, tb
):
    traits = t_ref.shape[0]
    row = lax.broadcasted_iota(jnp.int32, (traits, LANES), 0)
    diag = early[...]
    for s in range(traits):
        column = jnp.broadcast_to(t_ref[:, s : s + 1], (traits, LANES))
        tb[:, s * LANES : (s + 1) * LANES] = column
        diag = jnp.where(row == s, column, diag)
    part_c = 1.0 / (rec_c[...] + wide(diag, rec_c.shape[1]))
    z_c = part_c * rhs_c[...]
    put_all(sent, own_part(z_c, groups, width), width)
    part_n = 1.0 / (rec_n[...] + wide(diag, rec_n.shape[1]) * m_ref[...])
    z_n = part_n * rhs_n[...]
    prec_c[...] = part_c
    prec_n[...] = part_n
    dir_c[...] = z_c
    dir_n[...] = z_n
    rz[...] = lane_sum(rhs_n[...] * z_n) + lane_sum(own_part(rhs_c[...] * z_c, groups, width))


def map_first_kernel(width, got, c_ref, sent, mapped, full):
    at = pl.multiple_of(lax.axis_index("grp") * width, LANES)
    out = rows_times(full, got, c_ref[pl.ds(at, width), :], width)
    put_all(sent, out, width)
    mapped[...] = out


def map_next_kernel(
    width, got, c_ref, old_mapped, old_c, old_n, z_c, z_n, rz_old, sent, mapped, dir_c, dir_n, rz, full
):
    (rz_now,) = get_sums(got, 1, width)
    factor = rz_now / rz_old[...]
    rz[...] = rz_now
    dir_c[...] = z_c[...] + wide(factor, z_c.shape[1]) * old_c[...]
    dir_n[...] = z_n[...] + wide(factor, z_n.shape[1]) * old_n[...]
    kept = wide(factor, width) * old_mapped[...]
    at = pl.multiple_of(lax.axis_index("grp") * width, LANES)
    out = rows_times(full, got, c_ref[pl.ds(at, width), :], width) + kept
    put_all(sent, out, width)
    mapped[...] = out


def genomic_kernel(width, got, g_ref, m_ref, dir_n, sent, scaled, full):
    pulled = rows_times(full, got, g_ref[...], width)
    value = m_ref[...] * (dir_n[...] - pulled)
    scaled[...] = value
    left = value.astype(BF16)
    for r in range(sent.shape[0]):
        part = jnp.dot(left, g_ref[:, r * width : (r + 1) * width], preferred_element_type=F32)
        sent[r] = part.astype(BF16)


def remainder_kernel(groups, width, got, dir_c, dir_n, rec_c, rec_n, scaled, mapped, tb, *others):
    sent, sums = others[-1], others[:-1]
    pushed = jnp.sum(got[...].astype(F32), axis=0)
    rest = own_part(dir_c[...], groups, width) - pushed
    put_all(sent, rest, width)
    image_n = rec_n[...] * dir_n[...] + trait_mix(tb, scaled[...])
    curve = (
        lane_sum(dir_n[...] * image_n)
        + lane_sum(own_part(rec_c[...] * dir_c[...] * dir_c[...], groups, width))
        + lane_sum(mapped[...] * trait_mix(tb, rest))
    )
    put_sums(sent, [curve] + [one[...] for one in sums], width)


def step_kernel(
    groups, width, got, c_ref, dir_c, dir_n, rec_c, rec_n, rhs_c, rhs_n, scaled, prec_c, prec_n, tb,
    sent, step_out, rz_out, res_c_out, res_n_out, z_c_out, z_n_out, full,
):
    curve, rz = get_sums(got, 2, width)
    step = rz / curve
    step_out[...] = step
    rz_out[...] = rz
    res_n = rhs_n[...] - wide(step, rhs_n.shape[1]) * (rec_n[...] * dir_n[...] + trait_mix(tb, scaled[...]))
    z_n = prec_n[...] * res_n
    res_n_out[...] = res_n
    z_n_out[...] = z_n
    part = lane_sum(res_n * z_n)
    core_out = rows_times(full, got, c_ref[...], width)
    res_c = rhs_c[...] - wide(step, rhs_c.shape[1]) * (rec_c[...] * dir_c[...] + trait_mix(tb, core_out))
    z_c = prec_c[...] * res_c
    put_all(sent, own_part(z_c, groups, width), width)
    put_sums(sent, [part + lane_sum(own_part(res_c * z_c, groups, width))], width)
    res_c_out[...] = res_c
    z_c_out[...] = z_c


def final_kernel(
    width, got, c_ref, dir_c, dir_n, rec_c, rec_n, res_c, res_n, scaled, old_c, old_n, old_step, rz, tb,
    sol_c_far, sol_n_far, res_c_far, res_n_far, full, sol_c, sol_n, res_c_out, res_n_out, sems,
):
    pairs = ((sol_c, sol_c_far), (sol_n, sol_n_far), (res_n_out, res_n_far), (res_c_out, res_c_far))
    copies = [pltpu.make_async_copy(near, far, sems.at[k]) for k, (near, far) in enumerate(pairs)]
    (curve,) = get_sums(got, 1, width)
    step = rz[...] / curve
    step_c, step_n = wide(step, dir_c.shape[1]), wide(step, dir_n.shape[1])
    sol_c[...] = wide(old_step[...], dir_c.shape[1]) * old_c[...] + step_c * dir_c[...]
    sol_n[...] = wide(old_step[...], dir_n.shape[1]) * old_n[...] + step_n * dir_n[...]
    res_n_out[...] = res_n[...] - step_n * (rec_n[...] * dir_n[...] + trait_mix(tb, scaled[...]))
    for copy in copies[:3]:
        copy.start()
    core_out = rows_times(full, got, c_ref[...], width)
    res_c_out[...] = res_c[...] - step_c * (rec_c[...] * dir_c[...] + trait_mix(tb, core_out))
    copies[3].start()
    for copy in copies:
        copy.wait()


def call(kernel, outs, scratch=(), out_spec=VMEM_SPEC):
    def run(*args):
        return pl.pallas_call(
            kernel,
            out_shape=[jax.ShapeDtypeStruct(shape, dtype) for shape, dtype in outs],
            in_specs=[VMEM_SPEC] * len(args),
            out_specs=[out_spec] * len(outs),
            scratch_shapes=list(scratch),
            compiler_params=pltpu.CompilerParams(vmem_limit_bytes=GRANT),
            cost_estimate=pl.CostEstimate(flops=WORK, transcendentals=WORK, bytes_accessed=2**20),
        )(*args)

    return run


def make_kernel_body(groups, cores):
    parts = groups * cores

    def exchange(blocks):
        return lax.all_to_all(blocks, AXES, 0, 0, tiled=False)

    def body(rhs_c, rhs_n, rec_c, rec_n, core_inverse, block, m_inverse, t):
        traits, held = rhs_c.shape
        width = held // groups
        many = rhs_n.shape[1]
        m_row = m_inverse[None, :]
        core, non, own = ((traits, held), F32), ((traits, many), F32), ((traits, width), F32)
        lanes, mixer = ((1, LANES), F32), ((traits, traits * LANES), F32)
        plain = ((parts, traits, width), BF16)
        tailed = ((parts, traits, width + LANES), BF16)
        full = [pltpu.VMEM((traits, parts * width), BF16)]
        part = functools.partial

        (early,) = call(early_kernel, [((traits, LANES), F32)])()
        sent, dir_c, dir_n, rz, prec_c, prec_n, tb = call(
            part(begin_kernel, groups, width), [plain, core, non, lanes, core, non, mixer]
        )(rhs_c, rhs_n, rec_c, rec_n, m_row, t, early)
        sent, mapped = call(part(map_first_kernel, width), [plain, own], full)(exchange(sent), core_inverse)
        sent, scaled = call(part(genomic_kernel, width), [plain, non], full)(
            exchange(sent), block, m_row, dir_n
        )
        (sent,) = call(part(remainder_kernel, groups, width), [tailed])(
            exchange(sent), dir_c, dir_n, rec_c, rec_n, scaled, mapped, tb, rz
        )
        sent, step, rz, res_c, res_n, z_c, z_n = call(
            part(step_kernel, groups, width), [tailed, lanes, lanes, core, non, core, non], full
        )(exchange(sent), core_inverse, dir_c, dir_n, rec_c, rec_n, rhs_c, rhs_n, scaled, prec_c, prec_n, tb)
        old_c, old_n = dir_c, dir_n
        sent, mapped, dir_c, dir_n, rz = call(
            part(map_next_kernel, width), [plain, own, core, non, lanes], full
        )(exchange(sent), core_inverse, mapped, old_c, old_n, z_c, z_n, rz)
        sent, scaled = call(part(genomic_kernel, width), [plain, non], full)(
            exchange(sent), block, m_row, dir_n
        )
        (sent,) = call(part(remainder_kernel, groups, width), [tailed])(
            exchange(sent), dir_c, dir_n, rec_c, rec_n, scaled, mapped, tb
        )
        outs = [core, non, core, non]
        stage = [pltpu.VMEM(*x) for x in (core, non, core, non)] + [pltpu.SemaphoreType.DMA((4,))]
        return tuple(
            call(part(final_kernel, width), outs, full + stage, FAR_SPEC)(
                exchange(sent), core_inverse, dir_c, dir_n, rec_c, rec_n, res_c, res_n, scaled,
                old_c, old_n, step, rz, tb,
            )
        )

    return body


def solution(mesh):
    in_specs = (
        P(None, "cores"),
        P(None, ("grp", "cores")),
        P(None, "cores"),
        P(None, ("grp", "cores")),
        P("cores", None),
        P(("grp", "cores"), None),
        P(("grp", "cores")),
        P(),
    )
    out_specs = (
        P(None, "cores"),
        P(None, ("grp", "cores")),
        P(None, "cores"),
        P(None, ("grp", "cores")),
    )
    groups, cores = mesh.shape["grp"], mesh.shape["cores"]

    def body(rhs_core, *rest):
        fits = rhs_core.shape[1] % (groups * LANES) == 0
        make = make_kernel_body if fits else make_plain_body
        return make(groups, cores)(rhs_core, *rest)

    return jax.shard_map(body, mesh=mesh, in_specs=in_specs, out_specs=out_specs, check_vma=False)
```

```python
import functools

import jax
import jax.numpy as jnp
from jax import lax
from jax.experimental import pallas as pl
from jax.experimental.pallas import tpu as pltpu
from jax.sharding import PartitionSpec as P

ITERS = 2
AXES = ("cores", "grp")


def split3(value):
    hi = lax.reduce_precision(value, 8, 7)
    mid = lax.reduce_precision(value - hi, 8, 7)
    low = value - hi - mid
    return jnp.stack([hi, mid, low]).astype(jnp.bfloat16)


def mix(trait_inverse, x):
    return sum(trait_inverse[:, s : s + 1] * x[s : s + 1, :] for s in range(x.shape[0]))


def make_plain_body(groups, cores):
    parts = groups * cores

    def exchange(blocks):
        return lax.all_to_all(blocks, AXES, 0, 0, tiled=False)

    def gather(own, scalars=()):
        traits, width = own.shape
        sent = own.astype(jnp.bfloat16)
        if scalars:
            row = jnp.concatenate([split3(s) for s in scalars])
            row = jnp.pad(row, (0, 128 - row.shape[0]))[None]
            sent = jnp.concatenate([sent, jnp.pad(row, ((0, traits - 1), (0, 0)))], axis=1)
        got = exchange(jnp.broadcast_to(sent[None], (parts,) + sent.shape))
        full = got[:, :, :width].transpose(1, 0, 2).reshape(traits, parts * width)
        if not scalars:
            return full
        tail = got[:, 0, width : width + 3 * len(scalars)].astype(jnp.float32)
        sums = tail.reshape(parts, len(scalars), 3).sum((0, 2))
        return full, sums

    def scatter(partial, width):
        traits = partial.shape[0]
        blocks = partial.astype(jnp.bfloat16).reshape(traits, parts, width).transpose(1, 0, 2)
        return exchange(blocks).astype(jnp.float32).sum(0)

    def times_rows(full, rows):
        return lax.dot_general(full, rows, (((1,), (1,)), ((), ())), preferred_element_type=jnp.float32)

    def body(rhs_core, rhs_non, rec_core, rec_non, core_inverse, block, m_inverse, trait_inverse):
        traits, held = rhs_core.shape
        width = held // groups
        at = lax.axis_index("grp") * width

        def mine(x):
            return lax.dynamic_slice_in_dim(x, at, width, axis=1)

        rows_mine = lax.dynamic_slice_in_dim(core_inverse, at, width, axis=0)
        m_row = m_inverse[None, :]
        trait_diag = jnp.diagonal(trait_inverse)[:, None]
        prec_core = 1.0 / (rec_core + trait_diag)
        prec_non = 1.0 / (rec_non + trait_diag * m_row)
        sol_core, sol_non = jnp.zeros_like(rhs_core), jnp.zeros_like(rhs_non)
        res_core, res_non = rhs_core, rhs_non
        z_core, z_non = prec_core * res_core, prec_non * res_non
        dir_core, dir_non = jnp.zeros_like(z_core), jnp.zeros_like(z_non)
        mapped = jnp.zeros((traits, width), jnp.float32)
        rz_old = None
        for iteration in range(ITERS):
            rz_part = jnp.sum(res_non * z_non) + jnp.sum(mine(res_core * z_core))
            z_full, (rz,) = gather(mine(z_core), (rz_part,))
            z_mapped = times_rows(z_full, rows_mine)
            if iteration:
                factor = rz / rz_old
                mapped = z_mapped + factor * mapped
                dir_core = z_core + factor * dir_core
                dir_non = z_non + factor * dir_non
            else:
                mapped, dir_core, dir_non = z_mapped, z_core, z_non
            rz_old = rz
            mapped_full = gather(mapped)
            scaled = m_row * (dir_non - times_rows(mapped_full, block))
            pushed = scatter(
                jnp.dot(scaled.astype(jnp.bfloat16), block, preferred_element_type=jnp.float32), width
            )
            remainder = mine(dir_core) - pushed
            image_non = rec_non * dir_non + mix(trait_inverse, scaled)
            curve_part = (
                jnp.sum(dir_non * image_non)
                + jnp.sum(mine(rec_core * dir_core * dir_core))
                + jnp.sum(mapped * mix(trait_inverse, remainder))
            )
            rem_full, (curve,) = gather(remainder, (curve_part,))
            core_out = times_rows(rem_full, core_inverse)
            image_core = rec_core * dir_core + mix(trait_inverse, core_out)
            step = rz / curve
            sol_core = sol_core + step * dir_core
            sol_non = sol_non + step * dir_non
            res_core = res_core - step * image_core
            res_non = res_non - step * image_non
            z_core, z_non = prec_core * res_core, prec_non * res_non
        return sol_core, sol_non, res_core, res_non

    return body

LANES = 128
F32 = jnp.float32
BF16 = jnp.bfloat16
VMEM_SPEC = pl.BlockSpec(memory_space=pltpu.VMEM)
FAR_SPEC = pl.BlockSpec(memory_space=pltpu.HBM)
GRANT = 20 * 2**20
WORK = 10**8


def lane_sum(x):
    row = jnp.sum(x, axis=0, keepdims=True)
    out = row[:, :LANES]
    for k in range(LANES, row.shape[1], LANES):
        out = out + row[:, k : k + LANES]
    return out


def all_lanes(x):
    shift = LANES // 2
    while shift:
        x = x + pltpu.roll(x, shift, 1)
        shift //= 2
    return x


def wide(x, lanes):
    return jnp.concatenate([x] * (lanes // LANES), axis=1) if lanes > LANES else x


def trait_mix(tb_ref, x):
    out = None
    for s in range(x.shape[0]):
        term = wide(tb_ref[:, s * LANES : (s + 1) * LANES], x.shape[1]) * x[s : s + 1, :]
        out = term if out is None else out + term
    return out


def rows_times(full_ref, got_ref, rows, width):
    for r in range(got_ref.shape[0]):
        full_ref[:, r * width : (r + 1) * width] = got_ref[r, :, :width]
    return lax.dot_general(
        full_ref[...], rows, (((1,), (1,)), ((), ())), preferred_element_type=F32
    )


def put_all(sent_ref, own, width):
    value = own.astype(BF16)
    sent_ref[:, :, :width] = jnp.broadcast_to(value[None], (sent_ref.shape[0],) + value.shape)


def put_sums(sent_ref, sums, width):
    shape = (sent_ref.shape[1], LANES)
    row = lax.broadcasted_iota(jnp.int32, shape, 0)
    tail = jnp.zeros(shape, F32)
    for k, value in enumerate(sums):
        high = value.astype(BF16).astype(F32)
        tail = jnp.where(row == 2 * k, high, tail)
        tail = jnp.where(row == 2 * k + 1, value - high, tail)
    tail = tail.astype(BF16)
    sent_ref[:, :, width:] = jnp.broadcast_to(tail[None], (sent_ref.shape[0],) + shape)


def get_sums(got_ref, count, width):
    rows = all_lanes(jnp.sum(got_ref[:, :, width:].astype(F32), axis=0))
    return [rows[2 * k : 2 * k + 1] + rows[2 * k + 1 : 2 * k + 2] for k in range(count)]


def own_part(x, groups, width):
    part = x[:, :width]
    for k in range(1, groups):
        part = jnp.where(lax.axis_index("grp") == k, x[:, k * width : (k + 1) * width], part)
    return part


def early_kernel(out):
    out[...] = jnp.zeros_like(out)


def begin_kernel(
    groups, width, rhs_c, rhs_n, rec_c, rec_n, m_ref, t_ref, early, sent, dir_c, dir_n, rz, prec_c, prec_n, tb
):
    traits = t_ref.shape[0]
    row = lax.broadcasted_iota(jnp.int32, (traits, LANES), 0)
    diag = early[...]
    for s in range(traits):
        column = jnp.broadcast_to(t_ref[:, s : s + 1], (traits, LANES))
        tb[:, s * LANES : (s + 1) * LANES] = column
        diag = jnp.where(row == s, column, diag)
    part_c = 1.0 / (rec_c[...] + wide(diag, rec_c.shape[1]))
    z_c = part_c * rhs_c[...]
    put_all(sent, own_part(z_c, groups, width), width)
    part_n = 1.0 / (rec_n[...] + wide(diag, rec_n.shape[1]) * m_ref[...])
    z_n = part_n * rhs_n[...]
    prec_c[...] = part_c
    prec_n[...] = part_n
    dir_c[...] = z_c
    dir_n[...] = z_n
    rz[...] = lane_sum(rhs_n[...] * z_n) + lane_sum(own_part(rhs_c[...] * z_c, groups, width))


def map_first_kernel(width, got, c_ref, sent, mapped, full):
    at = pl.multiple_of(lax.axis_index("grp") * width, LANES)
    out = rows_times(full, got, c_ref[pl.ds(at, width), :], width)
    put_all(sent, out, width)
    mapped[...] = out


def map_next_kernel(
    width, got, c_ref, old_mapped, old_c, old_n, z_c, z_n, rz_old, sent, mapped, dir_c, dir_n, rz, full
):
    (rz_now,) = get_sums(got, 1, width)
    factor = rz_now / rz_old[...]
    rz[...] = rz_now
    dir_c[...] = z_c[...] + wide(factor, z_c.shape[1]) * old_c[...]
    dir_n[...] = z_n[...] + wide(factor, z_n.shape[1]) * old_n[...]
    kept = wide(factor, width) * old_mapped[...]
    at = pl.multiple_of(lax.axis_index("grp") * width, LANES)
    out = rows_times(full, got, c_ref[pl.ds(at, width), :], width) + kept
    put_all(sent, out, width)
    mapped[...] = out


def pull_kernel(width, got, g_ref, m_ref, dir_n, scaled, left, full):
    value = m_ref[...] * (dir_n[...] - rows_times(full, got, g_ref[...], width))
    scaled[...] = value
    left[...] = value.astype(BF16)


def push_kernel(width, left, g_ref, sent):
    for r in range(sent.shape[0]):
        part = jnp.dot(left[...], g_ref[:, r * width : (r + 1) * width], preferred_element_type=F32)
        sent[r] = part.astype(BF16)


def remainder_kernel(groups, width, got, dir_c, dir_n, rec_c, rec_n, scaled, mapped, tb, *others):
    sent, sums = others[-1], others[:-1]
    pushed = jnp.sum(got[...].astype(F32), axis=0)
    rest = own_part(dir_c[...], groups, width) - pushed
    put_all(sent, rest, width)
    image_n = rec_n[...] * dir_n[...] + trait_mix(tb, scaled[...])
    curve = (
        lane_sum(dir_n[...] * image_n)
        + lane_sum(own_part(rec_c[...] * dir_c[...] * dir_c[...], groups, width))
        + lane_sum(mapped[...] * trait_mix(tb, rest))
    )
    put_sums(sent, [curve] + [one[...] for one in sums], width)


def step_kernel(
    groups, width, got, c_ref, dir_c, dir_n, rec_c, rec_n, rhs_c, rhs_n, scaled, prec_c, prec_n, tb,
    sent, step_out, rz_out, res_c_out, res_n_out, z_c_out, z_n_out, full,
):
    curve, rz = get_sums(got, 2, width)
    step = rz / curve
    step_out[...] = step
    rz_out[...] = rz
    res_n = rhs_n[...] - wide(step, rhs_n.shape[1]) * (rec_n[...] * dir_n[...] + trait_mix(tb, scaled[...]))
    z_n = prec_n[...] * res_n
    res_n_out[...] = res_n
    z_n_out[...] = z_n
    part = lane_sum(res_n * z_n)
    core_out = rows_times(full, got, c_ref[...], width)
    res_c = rhs_c[...] - wide(step, rhs_c.shape[1]) * (rec_c[...] * dir_c[...] + trait_mix(tb, core_out))
    z_c = prec_c[...] * res_c
    put_all(sent, own_part(z_c, groups, width), width)
    put_sums(sent, [part + lane_sum(own_part(res_c * z_c, groups, width))], width)
    res_c_out[...] = res_c
    z_c_out[...] = z_c


def final_kernel(
    width, got, c_ref, dir_c, dir_n, rec_c, rec_n, res_c, res_n, scaled, old_c, old_n, old_step, rz, tb,
    sol_c_far, sol_n_far, res_c_far, res_n_far, full, sol_c, sol_n, res_c_out, res_n_out, sems,
):
    pairs = ((sol_c, sol_c_far), (sol_n, sol_n_far), (res_n_out, res_n_far), (res_c_out, res_c_far))
    copies = [pltpu.make_async_copy(near, far, sems.at[k]) for k, (near, far) in enumerate(pairs)]
    (curve,) = get_sums(got, 1, width)
    step = rz[...] / curve
    step_c, step_n = wide(step, dir_c.shape[1]), wide(step, dir_n.shape[1])
    sol_c[...] = wide(old_step[...], dir_c.shape[1]) * old_c[...] + step_c * dir_c[...]
    sol_n[...] = wide(old_step[...], dir_n.shape[1]) * old_n[...] + step_n * dir_n[...]
    res_n_out[...] = res_n[...] - step_n * (rec_n[...] * dir_n[...] + trait_mix(tb, scaled[...]))
    for copy in copies[:3]:
        copy.start()
    core_out = rows_times(full, got, c_ref[...], width)
    res_c_out[...] = res_c[...] - step_c * (rec_c[...] * dir_c[...] + trait_mix(tb, core_out))
    copies[3].start()
    for copy in copies:
        copy.wait()


def call(kernel, outs, scratch=(), out_spec=VMEM_SPEC):
    def run(*args):
        return pl.pallas_call(
            kernel,
            out_shape=[jax.ShapeDtypeStruct(shape, dtype) for shape, dtype in outs],
            in_specs=[VMEM_SPEC] * len(args),
            out_specs=[out_spec] * len(outs),
            scratch_shapes=list(scratch),
            compiler_params=pltpu.CompilerParams(vmem_limit_bytes=GRANT),
            cost_estimate=pl.CostEstimate(flops=WORK, transcendentals=WORK, bytes_accessed=2**20),
        )(*args)

    return run


def make_kernel_body(groups, cores):
    parts = groups * cores

    def exchange(blocks):
        return lax.all_to_all(blocks, AXES, 0, 0, tiled=False)

    def body(rhs_c, rhs_n, rec_c, rec_n, core_inverse, block, m_inverse, t):
        traits, held = rhs_c.shape
        width = held // groups
        many = rhs_n.shape[1]
        m_row = m_inverse[None, :]
        core, non, own = ((traits, held), F32), ((traits, many), F32), ((traits, width), F32)
        lanes, mixer = ((1, LANES), F32), ((traits, traits * LANES), F32)
        plain = ((parts, traits, width), BF16)
        tailed = ((parts, traits, width + LANES), BF16)
        near = ((traits, many), BF16)
        full = [pltpu.VMEM((traits, parts * width), BF16)]
        part = functools.partial

        (early,) = call(early_kernel, [((traits, LANES), F32)])()
        sent, dir_c, dir_n, rz, prec_c, prec_n, tb = call(
            part(begin_kernel, groups, width), [plain, core, non, lanes, core, non, mixer]
        )(rhs_c, rhs_n, rec_c, rec_n, m_row, t, early)
        sent, mapped = call(part(map_first_kernel, width), [plain, own], full)(exchange(sent), core_inverse)
        scaled, left = call(part(pull_kernel, width), [non, near], full)(exchange(sent), block, m_row, dir_n)
        (sent,) = call(part(push_kernel, width), [plain])(left, block)
        (sent,) = call(part(remainder_kernel, groups, width), [tailed])(
            exchange(sent), dir_c, dir_n, rec_c, rec_n, scaled, mapped, tb, rz
        )
        sent, step, rz, res_c, res_n, z_c, z_n = call(
            part(step_kernel, groups, width), [tailed, lanes, lanes, core, non, core, non], full
        )(exchange(sent), core_inverse, dir_c, dir_n, rec_c, rec_n, rhs_c, rhs_n, scaled, prec_c, prec_n, tb)
        old_c, old_n = dir_c, dir_n
        sent, mapped, dir_c, dir_n, rz = call(
            part(map_next_kernel, width), [plain, own, core, non, lanes], full
        )(exchange(sent), core_inverse, mapped, old_c, old_n, z_c, z_n, rz)
        scaled, left = call(part(pull_kernel, width), [non, near], full)(exchange(sent), block, m_row, dir_n)
        (sent,) = call(part(push_kernel, width), [plain])(left, block)
        (sent,) = call(part(remainder_kernel, groups, width), [tailed])(
            exchange(sent), dir_c, dir_n, rec_c, rec_n, scaled, mapped, tb
        )
        outs = [core, non, core, non]
        stage = [pltpu.VMEM(*x) for x in (core, non, core, non)] + [pltpu.SemaphoreType.DMA((4,))]
        return tuple(
            call(part(final_kernel, width), outs, full + stage, FAR_SPEC)(
                exchange(sent), core_inverse, dir_c, dir_n, rec_c, rec_n, res_c, res_n, scaled,
                old_c, old_n, step, rz, tb,
            )
        )

    return body


def solution(mesh):
    in_specs = (
        P(None, "cores"),
        P(None, ("grp", "cores")),
        P(None, "cores"),
        P(None, ("grp", "cores")),
        P("cores", None),
        P(("grp", "cores"), None),
        P(("grp", "cores")),
        P(),
    )
    out_specs = (
        P(None, "cores"),
        P(None, ("grp", "cores")),
        P(None, "cores"),
        P(None, ("grp", "cores")),
    )
    groups, cores = mesh.shape["grp"], mesh.shape["cores"]

    def body(rhs_core, *rest):
        fits = rhs_core.shape[1] % (groups * LANES) == 0
        make = make_kernel_body if fits else make_plain_body
        return make(groups, cores)(rhs_core, *rest)

    return jax.shard_map(body, mesh=mesh, in_specs=in_specs, out_specs=out_specs, check_vma=False)
```

```python
import functools

import jax
import jax.numpy as jnp
from jax import lax
from jax.experimental import pallas as pl
from jax.experimental.pallas import tpu as pltpu
from jax.sharding import PartitionSpec as P

ITERS = 2
AXES = ("cores", "grp")


def split3(value):
    hi = lax.reduce_precision(value, 8, 7)
    mid = lax.reduce_precision(value - hi, 8, 7)
    low = value - hi - mid
    return jnp.stack([hi, mid, low]).astype(jnp.bfloat16)


def mix(trait_inverse, x):
    return sum(trait_inverse[:, s : s + 1] * x[s : s + 1, :] for s in range(x.shape[0]))


def make_plain_body(groups, cores):
    parts = groups * cores

    def exchange(blocks):
        return lax.all_to_all(blocks, AXES, 0, 0, tiled=False)

    def gather(own, scalars=()):
        traits, width = own.shape
        sent = own.astype(jnp.bfloat16)
        if scalars:
            row = jnp.concatenate([split3(s) for s in scalars])
            row = jnp.pad(row, (0, 128 - row.shape[0]))[None]
            sent = jnp.concatenate([sent, jnp.pad(row, ((0, traits - 1), (0, 0)))], axis=1)
        got = exchange(jnp.broadcast_to(sent[None], (parts,) + sent.shape))
        full = got[:, :, :width].transpose(1, 0, 2).reshape(traits, parts * width)
        if not scalars:
            return full
        tail = got[:, 0, width : width + 3 * len(scalars)].astype(jnp.float32)
        sums = tail.reshape(parts, len(scalars), 3).sum((0, 2))
        return full, sums

    def scatter(partial, width):
        traits = partial.shape[0]
        blocks = partial.astype(jnp.bfloat16).reshape(traits, parts, width).transpose(1, 0, 2)
        return exchange(blocks).astype(jnp.float32).sum(0)

    def times_rows(full, rows):
        return lax.dot_general(full, rows, (((1,), (1,)), ((), ())), preferred_element_type=jnp.float32)

    def body(rhs_core, rhs_non, rec_core, rec_non, core_inverse, block, m_inverse, trait_inverse):
        traits, held = rhs_core.shape
        width = held // groups
        at = lax.axis_index("grp") * width

        def mine(x):
            return lax.dynamic_slice_in_dim(x, at, width, axis=1)

        rows_mine = lax.dynamic_slice_in_dim(core_inverse, at, width, axis=0)
        m_row = m_inverse[None, :]
        trait_diag = jnp.diagonal(trait_inverse)[:, None]
        prec_core = 1.0 / (rec_core + trait_diag)
        prec_non = 1.0 / (rec_non + trait_diag * m_row)
        sol_core, sol_non = jnp.zeros_like(rhs_core), jnp.zeros_like(rhs_non)
        res_core, res_non = rhs_core, rhs_non
        z_core, z_non = prec_core * res_core, prec_non * res_non
        dir_core, dir_non = jnp.zeros_like(z_core), jnp.zeros_like(z_non)
        mapped = jnp.zeros((traits, width), jnp.float32)
        rz_old = None
        for iteration in range(ITERS):
            rz_part = jnp.sum(res_non * z_non) + jnp.sum(mine(res_core * z_core))
            z_full, (rz,) = gather(mine(z_core), (rz_part,))
            z_mapped = times_rows(z_full, rows_mine)
            if iteration:
                factor = rz / rz_old
                mapped = z_mapped + factor * mapped
                dir_core = z_core + factor * dir_core
                dir_non = z_non + factor * dir_non
            else:
                mapped, dir_core, dir_non = z_mapped, z_core, z_non
            rz_old = rz
            mapped_full = gather(mapped)
            scaled = m_row * (dir_non - times_rows(mapped_full, block))
            pushed = scatter(
                jnp.dot(scaled.astype(jnp.bfloat16), block, preferred_element_type=jnp.float32), width
            )
            remainder = mine(dir_core) - pushed
            image_non = rec_non * dir_non + mix(trait_inverse, scaled)
            curve_part = (
                jnp.sum(dir_non * image_non)
                + jnp.sum(mine(rec_core * dir_core * dir_core))
                + jnp.sum(mapped * mix(trait_inverse, remainder))
            )
            rem_full, (curve,) = gather(remainder, (curve_part,))
            core_out = times_rows(rem_full, core_inverse)
            image_core = rec_core * dir_core + mix(trait_inverse, core_out)
            step = rz / curve
            sol_core = sol_core + step * dir_core
            sol_non = sol_non + step * dir_non
            res_core = res_core - step * image_core
            res_non = res_non - step * image_non
            z_core, z_non = prec_core * res_core, prec_non * res_non
        return sol_core, sol_non, res_core, res_non

    return body

LANES = 128
F32 = jnp.float32
BF16 = jnp.bfloat16
VMEM_SPEC = pl.BlockSpec(memory_space=pltpu.VMEM)
FAR_SPEC = pl.BlockSpec(memory_space=pltpu.HBM)
GRANT = 20 * 2**20
WORK = 10**8


def lane_sum(x):
    row = jnp.sum(x, axis=0, keepdims=True)
    out = row[:, :LANES]
    for k in range(LANES, row.shape[1], LANES):
        out = out + row[:, k : k + LANES]
    return out


def all_lanes(x):
    shift = LANES // 2
    while shift:
        x = x + pltpu.roll(x, shift, 1)
        shift //= 2
    return x


def wide(x, lanes):
    return jnp.concatenate([x] * (lanes // LANES), axis=1) if lanes > LANES else x


def trait_mix(tb_ref, x):
    out = None
    for s in range(x.shape[0]):
        term = wide(tb_ref[:, s * LANES : (s + 1) * LANES], x.shape[1]) * x[s : s + 1, :]
        out = term if out is None else out + term
    return out


def rows_times(full_ref, got_ref, rows, width, places):
    for r, place in enumerate(places):
        full_ref[:, place * width : (place + 1) * width] = got_ref[r]
    return lax.dot_general(
        full_ref[...], rows, (((1,), (1,)), ((), ())), preferred_element_type=F32
    )


def put_products(sent_ref, left, rows_ref, at, count, width, places):
    for block in sorted(set(places)):
        part = jnp.dot(
            left, rows_ref[pl.ds(at, count), block * width : (block + 1) * width], preferred_element_type=F32
        ).astype(BF16)
        for r, place in enumerate(places):
            if place == block:
                sent_ref[r, :, :width] = part


def put_all(sent_ref, own, width):
    value = own.astype(BF16)
    sent_ref[:, :, :width] = jnp.broadcast_to(value[None], (sent_ref.shape[0],) + value.shape)


def tail_slot(shape, k):
    lane = lax.broadcasted_iota(jnp.int32, shape, 1)
    return lane // (LANES // 2) == k % 2, 2 * (k // 2)


def put_sums(sent_ref, sums, width):
    shape = (sent_ref.shape[1], LANES)
    row = lax.broadcasted_iota(jnp.int32, shape, 0)
    tail = jnp.zeros(shape, F32)
    for k, value in enumerate(sums):
        half, first = tail_slot(shape, k)
        value = value + pltpu.roll(value, LANES // 2, 1)
        high = value.astype(BF16).astype(F32)
        tail = jnp.where(half & (row == first), high, tail)
        tail = jnp.where(half & (row == first + 1), value - high, tail)
    tail = tail.astype(BF16)
    sent_ref[:, :, width:] = jnp.broadcast_to(tail[None], (sent_ref.shape[0],) + shape)


def get_sums(got_ref, count, width):
    tail = jnp.sum(got_ref[:, :, width:].astype(F32), axis=0)
    out = []
    for k in range(count):
        half, first = tail_slot(tail.shape, k)
        rows = all_lanes(jnp.where(half, tail, 0.0))
        out.append(rows[first : first + 1] + rows[first + 1 : first + 2])
    return out


def own_part(x, groups, width):
    part = x[:, :width]
    for k in range(1, groups):
        part = jnp.where(lax.axis_index("grp") == k, x[:, k * width : (k + 1) * width], part)
    return part


def early_kernel(out):
    out[...] = jnp.zeros_like(out)


def begin_kernel(
    groups, width, rhs_c, rhs_n, rec_c, rec_n, m_ref, t_ref, early, sent, dir_c, dir_n, rz, prec_c, prec_n, tb
):
    traits = t_ref.shape[0]
    row = lax.broadcasted_iota(jnp.int32, (traits, LANES), 0)
    diag = early[...]
    for s in range(traits):
        column = jnp.broadcast_to(t_ref[:, s : s + 1], (traits, LANES))
        tb[:, s * LANES : (s + 1) * LANES] = column
        diag = jnp.where(row == s, column, diag)
    part_c = 1.0 / (rec_c[...] + wide(diag, rec_c.shape[1]))
    z_c = part_c * rhs_c[...]
    put_all(sent, own_part(z_c, groups, width), width)
    part_n = 1.0 / (rec_n[...] + wide(diag, rec_n.shape[1]) * m_ref[...])
    z_n = part_n * rhs_n[...]
    prec_c[...] = part_c
    prec_n[...] = part_n
    dir_c[...] = z_c
    dir_n[...] = z_n
    rz[...] = lane_sum(rhs_n[...] * z_n) + lane_sum(own_part(rhs_c[...] * z_c, groups, width))


def own_rows(width):
    return pl.multiple_of(lax.axis_index("grp") * width, LANES)


def map_first_kernel(groups, width, places, got, c_ref, vec_c, tb, sent, form, full):
    out = rows_times(full, got, c_ref[pl.ds(own_rows(width), width), :], width, places)
    put_all(sent, out, width)
    form[...] = lane_sum(out * trait_mix(tb, own_part(vec_c[...], groups, width)))


def map_next_kernel(groups, width, got, vec_c, tb, sent, form):
    out = jnp.sum(got[...].astype(F32), axis=0)
    put_all(sent, out, width)
    form[...] = lane_sum(out * trait_mix(tb, own_part(vec_c[...], groups, width)))


def pull_kernel(
    groups, width, places, got, g_ref, m_ref, vec_c, vec_n, rec_c, rec_n, form, tb, image_n, left, curve, full
):
    pulled = rows_times(full, got, g_ref[...], width, places)
    differ = vec_n[...] - pulled
    scaled = m_ref[...] * differ
    left[...] = scaled.astype(BF16)
    mixed = trait_mix(tb, scaled)
    weighted = rec_n[...] * vec_n[...]
    image_n[...] = weighted + mixed
    curve[...] = (
        form[...]
        + lane_sum(vec_n[...] * weighted + differ * mixed)
        + lane_sum(own_part(rec_c[...] * vec_c[...] * vec_c[...], groups, width))
    )


def push_kernel(width, places, left, g_ref, *others):
    sent, sums = others[-1], others[:-1]
    put_sums(sent, [one[...] for one in sums], width)
    put_products(sent, left[...], g_ref, 0, g_ref.shape[0], width, places)


def put_remainder(groups, width, chips, got, vec_c, c_ref, sent):
    pushed = jnp.sum(got[:, :, :width].astype(F32), axis=0)
    rest = (own_part(vec_c[...], groups, width) - pushed).astype(BF16)
    put_products(sent, rest, c_ref, own_rows(width), width, groups * width, chips)


def rest_first_kernel(
    groups, width, chips, got, dir_c, c_ref, rhs_n, image_n, prec_n,
    sent, step_out, rz_out, curve_out, res_n_out, z_n_out, rz_part, cross_part,
):
    put_remainder(groups, width, chips, got, dir_c, c_ref, sent)
    curve, rz = get_sums(got, 2, width)
    step = rz / curve
    step_out[...] = step
    rz_out[...] = rz
    curve_out[...] = curve
    res_n = rhs_n[...] - wide(step, rhs_n.shape[1]) * image_n[...]
    z_n = prec_n[...] * res_n
    res_n_out[...] = res_n
    z_n_out[...] = z_n
    rz_part[...] = lane_sum(res_n * z_n)
    cross_part[...] = lane_sum(z_n * image_n[...])


def step_kernel(
    groups, width, places, got, c_ref, dir_c, rec_c, rhs_c, prec_c, tb, step, rz_in, cross_in,
    sent, image_c_out, res_c_out, z_c_out, rz_part, cross_part,
):
    core_out = jnp.sum(got[...].astype(F32), axis=0)
    image_c = rec_c[...] * dir_c[...] + trait_mix(tb, core_out)
    res_c = rhs_c[...] - wide(step[...], rhs_c.shape[1]) * image_c
    z_c = prec_c[...] * res_c
    left = own_part(z_c, groups, width).astype(BF16)
    put_products(sent, left, c_ref, own_rows(width), width, width, places)
    image_c_out[...] = image_c
    res_c_out[...] = res_c
    z_c_out[...] = z_c
    rz_part[...] = rz_in[...] + lane_sum(own_part(res_c * z_c, groups, width))
    cross_part[...] = cross_in[...] + lane_sum(own_part(z_c * image_c, groups, width))


def rest_next_kernel(
    groups, width, chips, got, z_c, c_ref, z_n, dir_c, dir_n, res_n, image_n, image_z, old_step, old_rz, old_curve,
    sent, step_out, factor_out, sol_c, sol_n, res_n_out,
):
    put_remainder(groups, width, chips, got, z_c, c_ref, sent)
    curve_z, rz, cross = get_sums(got, 3, width)
    factor = rz / old_rz[...]
    step = rz / (curve_z + factor * (2.0 * cross + factor * old_curve[...]))
    step_out[...] = step
    factor_out[...] = factor
    held, many = z_c.shape[1], z_n.shape[1]
    sol_c[...] = wide(old_step[...] + step * factor, held) * dir_c[...] + wide(step, held) * z_c[...]
    sol_n[...] = wide(old_step[...] + step * factor, many) * dir_n[...] + wide(step, many) * z_n[...]
    res_n_out[...] = res_n[...] - wide(step, many) * (image_z[...] + wide(factor, many) * image_n[...])


def final_kernel(
    got, z_c, rec_c, res_c, image_c, step, factor, tb, sol_c, sol_n, res_n,
    sol_c_far, sol_n_far, res_c_far, res_n_far, res_c_out, sems,
):
    pairs = ((sol_c, sol_c_far), (sol_n, sol_n_far), (res_n, res_n_far), (res_c_out, res_c_far))
    copies = [pltpu.make_async_copy(near, far, sems.at[k]) for k, (near, far) in enumerate(pairs)]
    for copy in copies[:3]:
        copy.start()
    held = z_c.shape[1]
    core_out = jnp.sum(got[...].astype(F32), axis=0)
    image = rec_c[...] * z_c[...] + trait_mix(tb, core_out) + wide(factor[...], held) * image_c[...]
    res_c_out[...] = res_c[...] - wide(step[...], held) * image
    copies[3].start()
    for copy in copies:
        copy.wait()


def call(kernel, outs, scratch=(), out_spec=VMEM_SPEC):
    def run(*args):
        return pl.pallas_call(
            kernel,
            out_shape=[jax.ShapeDtypeStruct(shape, dtype) for shape, dtype in outs],
            in_specs=[VMEM_SPEC] * len(args),
            out_specs=[out_spec] * len(outs),
            scratch_shapes=list(scratch),
            compiler_params=pltpu.CompilerParams(vmem_limit_bytes=GRANT),
            cost_estimate=pl.CostEstimate(flops=WORK, transcendentals=WORK, bytes_accessed=2**20),
        )(*args)

    return run


def make_kernel_body(groups, cores):
    parts = groups * cores

    def exchange(blocks):
        return lax.all_to_all(blocks, ("grp", "cores"), 0, 0, tiled=False)

    def body(rhs_c, rhs_n, rec_c, rec_n, core_inverse, block, m_inverse, t):
        traits, held = rhs_c.shape
        width = held // groups
        many = rhs_n.shape[1]
        m_row = m_inverse[None, :]
        core, non, own = ((traits, held), F32), ((traits, many), F32), ((traits, width), F32)
        lanes, mixer = ((1, LANES), F32), ((traits, traits * LANES), F32)
        plain = ((parts, traits, width), BF16)
        tailed = ((parts, traits, width + LANES), BF16)
        double = ((parts, traits, held), BF16)
        near = ((traits, many), BF16)
        full = [pltpu.VMEM((traits, parts * width), BF16)]
        chips = [c for g in range(groups) for c in range(cores)]
        places = [c * groups + g for g in range(groups) for c in range(cores)]
        part = functools.partial

        (early,) = call(early_kernel, [((traits, LANES), F32)])()
        sent, dir_c, dir_n, rz, prec_c, prec_n, tb = call(
            part(begin_kernel, groups, width), [plain, core, non, lanes, core, non, mixer]
        )(rhs_c, rhs_n, rec_c, rec_n, m_row, t, early)
        pull = call(part(pull_kernel, groups, width, places), [non, near, lanes], full)
        push = call(part(push_kernel, width, places), [tailed])

        sent, form = call(part(map_first_kernel, groups, width, places), [plain, lanes], full)(
            exchange(sent), core_inverse, dir_c, tb
        )
        image_n, left, curve = pull(exchange(sent), block, m_row, dir_c, dir_n, rec_c, rec_n, form, tb)
        (sent,) = push(left, block, curve, rz)
        sent, step, rz, curve, res_n, z_n, rz_part, cross = call(
            part(rest_first_kernel, groups, width, chips), [double, lanes, lanes, lanes, non, non, lanes, lanes]
        )(exchange(sent), dir_c, core_inverse, rhs_n, image_n, prec_n)
        sent, image_c, res_c, z_c, rz_part, cross = call(
            part(step_kernel, groups, width, places), [plain, core, core, core, lanes, lanes]
        )(exchange(sent), core_inverse, dir_c, rec_c, rhs_c, prec_c, tb, step, rz_part, cross)

        sent, form = call(part(map_next_kernel, groups, width), [plain, lanes])(exchange(sent), z_c, tb)
        image_z, left, curve_z = pull(exchange(sent), block, m_row, z_c, z_n, rec_c, rec_n, form, tb)
        (sent,) = push(left, block, curve_z, rz_part, cross)
        sent, step, factor, sol_c, sol_n, res_n = call(
            part(rest_next_kernel, groups, width, chips), [double, lanes, lanes, core, non, non]
        )(exchange(sent), z_c, core_inverse, z_n, dir_c, dir_n, res_n, image_n, image_z, step, rz, curve)
        return tuple(
            call(
                final_kernel, [core, non, core, non],
                [pltpu.VMEM(*core), pltpu.SemaphoreType.DMA((4,))], FAR_SPEC,
            )(exchange(sent), z_c, rec_c, res_c, image_c, step, factor, tb, sol_c, sol_n, res_n)
        )

    return body


def solution(mesh):
    in_specs = (
        P(None, "cores"),
        P(None, ("grp", "cores")),
        P(None, "cores"),
        P(None, ("grp", "cores")),
        P("cores", None),
        P(("grp", "cores"), None),
        P(("grp", "cores")),
        P(),
    )
    out_specs = (
        P(None, "cores"),
        P(None, ("grp", "cores")),
        P(None, "cores"),
        P(None, ("grp", "cores")),
    )
    groups, cores = mesh.shape["grp"], mesh.shape["cores"]

    def body(rhs_core, *rest):
        fits = rhs_core.shape[1] % (groups * LANES) == 0 and rhs_core.shape[0] >= 4
        make = make_kernel_body if fits else make_plain_body
        return make(groups, cores)(rhs_core, *rest)

    return jax.shard_map(body, mesh=mesh, in_specs=in_specs, out_specs=out_specs, check_vma=False)
```

```python
import functools

import jax
import jax.numpy as jnp
from jax import lax
from jax.experimental import pallas as pl
from jax.experimental.pallas import tpu as pltpu
from jax.sharding import PartitionSpec as P

ITERS = 2
AXES = ("cores", "grp")


def split3(value):
    hi = lax.reduce_precision(value, 8, 7)
    mid = lax.reduce_precision(value - hi, 8, 7)
    low = value - hi - mid
    return jnp.stack([hi, mid, low]).astype(jnp.bfloat16)


def mix(trait_inverse, x):
    return sum(trait_inverse[:, s : s + 1] * x[s : s + 1, :] for s in range(x.shape[0]))


def make_plain_body(groups, cores):
    parts = groups * cores

    def exchange(blocks):
        return lax.all_to_all(blocks, AXES, 0, 0, tiled=False)

    def gather(own, scalars=()):
        traits, width = own.shape
        sent = own.astype(jnp.bfloat16)
        if scalars:
            row = jnp.concatenate([split3(s) for s in scalars])
            row = jnp.pad(row, (0, 128 - row.shape[0]))[None]
            sent = jnp.concatenate([sent, jnp.pad(row, ((0, traits - 1), (0, 0)))], axis=1)
        got = exchange(jnp.broadcast_to(sent[None], (parts,) + sent.shape))
        full = got[:, :, :width].transpose(1, 0, 2).reshape(traits, parts * width)
        if not scalars:
            return full
        tail = got[:, 0, width : width + 3 * len(scalars)].astype(jnp.float32)
        sums = tail.reshape(parts, len(scalars), 3).sum((0, 2))
        return full, sums

    def scatter(partial, width):
        traits = partial.shape[0]
        blocks = partial.astype(jnp.bfloat16).reshape(traits, parts, width).transpose(1, 0, 2)
        return exchange(blocks).astype(jnp.float32).sum(0)

    def times_rows(full, rows):
        return lax.dot_general(full, rows, (((1,), (1,)), ((), ())), preferred_element_type=jnp.float32)

    def body(rhs_core, rhs_non, rec_core, rec_non, core_inverse, block, m_inverse, trait_inverse):
        traits, held = rhs_core.shape
        width = held // groups
        at = lax.axis_index("grp") * width

        def mine(x):
            return lax.dynamic_slice_in_dim(x, at, width, axis=1)

        rows_mine = lax.dynamic_slice_in_dim(core_inverse, at, width, axis=0)
        m_row = m_inverse[None, :]
        trait_diag = jnp.diagonal(trait_inverse)[:, None]
        prec_core = 1.0 / (rec_core + trait_diag)
        prec_non = 1.0 / (rec_non + trait_diag * m_row)
        sol_core, sol_non = jnp.zeros_like(rhs_core), jnp.zeros_like(rhs_non)
        res_core, res_non = rhs_core, rhs_non
        z_core, z_non = prec_core * res_core, prec_non * res_non
        dir_core, dir_non = jnp.zeros_like(z_core), jnp.zeros_like(z_non)
        mapped = jnp.zeros((traits, width), jnp.float32)
        rz_old = None
        for iteration in range(ITERS):
            rz_part = jnp.sum(res_non * z_non) + jnp.sum(mine(res_core * z_core))
            z_full, (rz,) = gather(mine(z_core), (rz_part,))
            z_mapped = times_rows(z_full, rows_mine)
            if iteration:
                factor = rz / rz_old
                mapped = z_mapped + factor * mapped
                dir_core = z_core + factor * dir_core
                dir_non = z_non + factor * dir_non
            else:
                mapped, dir_core, dir_non = z_mapped, z_core, z_non
            rz_old = rz
            mapped_full = gather(mapped)
            scaled = m_row * (dir_non - times_rows(mapped_full, block))
            pushed = scatter(
                jnp.dot(scaled.astype(jnp.bfloat16), block, preferred_element_type=jnp.float32), width
            )
            remainder = mine(dir_core) - pushed
            image_non = rec_non * dir_non + mix(trait_inverse, scaled)
            curve_part = (
                jnp.sum(dir_non * image_non)
                + jnp.sum(mine(rec_core * dir_core * dir_core))
                + jnp.sum(mapped * mix(trait_inverse, remainder))
            )
            rem_full, (curve,) = gather(remainder, (curve_part,))
            core_out = times_rows(rem_full, core_inverse)
            image_core = rec_core * dir_core + mix(trait_inverse, core_out)
            step = rz / curve
            sol_core = sol_core + step * dir_core
            sol_non = sol_non + step * dir_non
            res_core = res_core - step * image_core
            res_non = res_non - step * image_non
            z_core, z_non = prec_core * res_core, prec_non * res_non
        return sol_core, sol_non, res_core, res_non

    return body

LANES = 128
F32 = jnp.float32
BF16 = jnp.bfloat16
VMEM_SPEC = pl.BlockSpec(memory_space=pltpu.VMEM)
FAR_SPEC = pl.BlockSpec(memory_space=pltpu.HBM)
GRANT = 20 * 2**20
WORK = 10**8


def lane_sum(x):
    row = jnp.sum(x, axis=0, keepdims=True)
    out = row[:, :LANES]
    for k in range(LANES, row.shape[1], LANES):
        out = out + row[:, k : k + LANES]
    return out


def all_lanes(x):
    shift = LANES // 2
    while shift:
        x = x + pltpu.roll(x, shift, 1)
        shift //= 2
    return x


def wide(x, lanes):
    return jnp.concatenate([x] * (lanes // LANES), axis=1) if lanes > LANES else x


def trait_mix(tb_ref, x):
    out = None
    for s in range(x.shape[0]):
        term = wide(tb_ref[:, s * LANES : (s + 1) * LANES], x.shape[1]) * x[s : s + 1, :]
        out = term if out is None else out + term
    return out


def rows_times(full_ref, got_ref, rows, width, places):
    for r, place in enumerate(places):
        full_ref[:, place * width : (place + 1) * width] = got_ref[r]
    dims = (((1,), (1,)), ((), ()))
    a, b = [], []
    step = 512
    for k in range(0, full_ref.shape[1], 4 * step):
        for j in range(2):
            x = slice(k + j * step, k + (j + 1) * step)
            a.append(lax.dot_general(full_ref[:, x], rows[:, x], dims, preferred_element_type=F32))
        for j in range(2, 4):
            y = slice(k + j * step, k + (j + 1) * step)
            b.append(lax.dot_general(rows[:, y], full_ref[:, y], dims, preferred_element_type=F32))
    return sum(a[1:], a[0]) + sum(b[1:], b[0]).T


def put_products(sent_ref, left, rows_ref, at, count, width, places):
    for block in sorted(set(places)):
        part = jnp.dot(
            left, rows_ref[pl.ds(at, count), block * width : (block + 1) * width], preferred_element_type=F32
        ).astype(BF16)
        for r, place in enumerate(places):
            if place == block:
                sent_ref[r, :, :width] = part


def put_all(sent_ref, own, width):
    value = own.astype(BF16)
    sent_ref[:, :, :width] = jnp.broadcast_to(value[None], (sent_ref.shape[0],) + value.shape)


def tail_slot(shape, k):
    return lax.broadcasted_iota(jnp.int32, shape, 1) // (LANES // 4) == k


def put_sums(sent_ref, sums):
    width = sent_ref.shape[2] - LANES
    shape = (2, LANES)
    row = lax.broadcasted_iota(jnp.int32, shape, 0)
    tail = jnp.zeros(shape, F32)
    for k, value in enumerate(sums):
        value = value + pltpu.roll(value, LANES // 2, 1)
        value = value + pltpu.roll(value, LANES // 4, 1)
        high = value.astype(BF16).astype(F32)
        tail = jnp.where(tail_slot(shape, k), jnp.where(row == 0, high, value - high), tail)
    tail = tail.astype(BF16)
    sent_ref[:, :, width:] = jnp.broadcast_to(tail[None], (sent_ref.shape[0],) + shape)


def put_folded(sent_ref, left, rows_ref, width, places):
    for r, place in enumerate(places):
        part = jnp.dot(
            left, rows_ref[:, place * width : (place + 1) * width], preferred_element_type=F32
        ).astype(BF16)
        for k in range(part.shape[0] // 2):
            sent_ref[r, :, k * width : (k + 1) * width] = part[2 * k : 2 * k + 2]


def get_folded(got_ref, width):
    both = jnp.sum(got_ref[...].astype(F32), axis=0)
    pairs = (both.shape[1] - LANES) // width
    block = jnp.concatenate([both[:, k * width : (k + 1) * width] for k in range(pairs)], axis=0)
    return block, both[:, pairs * width : pairs * width + LANES]


def get_sums(tail, count):
    out = []
    for k in range(count):
        rows = all_lanes(jnp.where(tail_slot(tail.shape, k), tail, 0.0))
        out.append(rows[0:1] + rows[1:2])
    return out


def own_part(x, groups, width):
    part = x[:, :width]
    for k in range(1, groups):
        part = jnp.where(lax.axis_index("grp") == k, x[:, k * width : (k + 1) * width], part)
    return part


def early_kernel(out):
    out[...] = jnp.zeros_like(out)


def begin_kernel(
    groups, width, rhs_c, rhs_n, rec_c, rec_n, m_ref, t_ref, early, sent, dir_c, dir_n, rz, prec_c, prec_n, tb
):
    traits = t_ref.shape[0]
    row = lax.broadcasted_iota(jnp.int32, (traits, LANES), 0)
    diag = early[...]
    for s in range(traits):
        column = jnp.broadcast_to(t_ref[:, s : s + 1], (traits, LANES))
        tb[:, s * LANES : (s + 1) * LANES] = column
        diag = jnp.where(row == s, column, diag)
    part_c = 1.0 / (rec_c[...] + wide(diag, rec_c.shape[1]))
    z_c = part_c * rhs_c[...]
    put_all(sent, own_part(z_c, groups, width), width)
    part_n = 1.0 / (rec_n[...] + wide(diag, rec_n.shape[1]) * m_ref[...])
    z_n = part_n * rhs_n[...]
    prec_c[...] = part_c
    prec_n[...] = part_n
    dir_c[...] = z_c
    dir_n[...] = z_n
    rz[...] = lane_sum(rhs_n[...] * z_n) + lane_sum(own_part(rhs_c[...] * z_c, groups, width))


def own_rows(width):
    return pl.multiple_of(lax.axis_index("grp") * width, LANES)


def map_first_kernel(groups, width, places, got, c_ref, vec_c, tb, sent, form, full):
    out = rows_times(full, got, c_ref[pl.ds(own_rows(width), width), :], width, places)
    put_all(sent, out, width)
    form[...] = lane_sum(out * trait_mix(tb, own_part(vec_c[...], groups, width)))


def map_next_kernel(groups, width, got, vec_c, tb, sent, form):
    out = jnp.sum(got[...].astype(F32), axis=0)
    put_all(sent, out, width)
    form[...] = lane_sum(out * trait_mix(tb, own_part(vec_c[...], groups, width)))


def pull_kernel(
    groups, width, places, got, g_ref, m_ref, vec_c, vec_n, rec_c, rec_n, form, tb, image_n, left, curve, full
):
    pulled = rows_times(full, got, g_ref[...], width, places)
    differ = vec_n[...] - pulled
    scaled = m_ref[...] * differ
    left[...] = scaled.astype(BF16)
    mixed = trait_mix(tb, scaled)
    weighted = rec_n[...] * vec_n[...]
    image_n[...] = weighted + mixed
    curve[...] = (
        form[...]
        + lane_sum(vec_n[...] * weighted + differ * mixed)
        + lane_sum(own_part(rec_c[...] * vec_c[...] * vec_c[...], groups, width))
    )


def push_kernel(width, places, left, g_ref, *others):
    sent, sums = others[-1], others[:-1]
    put_sums(sent, [one[...] for one in sums])
    put_folded(sent, left[...], g_ref, width, places)


def put_remainder(groups, width, chips, got, vec_c, c_ref, sent):
    pushed, tail = get_folded(got, width)
    rest = (own_part(vec_c[...], groups, width) - pushed).astype(BF16)
    put_products(sent, rest, c_ref, own_rows(width), width, groups * width, chips)
    return tail


def rest_first_kernel(
    groups, width, chips, got, dir_c, c_ref, rhs_n, image_n, prec_n,
    sent, step_out, rz_out, curve_out, res_n_out, z_n_out, rz_part, cross_part,
):
    tail = put_remainder(groups, width, chips, got, dir_c, c_ref, sent)
    curve, rz = get_sums(tail, 2)
    step = rz / curve
    step_out[...] = step
    rz_out[...] = rz
    curve_out[...] = curve
    res_n = rhs_n[...] - wide(step, rhs_n.shape[1]) * image_n[...]
    z_n = prec_n[...] * res_n
    res_n_out[...] = res_n
    z_n_out[...] = z_n
    rz_part[...] = lane_sum(res_n * z_n)
    cross_part[...] = lane_sum(z_n * image_n[...])


def step_kernel(
    groups, width, places, got, c_ref, dir_c, rec_c, rhs_c, prec_c, tb, step, rz_in, cross_in,
    sent, image_c_out, res_c_out, z_c_out, rz_part, cross_part,
):
    core_out = jnp.sum(got[...].astype(F32), axis=0)
    image_c = rec_c[...] * dir_c[...] + trait_mix(tb, core_out)
    res_c = rhs_c[...] - wide(step[...], rhs_c.shape[1]) * image_c
    z_c = prec_c[...] * res_c
    left = own_part(z_c, groups, width).astype(BF16)
    put_products(sent, left, c_ref, own_rows(width), width, width, places)
    image_c_out[...] = image_c
    res_c_out[...] = res_c
    z_c_out[...] = z_c
    rz_part[...] = rz_in[...] + lane_sum(own_part(res_c * z_c, groups, width))
    cross_part[...] = cross_in[...] + lane_sum(own_part(z_c * image_c, groups, width))


def rest_next_kernel(
    groups, width, chips, got, z_c, c_ref, z_n, dir_c, dir_n, res_n, image_n, image_z, old_step, old_rz, old_curve,
    sent, step_out, factor_out, sol_c, sol_n, res_n_out,
):
    tail = put_remainder(groups, width, chips, got, z_c, c_ref, sent)
    curve_z, rz, cross = get_sums(tail, 3)
    factor = rz / old_rz[...]
    step = rz / (curve_z + factor * (2.0 * cross + factor * old_curve[...]))
    step_out[...] = step
    factor_out[...] = factor
    held, many = z_c.shape[1], z_n.shape[1]
    sol_c[...] = wide(old_step[...] + step * factor, held) * dir_c[...] + wide(step, held) * z_c[...]
    sol_n[...] = wide(old_step[...] + step * factor, many) * dir_n[...] + wide(step, many) * z_n[...]
    res_n_out[...] = res_n[...] - wide(step, many) * (image_z[...] + wide(factor, many) * image_n[...])


def final_kernel(
    got, z_c, rec_c, res_c, image_c, step, factor, tb, sol_c, sol_n, res_n,
    sol_c_far, sol_n_far, res_c_far, res_n_far, res_c_out, sems,
):
    pairs = ((sol_c, sol_c_far), (sol_n, sol_n_far), (res_n, res_n_far), (res_c_out, res_c_far))
    copies = [pltpu.make_async_copy(near, far, sems.at[k]) for k, (near, far) in enumerate(pairs)]
    for copy in copies[:3]:
        copy.start()
    held = z_c.shape[1]
    core_out = jnp.sum(got[...].astype(F32), axis=0)
    image = rec_c[...] * z_c[...] + trait_mix(tb, core_out) + wide(factor[...], held) * image_c[...]
    res_c_out[...] = res_c[...] - wide(step[...], held) * image
    copies[3].start()
    for copy in copies:
        copy.wait()


def call(kernel, outs, scratch=(), out_spec=VMEM_SPEC):
    def run(*args):
        return pl.pallas_call(
            kernel,
            out_shape=[jax.ShapeDtypeStruct(shape, dtype) for shape, dtype in outs],
            in_specs=[VMEM_SPEC] * len(args),
            out_specs=[out_spec] * len(outs),
            scratch_shapes=list(scratch),
            compiler_params=pltpu.CompilerParams(vmem_limit_bytes=GRANT),
            cost_estimate=pl.CostEstimate(flops=WORK, transcendentals=WORK, bytes_accessed=2**20),
        )(*args)

    return run


def make_kernel_body(groups, cores):
    parts = groups * cores

    def exchange(blocks):
        return lax.all_to_all(blocks, ("grp", "cores"), 0, 0, tiled=False)

    def body(rhs_c, rhs_n, rec_c, rec_n, core_inverse, block, m_inverse, t):
        traits, held = rhs_c.shape
        width = held // groups
        many = rhs_n.shape[1]
        m_row = m_inverse[None, :]
        core, non, own = ((traits, held), F32), ((traits, many), F32), ((traits, width), F32)
        lanes, mixer = ((1, LANES), F32), ((traits, traits * LANES), F32)
        plain = ((parts, traits, width), BF16)
        tailed = ((parts, 2, traits // 2 * width + LANES), BF16)
        double = ((parts, traits, held), BF16)
        near = ((traits, many), BF16)
        full = [pltpu.VMEM((traits, parts * width), BF16)]
        chips = [c for g in range(groups) for c in range(cores)]
        places = [c * groups + g for g in range(groups) for c in range(cores)]
        part = functools.partial

        (early,) = call(early_kernel, [((traits, LANES), F32)])()
        sent, dir_c, dir_n, rz, prec_c, prec_n, tb = call(
            part(begin_kernel, groups, width), [plain, core, non, lanes, core, non, mixer]
        )(rhs_c, rhs_n, rec_c, rec_n, m_row, t, early)
        pull = call(part(pull_kernel, groups, width, places), [non, near, lanes], full)
        push = call(part(push_kernel, width, places), [tailed])

        sent, form = call(part(map_first_kernel, groups, width, places), [plain, lanes], full)(
            exchange(sent), core_inverse, dir_c, tb
        )
        image_n, left, curve = pull(exchange(sent), block, m_row, dir_c, dir_n, rec_c, rec_n, form, tb)
        (sent,) = push(left, block, curve, rz)
        sent, step, rz, curve, res_n, z_n, rz_part, cross = call(
            part(rest_first_kernel, groups, width, chips), [double, lanes, lanes, lanes, non, non, lanes, lanes]
        )(exchange(sent), dir_c, core_inverse, rhs_n, image_n, prec_n)
        sent, image_c, res_c, z_c, rz_part, cross = call(
            part(step_kernel, groups, width, places), [plain, core, core, core, lanes, lanes]
        )(exchange(sent), core_inverse, dir_c, rec_c, rhs_c, prec_c, tb, step, rz_part, cross)

        sent, form = call(part(map_next_kernel, groups, width), [plain, lanes])(exchange(sent), z_c, tb)
        image_z, left, curve_z = pull(exchange(sent), block, m_row, z_c, z_n, rec_c, rec_n, form, tb)
        (sent,) = push(left, block, curve_z, rz_part, cross)
        sent, step, factor, sol_c, sol_n, res_n = call(
            part(rest_next_kernel, groups, width, chips), [double, lanes, lanes, core, non, non]
        )(exchange(sent), z_c, core_inverse, z_n, dir_c, dir_n, res_n, image_n, image_z, step, rz, curve)
        return tuple(
            call(
                final_kernel, [core, non, core, non],
                [pltpu.VMEM(*core), pltpu.SemaphoreType.DMA((4,))], FAR_SPEC,
            )(exchange(sent), z_c, rec_c, res_c, image_c, step, factor, tb, sol_c, sol_n, res_n)
        )

    return body


def solution(mesh):
    in_specs = (
        P(None, "cores"),
        P(None, ("grp", "cores")),
        P(None, "cores"),
        P(None, ("grp", "cores")),
        P("cores", None),
        P(("grp", "cores"), None),
        P(("grp", "cores")),
        P(),
    )
    out_specs = (
        P(None, "cores"),
        P(None, ("grp", "cores")),
        P(None, "cores"),
        P(None, ("grp", "cores")),
    )
    groups, cores = mesh.shape["grp"], mesh.shape["cores"]

    def body(rhs_core, *rest):
        fits = rhs_core.shape[1] % (groups * LANES) == 0 and rhs_core.shape[0] % 2 == 0
        make = make_kernel_body if fits else make_plain_body
        return make(groups, cores)(rhs_core, *rest)

    return jax.shard_map(body, mesh=mesh, in_specs=in_specs, out_specs=out_specs, check_vma=False)
```

```python
import functools

import jax
import jax.numpy as jnp
from jax import lax
from jax.experimental import pallas as pl
from jax.experimental.pallas import tpu as pltpu
from jax.sharding import PartitionSpec as P

ITERS = 2
AXES = ("z", "y", "x", "grp")


def split3(value):
    hi = lax.reduce_precision(value, 8, 7)
    mid = lax.reduce_precision(value - hi, 8, 7)
    low = value - hi - mid
    return jnp.stack([hi, mid, low]).astype(jnp.bfloat16)


def mix(trait_inverse, x):
    return sum(trait_inverse[:, s : s + 1] * x[s : s + 1, :] for s in range(x.shape[0]))


def make_plain_body(groups, cores):
    parts = groups * cores

    def exchange(blocks):
        return lax.all_to_all(blocks, AXES, 0, 0, tiled=False)

    def gather(own, scalars=()):
        traits, width = own.shape
        sent = own.astype(jnp.bfloat16)
        if scalars:
            row = jnp.concatenate([split3(s) for s in scalars])
            row = jnp.pad(row, (0, 128 - row.shape[0]))[None]
            sent = jnp.concatenate([sent, jnp.pad(row, ((0, traits - 1), (0, 0)))], axis=1)
        got = exchange(jnp.broadcast_to(sent[None], (parts,) + sent.shape))
        full = got[:, :, :width].transpose(1, 0, 2).reshape(traits, parts * width)
        if not scalars:
            return full
        tail = got[:, 0, width : width + 3 * len(scalars)].astype(jnp.float32)
        sums = tail.reshape(parts, len(scalars), 3).sum((0, 2))
        return full, sums

    def scatter(partial, width):
        traits = partial.shape[0]
        blocks = partial.astype(jnp.bfloat16).reshape(traits, parts, width).transpose(1, 0, 2)
        return exchange(blocks).astype(jnp.float32).sum(0)

    def times_rows(full, rows):
        return lax.dot_general(full, rows, (((1,), (1,)), ((), ())), preferred_element_type=jnp.float32)

    def body(rhs_core, rhs_non, rec_core, rec_non, core_inverse, block, m_inverse, trait_inverse):
        traits, held = rhs_core.shape
        width = held // groups
        at = lax.axis_index("grp") * width

        def mine(x):
            return lax.dynamic_slice_in_dim(x, at, width, axis=1)

        rows_mine = lax.dynamic_slice_in_dim(core_inverse, at, width, axis=0)
        m_row = m_inverse[None, :]
        trait_diag = jnp.diagonal(trait_inverse)[:, None]
        prec_core = 1.0 / (rec_core + trait_diag)
        prec_non = 1.0 / (rec_non + trait_diag * m_row)
        sol_core, sol_non = jnp.zeros_like(rhs_core), jnp.zeros_like(rhs_non)
        res_core, res_non = rhs_core, rhs_non
        z_core, z_non = prec_core * res_core, prec_non * res_non
        dir_core, dir_non = jnp.zeros_like(z_core), jnp.zeros_like(z_non)
        mapped = jnp.zeros((traits, width), jnp.float32)
        rz_old = None
        for iteration in range(ITERS):
            rz_part = jnp.sum(res_non * z_non) + jnp.sum(mine(res_core * z_core))
            z_full, (rz,) = gather(mine(z_core), (rz_part,))
            z_mapped = times_rows(z_full, rows_mine)
            if iteration:
                factor = rz / rz_old
                mapped = z_mapped + factor * mapped
                dir_core = z_core + factor * dir_core
                dir_non = z_non + factor * dir_non
            else:
                mapped, dir_core, dir_non = z_mapped, z_core, z_non
            rz_old = rz
            mapped_full = gather(mapped)
            scaled = m_row * (dir_non - times_rows(mapped_full, block))
            pushed = scatter(
                jnp.dot(scaled.astype(jnp.bfloat16), block, preferred_element_type=jnp.float32), width
            )
            remainder = mine(dir_core) - pushed
            image_non = rec_non * dir_non + mix(trait_inverse, scaled)
            curve_part = (
                jnp.sum(dir_non * image_non)
                + jnp.sum(mine(rec_core * dir_core * dir_core))
                + jnp.sum(mapped * mix(trait_inverse, remainder))
            )
            rem_full, (curve,) = gather(remainder, (curve_part,))
            core_out = times_rows(rem_full, core_inverse)
            image_core = rec_core * dir_core + mix(trait_inverse, core_out)
            step = rz / curve
            sol_core = sol_core + step * dir_core
            sol_non = sol_non + step * dir_non
            res_core = res_core - step * image_core
            res_non = res_non - step * image_non
            z_core, z_non = prec_core * res_core, prec_non * res_non
        return sol_core, sol_non, res_core, res_non

    return body

LANES = 128
F32 = jnp.float32
BF16 = jnp.bfloat16
VMEM_SPEC = pl.BlockSpec(memory_space=pltpu.VMEM)
FAR_SPEC = pl.BlockSpec(memory_space=pltpu.HBM)
GRANT = 20 * 2**20
WORK = 10**8


def lane_sum(x):
    row = jnp.sum(x, axis=0, keepdims=True)
    out = row[:, :LANES]
    for k in range(LANES, row.shape[1], LANES):
        out = out + row[:, k : k + LANES]
    return out


def all_lanes(x):
    shift = LANES // 2
    while shift:
        x = x + pltpu.roll(x, shift, 1)
        shift //= 2
    return x


def wide(x, lanes):
    return jnp.concatenate([x] * (lanes // LANES), axis=1) if lanes > LANES else x


def trait_mix(tb_ref, x):
    out = None
    for s in range(x.shape[0]):
        term = wide(tb_ref[:, s * LANES : (s + 1) * LANES], x.shape[1]) * x[s : s + 1, :]
        out = term if out is None else out + term
    return out


def rows_times(full_ref, rows):
    dims = (((1,), (1,)), ((), ()))
    piece = 4 * LANES
    if full_ref.shape[1] % (4 * piece):
        return lax.dot_general(full_ref[...], rows, dims, preferred_element_type=F32)
    left, right = [], []
    for k in range(0, full_ref.shape[1], piece):
        at = slice(k, k + piece)
        if k // piece % 4 < 2:
            left.append(lax.dot_general(full_ref[:, at], rows[:, at], dims, preferred_element_type=F32))
        else:
            right.append(lax.dot_general(rows[:, at], full_ref[:, at], dims, preferred_element_type=F32))
    return sum(left[1:], left[0]) + sum(right[1:], right[0]).T


def put_full(full_ref, got_ref, first, width, places):
    traits = got_ref.shape[1]
    for r, place in enumerate(places):
        full_ref[first : first + traits, place * width : (place + 1) * width] = got_ref[r]


def put_products(sent_ref, left, rows_ref, at, width, places):
    for r, place in enumerate(places):
        rows = rows_ref[pl.ds(at, width), place * width : (place + 1) * width]
        sent_ref[r] = jnp.dot(left, rows, preferred_element_type=F32).astype(BF16)


def put_all(sent_ref, own, width):
    value = own.astype(BF16)
    sent_ref[:, :, :width] = jnp.broadcast_to(value[None], (sent_ref.shape[0],) + value.shape)


def tail_slot(shape, k):
    return lax.broadcasted_iota(jnp.int32, shape, 1) // (LANES // 4) == k


def put_sums(sent_ref, sums):
    width = sent_ref.shape[2] - LANES
    shape = (2, LANES)
    row = lax.broadcasted_iota(jnp.int32, shape, 0)
    tail = jnp.zeros(shape, F32)
    for k, value in enumerate(sums):
        value = value + pltpu.roll(value, LANES // 2, 1)
        value = value + pltpu.roll(value, LANES // 4, 1)
        high = value.astype(BF16).astype(F32)
        tail = jnp.where(tail_slot(shape, k), jnp.where(row == 0, high, value - high), tail)
    tail = tail.astype(BF16)
    sent_ref[:, :, width:] = jnp.broadcast_to(tail[None], (sent_ref.shape[0],) + shape)


def put_folded(sent_ref, left, rows_ref, width, places):
    for r, place in enumerate(places):
        part = jnp.dot(
            left, rows_ref[:, place * width : (place + 1) * width], preferred_element_type=F32
        ).astype(BF16)
        for k in range(part.shape[0] // 2):
            sent_ref[r, :, k * width : (k + 1) * width] = part[2 * k : 2 * k + 2]


def get_folded(got_ref, width):
    both = jnp.sum(got_ref[...].astype(F32), axis=0)
    pairs = (both.shape[1] - LANES) // width
    block = jnp.concatenate([both[:, k * width : (k + 1) * width] for k in range(pairs)], axis=0)
    return block, both[:, pairs * width : pairs * width + LANES]


def get_sums(tail, count):
    out = []
    for k in range(count):
        rows = all_lanes(jnp.where(tail_slot(tail.shape, k), tail, 0.0))
        out.append(rows[0:1] + rows[1:2])
    return out


def own_part(x, groups, width):
    part = x[:, :width]
    for k in range(1, groups):
        part = jnp.where(lax.axis_index("grp") == k, x[:, k * width : (k + 1) * width], part)
    return part


def early_kernel(out):
    out[...] = jnp.zeros_like(out)


def begin_kernel(
    groups, width, rhs_c, rhs_n, rec_c, rec_n, m_ref, t_ref, early, sent, dir_c, dir_n, rz, prec_c, prec_n, tb
):
    traits = t_ref.shape[0]
    row = lax.broadcasted_iota(jnp.int32, (traits, LANES), 0)
    diag = early[...]
    for s in range(traits):
        column = jnp.broadcast_to(t_ref[:, s : s + 1], (traits, LANES))
        tb[:, s * LANES : (s + 1) * LANES] = column
        diag = jnp.where(row == s, column, diag)
    part_c = 1.0 / (rec_c[...] + wide(diag, rec_c.shape[1]))
    z_c = part_c * rhs_c[...]
    put_all(sent, own_part(z_c, groups, width), width)
    part_n = 1.0 / (rec_n[...] + wide(diag, rec_n.shape[1]) * m_ref[...])
    z_n = part_n * rhs_n[...]
    prec_c[...] = part_c
    prec_n[...] = part_n
    dir_c[...] = z_c
    dir_n[...] = z_n
    rz[...] = lane_sum(rhs_n[...] * z_n) + lane_sum(own_part(rhs_c[...] * z_c, groups, width))


def own_rows(width):
    return pl.multiple_of(lax.axis_index("grp") * width, LANES)


def core_form(mapped, own, record, tb):
    return lane_sum(mapped * trait_mix(tb, own) + record * own * own)


def map_first_kernel(groups, width, places, got, c_ref, dir_c, rec_c, tb, sent, form, full):
    put_full(full, got, 0, width, places)
    out = rows_times(full, c_ref[pl.ds(own_rows(width), width), :])
    put_all(sent, out, width)
    form[...] = core_form(out, own_part(dir_c[...], groups, width), own_part(rec_c[...], groups, width), tb)


def map_next_kernel(groups, width, got, z_own, rec_c, tb, sent, form):
    out = jnp.sum(got[...].astype(F32), axis=0)
    put_all(sent, out, width)
    form[...] = core_form(out, z_own[...], own_part(rec_c[...], groups, width), tb)


def pull_kernel(width, places, got, g_ref, m_ref, vec_n, rec_n, form, tb, image_n, left, curve, full):
    put_full(full, got, 0, width, places)
    differ = vec_n[...] - rows_times(full, g_ref[...])
    scaled = m_ref[...] * differ
    left[...] = scaled.astype(BF16)
    mixed = trait_mix(tb, scaled)
    weighted = rec_n[...] * vec_n[...]
    image_n[...] = weighted + mixed
    curve[...] = form[...] + lane_sum(vec_n[...] * weighted + differ * mixed)


def push_kernel(width, places, left, g_ref, *others):
    sent, sums = others[-1], others[:-1]
    put_sums(sent, [one[...] for one in sums])
    put_folded(sent, left[...], g_ref, width, places)


def rest_first_kernel(
    groups, width, places, got, dir_c, c_ref, rhs_n, image_n, prec_n,
    sent, step_out, rz_out, curve_out, res_n_out, z_n_out, rz_part, cross_part,
):
    pushed, tail = get_folded(got, width)
    left = (own_part(dir_c[...], groups, width) - pushed).astype(BF16)
    put_products(sent, left, c_ref, own_rows(width), width, places)
    curve, rz = get_sums(tail, 2)
    step = rz / curve
    step_out[...] = step
    rz_out[...] = rz
    curve_out[...] = curve
    res_n = rhs_n[...] - wide(step, rhs_n.shape[1]) * image_n[...]
    z_n = prec_n[...] * res_n
    res_n_out[...] = res_n
    z_n_out[...] = z_n
    rz_part[...] = lane_sum(res_n * z_n)
    cross_part[...] = lane_sum(z_n * image_n[...])


def step_kernel(
    groups, width, places, got, c_ref, dir_c, rec_c, rhs_c, prec_c, tb, step, rz_in, cross_in,
    sent, core_own, z_own, rz_part, cross_part,
):
    def mine(ref):
        return own_part(ref[...], groups, width)

    core_out = jnp.sum(got[...].astype(F32), axis=0)
    image = mine(rec_c) * mine(dir_c) + trait_mix(tb, core_out)
    res = mine(rhs_c) - wide(step[...], width) * image
    z = mine(prec_c) * res
    put_products(sent, z.astype(BF16), c_ref, own_rows(width), width, places)
    core_own[...] = core_out
    z_own[...] = z
    rz_part[...] = rz_in[...] + lane_sum(res * z)
    cross_part[...] = cross_in[...] + lane_sum(z * image)


def rest_next_kernel(
    width, places, got, z_own, c_ref, z_n, dir_n, res_n, image_n, image_z, old_step, old_rz, old_curve,
    sent, step_out, factor_out, sol_n, res_n_out,
):
    pushed, tail = get_folded(got, width)
    put_products(sent, (z_own[...] - pushed).astype(BF16), c_ref, own_rows(width), width, places)
    curve_z, rz, cross = get_sums(tail, 3)
    factor = rz / old_rz[...]
    step = rz / (curve_z + factor * (2.0 * cross + factor * old_curve[...]))
    step_out[...] = step
    factor_out[...] = factor
    many = z_n.shape[1]
    sol_n[...] = wide(old_step[...] + step * factor, many) * dir_n[...] + wide(step, many) * z_n[...]
    res_n_out[...] = res_n[...] - wide(step, many) * (image_z[...] + wide(factor, many) * image_n[...])


def pair_kernel(got, core_own, both):
    traits = core_own.shape[0]
    both[:traits] = core_own[...]
    both[traits:] = jnp.sum(got[...].astype(F32), axis=0)


def final_kernel(
    groups, width, dir_c, rec_c, rhs_c, prec_c, tb, first, second, ratio, sol_n, res_n, *refs
):
    pieces, (sol_c_far, sol_n_far, res_c_far, res_n_far, sol_c, res_c, sems) = refs[:groups], refs[groups:]
    pairs = ((sol_n, sol_n_far), (res_n, res_n_far), (sol_c, sol_c_far), (res_c, res_c_far))
    copies = [pltpu.make_async_copy(near, far, sems.at[k]) for k, (near, far) in enumerate(pairs)]
    copies[0].start()
    copies[1].start()
    traits = dir_c.shape[0]
    early = wide(first[...] + second[...] * ratio[...], width)
    old, new, mixed = wide(first[...], width), wide(second[...], width), wide(ratio[...], width)
    here = lax.axis_index("grp")
    for block in range(groups):
        both = pieces[0][...]
        for k in range(1, groups):
            both = jnp.where(here == (block + k) % groups, pieces[k][...], both)
        at = slice(block * width, (block + 1) * width)
        image = rec_c[:, at] * dir_c[:, at] + trait_mix(tb, both[:traits])
        res = rhs_c[:, at] - old * image
        z = prec_c[:, at] * res
        sol_c[:, at] = early * dir_c[:, at] + new * z
        res_c[:, at] = res - new * (rec_c[:, at] * z + trait_mix(tb, both[traits:]) + mixed * image)
    copies[2].start()
    copies[3].start()
    for copy in copies:
        copy.wait()


def call(kernel, outs, scratch=(), out_spec=VMEM_SPEC):
    def run(*args):
        return pl.pallas_call(
            kernel,
            out_shape=[jax.ShapeDtypeStruct(shape, dtype) for shape, dtype in outs],
            in_specs=[VMEM_SPEC] * len(args),
            out_specs=[out_spec] * len(outs),
            scratch_shapes=list(scratch),
            compiler_params=pltpu.CompilerParams(vmem_limit_bytes=GRANT),
            cost_estimate=pl.CostEstimate(flops=WORK, transcendentals=WORK, bytes_accessed=2**20),
        )(*args)

    return run


def make_kernel_body(groups, cores):
    parts = groups * cores

    def exchange(blocks):
        return lax.all_to_all(blocks, ("x", "grp", "z", "y"), 0, 0, tiled=False)

    def body(rhs_c, rhs_n, rec_c, rec_n, core_inverse, block, m_inverse, t):
        traits, held = rhs_c.shape
        width = held // groups
        many = rhs_n.shape[1]
        m_row = m_inverse[None, :]
        core, non, own = ((traits, held), F32), ((traits, many), F32), ((traits, width), F32)
        lanes, mixer = ((1, LANES), F32), ((traits, traits * LANES), F32)
        plain = ((parts, traits, width), BF16)
        tailed = ((parts, 2, traits // 2 * width + LANES), BF16)
        near = ((traits, many), BF16)
        full = [pltpu.VMEM((traits, parts * width), BF16)]
        places = [
            ((z * 2 + y) * 2 + x) * groups + g
            for x in range(2) for g in range(groups) for z in range(cores // 4) for y in range(2)
        ]
        part = functools.partial

        (early,) = call(early_kernel, [((traits, LANES), F32)])()
        sent, dir_c, dir_n, rz, prec_c, prec_n, tb = call(
            part(begin_kernel, groups, width), [plain, core, non, lanes, core, non, mixer]
        )(rhs_c, rhs_n, rec_c, rec_n, m_row, t, early)
        pull = call(part(pull_kernel, width, places), [non, near, lanes], full)
        push = call(part(push_kernel, width, places), [tailed])

        sent, form = call(part(map_first_kernel, groups, width, places), [plain, lanes], full)(
            exchange(sent), core_inverse, dir_c, rec_c, tb
        )
        image_n, left, curve = pull(exchange(sent), block, m_row, dir_n, rec_n, form, tb)
        (sent,) = push(left, block, curve, rz)
        sent, step, rz, curve, res_n, z_n, rz_part, cross = call(
            part(rest_first_kernel, groups, width, places), [plain, lanes, lanes, lanes, non, non, lanes, lanes]
        )(exchange(sent), dir_c, core_inverse, rhs_n, image_n, prec_n)
        sent, core_own, z_own, rz_part, cross = call(
            part(step_kernel, groups, width, places), [plain, own, own, lanes, lanes]
        )(exchange(sent), core_inverse, dir_c, rec_c, rhs_c, prec_c, tb, step, rz_part, cross)

        sent, form = call(part(map_next_kernel, groups, width), [plain, lanes])(exchange(sent), z_own, rec_c, tb)
        image_z, left, curve_z = pull(exchange(sent), block, m_row, z_n, rec_n, form, tb)
        (sent,) = push(left, block, curve_z, rz_part, cross)
        sent, next_step, factor, sol_n, res_n = call(
            part(rest_next_kernel, width, places), [plain, lanes, lanes, non, non]
        )(exchange(sent), z_own, core_inverse, z_n, dir_n, res_n, image_n, image_z, step, rz, curve)
        (both,) = call(pair_kernel, [((2 * traits, width), F32)])(exchange(sent), core_own)
        pieces = [both]
        for k in range(1, groups):
            pieces.append(lax.ppermute(both, "grp", [(g, (g + k) % groups) for g in range(groups)]))
        scratch = [pltpu.VMEM(*core), pltpu.VMEM(*core), pltpu.SemaphoreType.DMA((4,))]
        return tuple(
            call(part(final_kernel, groups, width), [core, non, core, non], scratch, FAR_SPEC)(
                dir_c, rec_c, rhs_c, prec_c, tb, step, next_step, factor, sol_n, res_n, *pieces
            )
        )

    return body


def solution(mesh):
    groups, cores = mesh.shape["grp"], mesh.shape["cores"]
    fine = cores % 4 == 0
    if fine:
        mesh = jax.sharding.Mesh(mesh.devices.reshape(groups, cores // 4, 2, 2), ("grp", "z", "y", "x"))
        c = ("z", "y", "x")
    else:
        c = ("cores",)
    gc = ("grp",) + c
    in_specs = (P(None, c), P(None, gc), P(None, c), P(None, gc), P(c, None), P(gc, None), P(gc), P())
    out_specs = (P(None, c), P(None, gc), P(None, c), P(None, gc))

    def body(rhs_core, *rest):
        fits = fine and rhs_core.shape[1] % (groups * LANES) == 0 and rhs_core.shape[0] % 2 == 0
        make = make_kernel_body if fits else make_plain_body
        return make(groups, cores)(rhs_core, *rest)

    return jax.shard_map(body, mesh=mesh, in_specs=in_specs, out_specs=out_specs, check_vma=False)
```

```python
import functools

import jax
import jax.numpy as jnp
from jax import lax
from jax.experimental import pallas as pl
from jax.experimental.pallas import tpu as pltpu
from jax.sharding import PartitionSpec as P

ITERS = 2
AXES = ("z", "y", "x", "grp")


def split3(value):
    hi = lax.reduce_precision(value, 8, 7)
    mid = lax.reduce_precision(value - hi, 8, 7)
    low = value - hi - mid
    return jnp.stack([hi, mid, low]).astype(jnp.bfloat16)


def mix(trait_inverse, x):
    return sum(trait_inverse[:, s : s + 1] * x[s : s + 1, :] for s in range(x.shape[0]))


def make_plain_body(groups, cores):
    parts = groups * cores

    def exchange(blocks):
        return lax.all_to_all(blocks, AXES, 0, 0, tiled=False)

    def gather(own, scalars=()):
        traits, width = own.shape
        sent = own.astype(jnp.bfloat16)
        if scalars:
            row = jnp.concatenate([split3(s) for s in scalars])
            row = jnp.pad(row, (0, 128 - row.shape[0]))[None]
            sent = jnp.concatenate([sent, jnp.pad(row, ((0, traits - 1), (0, 0)))], axis=1)
        got = exchange(jnp.broadcast_to(sent[None], (parts,) + sent.shape))
        full = got[:, :, :width].transpose(1, 0, 2).reshape(traits, parts * width)
        if not scalars:
            return full
        tail = got[:, 0, width : width + 3 * len(scalars)].astype(jnp.float32)
        sums = tail.reshape(parts, len(scalars), 3).sum((0, 2))
        return full, sums

    def scatter(partial, width):
        traits = partial.shape[0]
        blocks = partial.astype(jnp.bfloat16).reshape(traits, parts, width).transpose(1, 0, 2)
        return exchange(blocks).astype(jnp.float32).sum(0)

    def times_rows(full, rows):
        return lax.dot_general(full, rows, (((1,), (1,)), ((), ())), preferred_element_type=jnp.float32)

    def body(rhs_core, rhs_non, rec_core, rec_non, core_inverse, block, m_inverse, trait_inverse):
        traits, held = rhs_core.shape
        width = held // groups
        at = lax.axis_index("grp") * width

        def mine(x):
            return lax.dynamic_slice_in_dim(x, at, width, axis=1)

        rows_mine = lax.dynamic_slice_in_dim(core_inverse, at, width, axis=0)
        m_row = m_inverse[None, :]
        trait_diag = jnp.diagonal(trait_inverse)[:, None]
        prec_core = 1.0 / (rec_core + trait_diag)
        prec_non = 1.0 / (rec_non + trait_diag * m_row)
        sol_core, sol_non = jnp.zeros_like(rhs_core), jnp.zeros_like(rhs_non)
        res_core, res_non = rhs_core, rhs_non
        z_core, z_non = prec_core * res_core, prec_non * res_non
        dir_core, dir_non = jnp.zeros_like(z_core), jnp.zeros_like(z_non)
        mapped = jnp.zeros((traits, width), jnp.float32)
        rz_old = None
        for iteration in range(ITERS):
            rz_part = jnp.sum(res_non * z_non) + jnp.sum(mine(res_core * z_core))
            z_full, (rz,) = gather(mine(z_core), (rz_part,))
            z_mapped = times_rows(z_full, rows_mine)
            if iteration:
                factor = rz / rz_old
                mapped = z_mapped + factor * mapped
                dir_core = z_core + factor * dir_core
                dir_non = z_non + factor * dir_non
            else:
                mapped, dir_core, dir_non = z_mapped, z_core, z_non
            rz_old = rz
            mapped_full = gather(mapped)
            scaled = m_row * (dir_non - times_rows(mapped_full, block))
            pushed = scatter(
                jnp.dot(scaled.astype(jnp.bfloat16), block, preferred_element_type=jnp.float32), width
            )
            remainder = mine(dir_core) - pushed
            image_non = rec_non * dir_non + mix(trait_inverse, scaled)
            curve_part = (
                jnp.sum(dir_non * image_non)
                + jnp.sum(mine(rec_core * dir_core * dir_core))
                + jnp.sum(mapped * mix(trait_inverse, remainder))
            )
            rem_full, (curve,) = gather(remainder, (curve_part,))
            core_out = times_rows(rem_full, core_inverse)
            image_core = rec_core * dir_core + mix(trait_inverse, core_out)
            step = rz / curve
            sol_core = sol_core + step * dir_core
            sol_non = sol_non + step * dir_non
            res_core = res_core - step * image_core
            res_non = res_non - step * image_non
            z_core, z_non = prec_core * res_core, prec_non * res_non
        return sol_core, sol_non, res_core, res_non

    return body

LANES = 128
F32 = jnp.float32
BF16 = jnp.bfloat16
VMEM_SPEC = pl.BlockSpec(memory_space=pltpu.VMEM)
FAR_SPEC = pl.BlockSpec(memory_space=pltpu.HBM)
GRANT = 20 * 2**20
WORK = 10**8


def lane_sum(x):
    row = jnp.sum(x, axis=0, keepdims=True)
    out = row[:, :LANES]
    for k in range(LANES, row.shape[1], LANES):
        out = out + row[:, k : k + LANES]
    return out


def all_lanes(x):
    shift = LANES // 2
    while shift:
        x = x + pltpu.roll(x, shift, 1)
        shift //= 2
    return x


def wide(x, lanes):
    return jnp.concatenate([x] * (lanes // LANES), axis=1) if lanes > LANES else x


def trait_mix(tb_ref, x):
    out = None
    for s in range(x.shape[0]):
        term = wide(tb_ref[:, s * LANES : (s + 1) * LANES], x.shape[1]) * x[s : s + 1, :]
        out = term if out is None else out + term
    return out


def rows_times(full_ref, rows):
    dims = (((1,), (1,)), ((), ()))
    piece = 2 * LANES
    if full_ref.shape[1] % piece or full_ref.shape[1] == piece:
        return lax.dot_general(full_ref[...], rows, dims, preferred_element_type=F32)
    left, right = [], []
    for n, k in enumerate(range(0, full_ref.shape[1], piece)):
        at = slice(k, k + piece)
        if n % 5 % 2 == 0:
            left.append(lax.dot_general(full_ref[:, at], rows[:, at], dims, preferred_element_type=F32))
        else:
            right.append(lax.dot_general(rows[:, at], full_ref[:, at], dims, preferred_element_type=F32))
    return sum(left[1:], left[0]) + sum(right[1:], right[0]).T


def put_full(full_ref, got_ref, first, width, places):
    traits = got_ref.shape[1]
    for r, place in enumerate(places):
        full_ref[first : first + traits, place * width : (place + 1) * width] = got_ref[r]


def put_products(sent_ref, left, rows_ref, at, width, places):
    for r, place in enumerate(places):
        rows = rows_ref[pl.ds(at, width), place * width : (place + 1) * width]
        sent_ref[r] = jnp.dot(left, rows, preferred_element_type=F32).astype(BF16)


def put_all(sent_ref, own, width):
    value = own.astype(BF16)
    sent_ref[:, :, :width] = jnp.broadcast_to(value[None], (sent_ref.shape[0],) + value.shape)


def tail_slot(shape, k):
    return lax.broadcasted_iota(jnp.int32, shape, 1) // (LANES // 4) == k


def put_sums(sent_ref, sums):
    width = sent_ref.shape[2] - LANES
    shape = (2, LANES)
    row = lax.broadcasted_iota(jnp.int32, shape, 0)
    tail = jnp.zeros(shape, F32)
    for k, value in enumerate(sums):
        value = value + pltpu.roll(value, LANES // 2, 1)
        value = value + pltpu.roll(value, LANES // 4, 1)
        high = value.astype(BF16).astype(F32)
        tail = jnp.where(tail_slot(shape, k), jnp.where(row == 0, high, value - high), tail)
    tail = tail.astype(BF16)
    sent_ref[:, :, width:] = jnp.broadcast_to(tail[None], (sent_ref.shape[0],) + shape)


def put_folded(sent_ref, left, rows_ref, width, places):
    for r, place in enumerate(places):
        part = jnp.dot(
            left, rows_ref[:, place * width : (place + 1) * width], preferred_element_type=F32
        ).astype(BF16)
        for k in range(part.shape[0] // 2):
            sent_ref[r, :, k * width : (k + 1) * width] = part[2 * k : 2 * k + 2]


def get_folded(got_ref, width):
    both = jnp.sum(got_ref[...].astype(F32), axis=0)
    pairs = (both.shape[1] - LANES) // width
    block = jnp.concatenate([both[:, k * width : (k + 1) * width] for k in range(pairs)], axis=0)
    return block, both[:, pairs * width : pairs * width + LANES]


def get_sums(tail, count):
    out = []
    for k in range(count):
        rows = all_lanes(jnp.where(tail_slot(tail.shape, k), tail, 0.0))
        out.append(rows[0:1] + rows[1:2])
    return out


def own_part(x, groups, width):
    part = x[:, :width]
    for k in range(1, groups):
        part = jnp.where(lax.axis_index("grp") == k, x[:, k * width : (k + 1) * width], part)
    return part


def early_kernel(out):
    out[...] = jnp.zeros_like(out)


def begin_kernel(
    groups, width, rhs_c, rhs_n, rec_c, rec_n, m_ref, t_ref, early, sent, dir_c, dir_n, rz, prec_c, prec_n, tb
):
    traits = t_ref.shape[0]
    row = lax.broadcasted_iota(jnp.int32, (traits, LANES), 0)
    diag = early[...]
    for s in range(traits):
        column = jnp.broadcast_to(t_ref[:, s : s + 1], (traits, LANES))
        tb[:, s * LANES : (s + 1) * LANES] = column
        diag = jnp.where(row == s, column, diag)
    part_c = 1.0 / (rec_c[...] + wide(diag, rec_c.shape[1]))
    z_c = part_c * rhs_c[...]
    put_all(sent, own_part(z_c, groups, width), width)
    part_n = 1.0 / (rec_n[...] + wide(diag, rec_n.shape[1]) * m_ref[...])
    z_n = part_n * rhs_n[...]
    prec_c[...] = part_c
    prec_n[...] = part_n
    dir_c[...] = z_c
    dir_n[...] = z_n
    rz[...] = lane_sum(rhs_n[...] * z_n) + lane_sum(own_part(rhs_c[...] * z_c, groups, width))


def own_rows(width):
    return pl.multiple_of(lax.axis_index("grp") * width, LANES)


def core_form(mapped, own, record, tb):
    return lane_sum(mapped * trait_mix(tb, own) + record * own * own)


def map_first_kernel(groups, width, places, got, c_ref, dir_c, rec_c, tb, sent, form, full):
    put_full(full, got, 0, width, places)
    out = rows_times(full, c_ref[pl.ds(own_rows(width), width), :])
    put_all(sent, out, width)
    form[...] = core_form(out, own_part(dir_c[...], groups, width), own_part(rec_c[...], groups, width), tb)


def map_next_kernel(groups, width, got, z_own, rec_c, tb, sent, form):
    out = jnp.sum(got[...].astype(F32), axis=0)
    put_all(sent, out, width)
    form[...] = core_form(out, z_own[...], own_part(rec_c[...], groups, width), tb)


def pull_kernel(width, places, got, g_ref, m_ref, vec_n, rec_n, form, tb, image_n, left, curve, full):
    put_full(full, got, 0, width, places)
    differ = vec_n[...] - rows_times(full, g_ref[...])
    scaled = m_ref[...] * differ
    left[...] = scaled.astype(BF16)
    mixed = trait_mix(tb, scaled)
    weighted = rec_n[...] * vec_n[...]
    image_n[...] = weighted + mixed
    curve[...] = form[...] + lane_sum(vec_n[...] * weighted + differ * mixed)


def push_kernel(width, places, left, g_ref, *others):
    sent, sums = others[-1], others[:-1]
    put_sums(sent, [one[...] for one in sums])
    put_folded(sent, left[...], g_ref, width, places)


def rest_first_kernel(
    groups, width, places, got, dir_c, c_ref, rhs_n, image_n, prec_n,
    sent, step_out, rz_out, curve_out, res_n_out, z_n_out, rz_part, cross_part,
):
    pushed, tail = get_folded(got, width)
    left = (own_part(dir_c[...], groups, width) - pushed).astype(BF16)
    put_products(sent, left, c_ref, own_rows(width), width, places)
    curve, rz = get_sums(tail, 2)
    step = rz / curve
    step_out[...] = step
    rz_out[...] = rz
    curve_out[...] = curve
    res_n = rhs_n[...] - wide(step, rhs_n.shape[1]) * image_n[...]
    z_n = prec_n[...] * res_n
    res_n_out[...] = res_n
    z_n_out[...] = z_n
    rz_part[...] = lane_sum(res_n * z_n)
    cross_part[...] = lane_sum(z_n * image_n[...])


def step_kernel(
    groups, width, places, got, c_ref, dir_c, rec_c, rhs_c, prec_c, tb, step, rz_in, cross_in,
    sent, core_own, z_own, rz_part, cross_part,
):
    def mine(ref):
        return own_part(ref[...], groups, width)

    core_out = jnp.sum(got[...].astype(F32), axis=0)
    image = mine(rec_c) * mine(dir_c) + trait_mix(tb, core_out)
    res = mine(rhs_c) - wide(step[...], width) * image
    z = mine(prec_c) * res
    put_products(sent, z.astype(BF16), c_ref, own_rows(width), width, places)
    core_own[...] = core_out
    z_own[...] = z
    rz_part[...] = rz_in[...] + lane_sum(res * z)
    cross_part[...] = cross_in[...] + lane_sum(z * image)


def rest_next_kernel(
    width, places, got, z_own, c_ref, z_n, dir_n, res_n, image_n, image_z, old_step, old_rz, old_curve,
    sent, step_out, factor_out, sol_n, res_n_out,
):
    pushed, tail = get_folded(got, width)
    put_products(sent, (z_own[...] - pushed).astype(BF16), c_ref, own_rows(width), width, places)
    curve_z, rz, cross = get_sums(tail, 3)
    factor = rz / old_rz[...]
    step = rz / (curve_z + factor * (2.0 * cross + factor * old_curve[...]))
    step_out[...] = step
    factor_out[...] = factor
    many = z_n.shape[1]
    sol_n[...] = wide(old_step[...] + step * factor, many) * dir_n[...] + wide(step, many) * z_n[...]
    res_n_out[...] = res_n[...] - wide(step, many) * (image_z[...] + wide(factor, many) * image_n[...])


def pair_kernel(got, core_own, both):
    traits = core_own.shape[0]
    both[:traits] = core_own[...]
    both[traits:] = jnp.sum(got[...].astype(F32), axis=0)


def final_kernel(
    groups, width, dir_c, rec_c, rhs_c, prec_c, tb, first, second, ratio, sol_n, res_n, *refs
):
    pieces, (sol_c_far, sol_n_far, res_c_far, res_n_far, sol_c, res_c, sems) = refs[:groups], refs[groups:]
    pairs = ((sol_n, sol_n_far), (res_n, res_n_far), (sol_c, sol_c_far), (res_c, res_c_far))
    copies = [pltpu.make_async_copy(near, far, sems.at[k]) for k, (near, far) in enumerate(pairs)]
    copies[0].start()
    copies[1].start()
    traits = dir_c.shape[0]
    early = wide(first[...] + second[...] * ratio[...], width)
    old, new, mixed = wide(first[...], width), wide(second[...], width), wide(ratio[...], width)
    here = lax.axis_index("grp")
    for block in range(groups):
        both = pieces[0][...]
        for k in range(1, groups):
            both = jnp.where(here == (block + k) % groups, pieces[k][...], both)
        at = slice(block * width, (block + 1) * width)
        image = rec_c[:, at] * dir_c[:, at] + trait_mix(tb, both[:traits])
        res = rhs_c[:, at] - old * image
        z = prec_c[:, at] * res
        sol_c[:, at] = early * dir_c[:, at] + new * z
        res_c[:, at] = res - new * (rec_c[:, at] * z + trait_mix(tb, both[traits:]) + mixed * image)
    copies[2].start()
    copies[3].start()
    for copy in copies:
        copy.wait()


def call(kernel, outs, scratch=(), out_spec=VMEM_SPEC):
    def run(*args):
        return pl.pallas_call(
            kernel,
            out_shape=[jax.ShapeDtypeStruct(shape, dtype) for shape, dtype in outs],
            in_specs=[VMEM_SPEC] * len(args),
            out_specs=[out_spec] * len(outs),
            scratch_shapes=list(scratch),
            compiler_params=pltpu.CompilerParams(vmem_limit_bytes=GRANT),
            cost_estimate=pl.CostEstimate(flops=WORK, transcendentals=WORK, bytes_accessed=2**20),
        )(*args)

    return run


def make_kernel_body(groups, cores):
    parts = groups * cores

    def exchange(blocks):
        return lax.all_to_all(blocks, ("x", "grp", "z", "y"), 0, 0, tiled=False)

    def body(rhs_c, rhs_n, rec_c, rec_n, core_inverse, block, m_inverse, t):
        traits, held = rhs_c.shape
        width = held // groups
        many = rhs_n.shape[1]
        m_row = m_inverse[None, :]
        core, non, own = ((traits, held), F32), ((traits, many), F32), ((traits, width), F32)
        lanes, mixer = ((1, LANES), F32), ((traits, traits * LANES), F32)
        plain = ((parts, traits, width), BF16)
        tailed = ((parts, 2, traits // 2 * width + LANES), BF16)
        near = ((traits, many), BF16)
        full = [pltpu.VMEM((traits, parts * width), BF16)]
        places = [
            ((z * 2 + y) * 2 + x) * groups + g
            for x in range(2) for g in range(groups) for z in range(cores // 4) for y in range(2)
        ]
        part = functools.partial

        (early,) = call(early_kernel, [((traits, LANES), F32)])()
        sent, dir_c, dir_n, rz, prec_c, prec_n, tb = call(
            part(begin_kernel, groups, width), [plain, core, non, lanes, core, non, mixer]
        )(rhs_c, rhs_n, rec_c, rec_n, m_row, t, early)
        pull = call(part(pull_kernel, width, places), [non, near, lanes], full)
        push = call(part(push_kernel, width, places), [tailed])

        sent, form = call(part(map_first_kernel, groups, width, places), [plain, lanes], full)(
            exchange(sent), core_inverse, dir_c, rec_c, tb
        )
        image_n, left, curve = pull(exchange(sent), block, m_row, dir_n, rec_n, form, tb)
        (sent,) = push(left, block, curve, rz)
        sent, step, rz, curve, res_n, z_n, rz_part, cross = call(
            part(rest_first_kernel, groups, width, places), [plain, lanes, lanes, lanes, non, non, lanes, lanes]
        )(exchange(sent), dir_c, core_inverse, rhs_n, image_n, prec_n)
        sent, core_own, z_own, rz_part, cross = call(
            part(step_kernel, groups, width, places), [plain, own, own, lanes, lanes]
        )(exchange(sent), core_inverse, dir_c, rec_c, rhs_c, prec_c, tb, step, rz_part, cross)

        sent, form = call(part(map_next_kernel, groups, width), [plain, lanes])(exchange(sent), z_own, rec_c, tb)
        image_z, left, curve_z = pull(exchange(sent), block, m_row, z_n, rec_n, form, tb)
        (sent,) = push(left, block, curve_z, rz_part, cross)
        sent, next_step, factor, sol_n, res_n = call(
            part(rest_next_kernel, width, places), [plain, lanes, lanes, non, non]
        )(exchange(sent), z_own, core_inverse, z_n, dir_n, res_n, image_n, image_z, step, rz, curve)
        (both,) = call(pair_kernel, [((2 * traits, width), F32)])(exchange(sent), core_own)
        pieces = [both]
        for k in range(1, groups):
            pieces.append(lax.ppermute(both, "grp", [(g, (g + k) % groups) for g in range(groups)]))
        scratch = [pltpu.VMEM(*core), pltpu.VMEM(*core), pltpu.SemaphoreType.DMA((4,))]
        return tuple(
            call(part(final_kernel, groups, width), [core, non, core, non], scratch, FAR_SPEC)(
                dir_c, rec_c, rhs_c, prec_c, tb, step, next_step, factor, sol_n, res_n, *pieces
            )
        )

    return body


def solution(mesh):
    groups, cores = mesh.shape["grp"], mesh.shape["cores"]
    fine = cores % 4 == 0
    if fine:
        mesh = jax.sharding.Mesh(mesh.devices.reshape(groups, cores // 4, 2, 2), ("grp", "z", "y", "x"))
        c = ("z", "y", "x")
    else:
        c = ("cores",)
    gc = ("grp",) + c
    in_specs = (P(None, c), P(None, gc), P(None, c), P(None, gc), P(c, None), P(gc, None), P(gc), P())
    out_specs = (P(None, c), P(None, gc), P(None, c), P(None, gc))

    def body(rhs_core, *rest):
        fits = fine and rhs_core.shape[1] % (groups * LANES) == 0 and rhs_core.shape[0] % 2 == 0
        make = make_kernel_body if fits else make_plain_body
        return make(groups, cores)(rhs_core, *rest)

    return jax.shard_map(body, mesh=mesh, in_specs=in_specs, out_specs=out_specs, check_vma=False)
```

```python
import functools

import jax
import jax.numpy as jnp
from jax import lax
from jax.experimental import pallas as pl
from jax.experimental.pallas import tpu as pltpu
from jax.sharding import PartitionSpec as P

ITERS = 2
AXES = ("z", "y", "x", "grp")


def split3(value):
    hi = lax.reduce_precision(value, 8, 7)
    mid = lax.reduce_precision(value - hi, 8, 7)
    low = value - hi - mid
    return jnp.stack([hi, mid, low]).astype(jnp.bfloat16)


def mix(trait_inverse, x):
    return sum(trait_inverse[:, s : s + 1] * x[s : s + 1, :] for s in range(x.shape[0]))


def make_plain_body(groups, cores):
    parts = groups * cores

    def exchange(blocks):
        return lax.all_to_all(blocks, AXES, 0, 0, tiled=False)

    def gather(own, scalars=()):
        traits, width = own.shape
        sent = own.astype(jnp.bfloat16)
        if scalars:
            row = jnp.concatenate([split3(s) for s in scalars])
            row = jnp.pad(row, (0, 128 - row.shape[0]))[None]
            sent = jnp.concatenate([sent, jnp.pad(row, ((0, traits - 1), (0, 0)))], axis=1)
        got = exchange(jnp.broadcast_to(sent[None], (parts,) + sent.shape))
        full = got[:, :, :width].transpose(1, 0, 2).reshape(traits, parts * width)
        if not scalars:
            return full
        tail = got[:, 0, width : width + 3 * len(scalars)].astype(jnp.float32)
        sums = tail.reshape(parts, len(scalars), 3).sum((0, 2))
        return full, sums

    def scatter(partial, width):
        traits = partial.shape[0]
        blocks = partial.astype(jnp.bfloat16).reshape(traits, parts, width).transpose(1, 0, 2)
        return exchange(blocks).astype(jnp.float32).sum(0)

    def times_rows(full, rows):
        return lax.dot_general(full, rows, (((1,), (1,)), ((), ())), preferred_element_type=jnp.float32)

    def body(rhs_core, rhs_non, rec_core, rec_non, core_inverse, block, m_inverse, trait_inverse):
        traits, held = rhs_core.shape
        width = held // groups
        at = lax.axis_index("grp") * width

        def mine(x):
            return lax.dynamic_slice_in_dim(x, at, width, axis=1)

        rows_mine = lax.dynamic_slice_in_dim(core_inverse, at, width, axis=0)
        m_row = m_inverse[None, :]
        trait_diag = jnp.diagonal(trait_inverse)[:, None]
        prec_core = 1.0 / (rec_core + trait_diag)
        prec_non = 1.0 / (rec_non + trait_diag * m_row)
        sol_core, sol_non = jnp.zeros_like(rhs_core), jnp.zeros_like(rhs_non)
        res_core, res_non = rhs_core, rhs_non
        z_core, z_non = prec_core * res_core, prec_non * res_non
        dir_core, dir_non = jnp.zeros_like(z_core), jnp.zeros_like(z_non)
        mapped = jnp.zeros((traits, width), jnp.float32)
        rz_old = None
        for iteration in range(ITERS):
            rz_part = jnp.sum(res_non * z_non) + jnp.sum(mine(res_core * z_core))
            z_full, (rz,) = gather(mine(z_core), (rz_part,))
            z_mapped = times_rows(z_full, rows_mine)
            if iteration:
                factor = rz / rz_old
                mapped = z_mapped + factor * mapped
                dir_core = z_core + factor * dir_core
                dir_non = z_non + factor * dir_non
            else:
                mapped, dir_core, dir_non = z_mapped, z_core, z_non
            rz_old = rz
            mapped_full = gather(mapped)
            scaled = m_row * (dir_non - times_rows(mapped_full, block))
            pushed = scatter(
                jnp.dot(scaled.astype(jnp.bfloat16), block, preferred_element_type=jnp.float32), width
            )
            remainder = mine(dir_core) - pushed
            image_non = rec_non * dir_non + mix(trait_inverse, scaled)
            curve_part = (
                jnp.sum(dir_non * image_non)
                + jnp.sum(mine(rec_core * dir_core * dir_core))
                + jnp.sum(mapped * mix(trait_inverse, remainder))
            )
            rem_full, (curve,) = gather(remainder, (curve_part,))
            core_out = times_rows(rem_full, core_inverse)
            image_core = rec_core * dir_core + mix(trait_inverse, core_out)
            step = rz / curve
            sol_core = sol_core + step * dir_core
            sol_non = sol_non + step * dir_non
            res_core = res_core - step * image_core
            res_non = res_non - step * image_non
            z_core, z_non = prec_core * res_core, prec_non * res_non
        return sol_core, sol_non, res_core, res_non

    return body

LANES = 128
F32 = jnp.float32
BF16 = jnp.bfloat16
VMEM_SPEC = pl.BlockSpec(memory_space=pltpu.VMEM)
FAR_SPEC = pl.BlockSpec(memory_space=pltpu.HBM)
GRANT = 20 * 2**20
WORK = 10**8


def lane_sum(x):
    row = jnp.sum(x, axis=0, keepdims=True)
    out = row[:, :LANES]
    for k in range(LANES, row.shape[1], LANES):
        out = out + row[:, k : k + LANES]
    return out


def all_lanes(x):
    shift = LANES // 2
    while shift:
        x = x + pltpu.roll(x, shift, 1)
        shift //= 2
    return x


def wide(x, lanes):
    return jnp.concatenate([x] * (lanes // LANES), axis=1) if lanes > LANES else x


def trait_mix(tb_ref, x):
    out = None
    for s in range(x.shape[0]):
        term = wide(tb_ref[:, s * LANES : (s + 1) * LANES], x.shape[1]) * x[s : s + 1, :]
        out = term if out is None else out + term
    return out


def rows_times(full_ref, rows):
    dims = (((1,), (1,)), ((), ()))
    piece = 2 * LANES
    if full_ref.shape[1] % piece or full_ref.shape[1] == piece:
        return lax.dot_general(full_ref[...], rows, dims, preferred_element_type=F32)
    left, right = [], []
    for n, k in enumerate(range(0, full_ref.shape[1], piece)):
        at = slice(k, k + piece)
        if n % 5 % 2 == 0:
            left.append(lax.dot_general(full_ref[:, at], rows[:, at], dims, preferred_element_type=F32))
        else:
            right.append(lax.dot_general(rows[:, at], full_ref[:, at], dims, preferred_element_type=F32))
    return sum(left[1:], left[0]) + sum(right[1:], right[0]).T


def put_full(full_ref, got_ref, first, width, places):
    traits = got_ref.shape[1]
    for r, place in enumerate(places):
        full_ref[first : first + traits, place * width : (place + 1) * width] = got_ref[r]


def put_products(sent_ref, left, rows_ref, at, width, places):
    for r, place in enumerate(places):
        rows = rows_ref[pl.ds(at, width), place * width : (place + 1) * width]
        sent_ref[r] = jnp.dot(left, rows, preferred_element_type=F32).astype(BF16)


def put_all(sent_ref, own, width):
    value = own.astype(BF16)
    sent_ref[:, :, :width] = jnp.broadcast_to(value[None], (sent_ref.shape[0],) + value.shape)


def tail_slot(shape, k):
    return lax.broadcasted_iota(jnp.int32, shape, 1) // (LANES // 4) == k


def put_sums(sent_ref, sums):
    width = sent_ref.shape[2] - LANES
    shape = (2, LANES)
    row = lax.broadcasted_iota(jnp.int32, shape, 0)
    tail = jnp.zeros(shape, F32)
    for k, value in enumerate(sums):
        value = value + pltpu.roll(value, LANES // 2, 1)
        value = value + pltpu.roll(value, LANES // 4, 1)
        high = value.astype(BF16).astype(F32)
        tail = jnp.where(tail_slot(shape, k), jnp.where(row == 0, high, value - high), tail)
    tail = tail.astype(BF16)
    sent_ref[:, :, width:] = jnp.broadcast_to(tail[None], (sent_ref.shape[0],) + shape)


def put_folded(sent_ref, left, rows_ref, width, places):
    for r, place in enumerate(places):
        part = jnp.dot(
            left, rows_ref[:, place * width : (place + 1) * width], preferred_element_type=F32
        ).astype(BF16)
        for k in range(part.shape[0] // 2):
            sent_ref[r, :, k * width : (k + 1) * width] = part[2 * k : 2 * k + 2]


def get_folded(got_ref, width):
    both = jnp.sum(got_ref[...].astype(F32), axis=0)
    pairs = (both.shape[1] - LANES) // width
    block = jnp.concatenate([both[:, k * width : (k + 1) * width] for k in range(pairs)], axis=0)
    return block, both[:, pairs * width : pairs * width + LANES]


def get_sums(tail, count):
    out = []
    for k in range(count):
        rows = all_lanes(jnp.where(tail_slot(tail.shape, k), tail, 0.0))
        out.append(rows[0:1] + rows[1:2])
    return out


def own_part(x, groups, width):
    part = x[:, :width]
    for k in range(1, groups):
        part = jnp.where(lax.axis_index("grp") == k, x[:, k * width : (k + 1) * width], part)
    return part


def early_kernel(out):
    out[...] = jnp.zeros_like(out)


def begin_kernel(
    groups, width, rhs_c, rhs_n, rec_c, rec_n, m_ref, t_ref, early, sent, dir_c, dir_n, rz, prec_c, prec_n, tb
):
    traits = t_ref.shape[0]
    row = lax.broadcasted_iota(jnp.int32, (traits, LANES), 0)
    diag = early[...]
    for s in range(traits):
        column = jnp.broadcast_to(t_ref[:, s : s + 1], (traits, LANES))
        tb[:, s * LANES : (s + 1) * LANES] = column
        diag = jnp.where(row == s, column, diag)
    part_c = 1.0 / (rec_c[...] + wide(diag, rec_c.shape[1]))
    z_c = part_c * rhs_c[...]
    put_all(sent, own_part(z_c, groups, width), width)
    part_n = 1.0 / (rec_n[...] + wide(diag, rec_n.shape[1]) * m_ref[...])
    z_n = part_n * rhs_n[...]
    prec_c[...] = part_c
    prec_n[...] = part_n
    dir_c[...] = z_c
    dir_n[...] = z_n
    rz[...] = lane_sum(rhs_n[...] * z_n) + lane_sum(own_part(rhs_c[...] * z_c, groups, width))


def own_rows(width):
    return pl.multiple_of(lax.axis_index("grp") * width, LANES)


def core_form(mapped, own, record, tb):
    return lane_sum(mapped * trait_mix(tb, own) + record * own * own)


def map_first_kernel(groups, width, places, got, c_ref, dir_c, rec_c, tb, sent, form, full):
    put_full(full, got, 0, width, places)
    out = rows_times(full, c_ref[pl.ds(own_rows(width), width), :])
    put_all(sent, out, width)
    form[...] = core_form(out, own_part(dir_c[...], groups, width), own_part(rec_c[...], groups, width), tb)


def map_next_kernel(groups, width, got, z_own, rec_c, tb, sent, form):
    out = jnp.sum(got[...].astype(F32), axis=0)
    put_all(sent, out, width)
    form[...] = core_form(out, z_own[...], own_part(rec_c[...], groups, width), tb)


def pull_kernel(width, places, got, g_ref, m_ref, vec_n, rec_n, form, tb, image_n, left, curve, full):
    put_full(full, got, 0, width, places)
    differ = vec_n[...] - rows_times(full, g_ref[...])
    scaled = m_ref[...] * differ
    left[...] = scaled.astype(BF16)
    mixed = trait_mix(tb, scaled)
    weighted = rec_n[...] * vec_n[...]
    image_n[...] = weighted + mixed
    curve[...] = form[...] + lane_sum(vec_n[...] * weighted + differ * mixed)


def push_kernel(width, places, left, g_ref, *others):
    sent, sums = others[-1], others[:-1]
    put_sums(sent, [one[...] for one in sums])
    put_folded(sent, left[...], g_ref, width, places)


def rest_first_kernel(
    groups, width, places, got, dir_c, c_ref, rhs_n, image_n, prec_n,
    sent, step_out, rz_out, curve_out, res_n_out, z_n_out, rz_part, cross_part,
):
    pushed, tail = get_folded(got, width)
    left = (own_part(dir_c[...], groups, width) - pushed).astype(BF16)
    put_products(sent, left, c_ref, own_rows(width), width, places)
    curve, rz = get_sums(tail, 2)
    step = rz / curve
    step_out[...] = step
    rz_out[...] = rz
    curve_out[...] = curve
    res_n = rhs_n[...] - wide(step, rhs_n.shape[1]) * image_n[...]
    z_n = prec_n[...] * res_n
    res_n_out[...] = res_n
    z_n_out[...] = z_n
    rz_part[...] = lane_sum(res_n * z_n)
    cross_part[...] = lane_sum(z_n * image_n[...])


def step_kernel(
    groups, width, places, got, c_ref, dir_c, rec_c, rhs_c, prec_c, tb, step, rz_in, cross_in,
    sent, core_own, z_own, rz_part, cross_part,
):
    def mine(ref):
        return own_part(ref[...], groups, width)

    core_out = jnp.sum(got[...].astype(F32), axis=0)
    image = mine(rec_c) * mine(dir_c) + trait_mix(tb, core_out)
    res = mine(rhs_c) - wide(step[...], width) * image
    z = mine(prec_c) * res
    put_products(sent, z.astype(BF16), c_ref, own_rows(width), width, places)
    core_own[...] = core_out
    z_own[...] = z
    rz_part[...] = rz_in[...] + lane_sum(res * z)
    cross_part[...] = cross_in[...] + lane_sum(z * image)


def rest_next_kernel(
    width, places, got, z_own, c_ref, z_n, dir_n, res_n, image_n, image_z, old_step, old_rz, old_curve,
    sent, step_out, factor_out, sol_n, res_n_out,
):
    pushed, tail = get_folded(got, width)
    put_products(sent, (z_own[...] - pushed).astype(BF16), c_ref, own_rows(width), width, places)
    curve_z, rz, cross = get_sums(tail, 3)
    factor = rz / old_rz[...]
    step = rz / (curve_z + factor * (2.0 * cross + factor * old_curve[...]))
    step_out[...] = step
    factor_out[...] = factor
    many = z_n.shape[1]
    sol_n[...] = wide(old_step[...] + step * factor, many) * dir_n[...] + wide(step, many) * z_n[...]
    res_n_out[...] = res_n[...] - wide(step, many) * (image_z[...] + wide(factor, many) * image_n[...])


def pair_kernel(got, core_own, both):
    traits = core_own.shape[0]
    both[:traits] = core_own[...]
    both[traits:] = jnp.sum(got[...].astype(F32), axis=0)


def final_kernel(
    groups, width, dir_c, rec_c, rhs_c, prec_c, tb, first, second, ratio, sol_n, res_n, *refs
):
    pieces, (sol_c_far, sol_n_far, res_c_far, res_n_far, sol_c, res_c, sems) = refs[:groups], refs[groups:]
    pairs = ((sol_n, sol_n_far), (res_n, res_n_far), (sol_c, sol_c_far), (res_c, res_c_far))
    copies = [pltpu.make_async_copy(near, far, sems.at[k]) for k, (near, far) in enumerate(pairs)]
    copies[0].start()
    copies[1].start()
    traits = dir_c.shape[0]
    early = wide(first[...] + second[...] * ratio[...], width)
    old, new, mixed = wide(first[...], width), wide(second[...], width), wide(ratio[...], width)
    here = lax.axis_index("grp")
    for block in range(groups):
        both = pieces[0][...]
        for k in range(1, groups):
            both = jnp.where(here == (block + k) % groups, pieces[k][...], both)
        at = slice(block * width, (block + 1) * width)
        image = rec_c[:, at] * dir_c[:, at] + trait_mix(tb, both[:traits])
        res = rhs_c[:, at] - old * image
        z = prec_c[:, at] * res
        sol_c[:, at] = early * dir_c[:, at] + new * z
        res_c[:, at] = res - new * (rec_c[:, at] * z + trait_mix(tb, both[traits:]) + mixed * image)
    copies[2].start()
    copies[3].start()
    for copy in copies:
        copy.wait()


def call(kernel, outs, scratch=(), out_spec=VMEM_SPEC):
    def run(*args):
        return pl.pallas_call(
            kernel,
            out_shape=[jax.ShapeDtypeStruct(shape, dtype) for shape, dtype in outs],
            in_specs=[VMEM_SPEC] * len(args),
            out_specs=[out_spec] * len(outs),
            scratch_shapes=list(scratch),
            compiler_params=pltpu.CompilerParams(vmem_limit_bytes=GRANT),
            cost_estimate=pl.CostEstimate(flops=WORK, transcendentals=WORK, bytes_accessed=2**20),
        )(*args)

    return run


def make_kernel_body(groups, cores):
    parts = groups * cores

    def exchange(blocks):
        return lax.all_to_all(blocks, ("y", "grp", "z", "x"), 0, 0, tiled=False)

    def body(rhs_c, rhs_n, rec_c, rec_n, core_inverse, block, m_inverse, t):
        traits, held = rhs_c.shape
        width = held // groups
        many = rhs_n.shape[1]
        m_row = m_inverse[None, :]
        core, non, own = ((traits, held), F32), ((traits, many), F32), ((traits, width), F32)
        lanes, mixer = ((1, LANES), F32), ((traits, traits * LANES), F32)
        plain = ((parts, traits, width), BF16)
        tailed = ((parts, 2, traits // 2 * width + LANES), BF16)
        near = ((traits, many), BF16)
        full = [pltpu.VMEM((traits, parts * width), BF16)]
        places = [
            ((z * 2 + y) * 2 + x) * groups + g
            for y in range(2) for g in range(groups) for z in range(cores // 4) for x in range(2)
        ]
        part = functools.partial

        (early,) = call(early_kernel, [((traits, LANES), F32)])()
        sent, dir_c, dir_n, rz, prec_c, prec_n, tb = call(
            part(begin_kernel, groups, width), [plain, core, non, lanes, core, non, mixer]
        )(rhs_c, rhs_n, rec_c, rec_n, m_row, t, early)
        pull = call(part(pull_kernel, width, places), [non, near, lanes], full)
        push = call(part(push_kernel, width, places), [tailed])

        sent, form = call(part(map_first_kernel, groups, width, places), [plain, lanes], full)(
            exchange(sent), core_inverse, dir_c, rec_c, tb
        )
        image_n, left, curve = pull(exchange(sent), block, m_row, dir_n, rec_n, form, tb)
        (sent,) = push(left, block, curve, rz)
        sent, step, rz, curve, res_n, z_n, rz_part, cross = call(
            part(rest_first_kernel, groups, width, places), [plain, lanes, lanes, lanes, non, non, lanes, lanes]
        )(exchange(sent), dir_c, core_inverse, rhs_n, image_n, prec_n)
        sent, core_own, z_own, rz_part, cross = call(
            part(step_kernel, groups, width, places), [plain, own, own, lanes, lanes]
        )(exchange(sent), core_inverse, dir_c, rec_c, rhs_c, prec_c, tb, step, rz_part, cross)

        sent, form = call(part(map_next_kernel, groups, width), [plain, lanes])(exchange(sent), z_own, rec_c, tb)
        image_z, left, curve_z = pull(exchange(sent), block, m_row, z_n, rec_n, form, tb)
        (sent,) = push(left, block, curve_z, rz_part, cross)
        sent, next_step, factor, sol_n, res_n = call(
            part(rest_next_kernel, width, places), [plain, lanes, lanes, non, non]
        )(exchange(sent), z_own, core_inverse, z_n, dir_n, res_n, image_n, image_z, step, rz, curve)
        (both,) = call(pair_kernel, [((2 * traits, width), F32)])(exchange(sent), core_own)
        pieces = [both]
        for k in range(1, groups):
            pieces.append(lax.ppermute(both, "grp", [(g, (g + k) % groups) for g in range(groups)]))
        scratch = [pltpu.VMEM(*core), pltpu.VMEM(*core), pltpu.SemaphoreType.DMA((4,))]
        return tuple(
            call(part(final_kernel, groups, width), [core, non, core, non], scratch, FAR_SPEC)(
                dir_c, rec_c, rhs_c, prec_c, tb, step, next_step, factor, sol_n, res_n, *pieces
            )
        )

    return body


def solution(mesh):
    groups, cores = mesh.shape["grp"], mesh.shape["cores"]
    fine = cores % 4 == 0
    if fine:
        mesh = jax.sharding.Mesh(mesh.devices.reshape(groups, cores // 4, 2, 2), ("grp", "z", "y", "x"))
        c = ("z", "y", "x")
    else:
        c = ("cores",)
    gc = ("grp",) + c
    in_specs = (P(None, c), P(None, gc), P(None, c), P(None, gc), P(c, None), P(gc, None), P(gc), P())
    out_specs = (P(None, c), P(None, gc), P(None, c), P(None, gc))

    def body(rhs_core, *rest):
        fits = fine and rhs_core.shape[1] % (groups * LANES) == 0 and rhs_core.shape[0] % 2 == 0
        make = make_kernel_body if fits else make_plain_body
        return make(groups, cores)(rhs_core, *rest)

    return jax.shard_map(body, mesh=mesh, in_specs=in_specs, out_specs=out_specs, check_vma=False)
```

```python
import functools

import jax
import jax.numpy as jnp
from jax import lax
from jax.experimental import pallas as pl
from jax.experimental.pallas import tpu as pltpu
from jax.sharding import PartitionSpec as P

ITERS = 2
AXES = ("z", "y", "x", "grp")


def split3(value):
    hi = lax.reduce_precision(value, 8, 7)
    mid = lax.reduce_precision(value - hi, 8, 7)
    low = value - hi - mid
    return jnp.stack([hi, mid, low]).astype(jnp.bfloat16)


def mix(trait_inverse, x):
    return sum(trait_inverse[:, s : s + 1] * x[s : s + 1, :] for s in range(x.shape[0]))


def make_plain_body(groups, cores):
    parts = groups * cores

    def exchange(blocks):
        return lax.all_to_all(blocks, AXES, 0, 0, tiled=False)

    def gather(own, scalars=()):
        traits, width = own.shape
        sent = own.astype(jnp.bfloat16)
        if scalars:
            row = jnp.concatenate([split3(s) for s in scalars])
            row = jnp.pad(row, (0, 128 - row.shape[0]))[None]
            sent = jnp.concatenate([sent, jnp.pad(row, ((0, traits - 1), (0, 0)))], axis=1)
        got = exchange(jnp.broadcast_to(sent[None], (parts,) + sent.shape))
        full = got[:, :, :width].transpose(1, 0, 2).reshape(traits, parts * width)
        if not scalars:
            return full
        tail = got[:, 0, width : width + 3 * len(scalars)].astype(jnp.float32)
        sums = tail.reshape(parts, len(scalars), 3).sum((0, 2))
        return full, sums

    def scatter(partial, width):
        traits = partial.shape[0]
        blocks = partial.astype(jnp.bfloat16).reshape(traits, parts, width).transpose(1, 0, 2)
        return exchange(blocks).astype(jnp.float32).sum(0)

    def times_rows(full, rows):
        return lax.dot_general(full, rows, (((1,), (1,)), ((), ())), preferred_element_type=jnp.float32)

    def body(rhs_core, rhs_non, rec_core, rec_non, core_inverse, block, m_inverse, trait_inverse):
        traits, held = rhs_core.shape
        width = held // groups
        at = lax.axis_index("grp") * width

        def mine(x):
            return lax.dynamic_slice_in_dim(x, at, width, axis=1)

        rows_mine = lax.dynamic_slice_in_dim(core_inverse, at, width, axis=0)
        m_row = m_inverse[None, :]
        trait_diag = jnp.diagonal(trait_inverse)[:, None]
        prec_core = 1.0 / (rec_core + trait_diag)
        prec_non = 1.0 / (rec_non + trait_diag * m_row)
        sol_core, sol_non = jnp.zeros_like(rhs_core), jnp.zeros_like(rhs_non)
        res_core, res_non = rhs_core, rhs_non
        z_core, z_non = prec_core * res_core, prec_non * res_non
        dir_core, dir_non = jnp.zeros_like(z_core), jnp.zeros_like(z_non)
        mapped = jnp.zeros((traits, width), jnp.float32)
        rz_old = None
        for iteration in range(ITERS):
            rz_part = jnp.sum(res_non * z_non) + jnp.sum(mine(res_core * z_core))
            z_full, (rz,) = gather(mine(z_core), (rz_part,))
            z_mapped = times_rows(z_full, rows_mine)
            if iteration:
                factor = rz / rz_old
                mapped = z_mapped + factor * mapped
                dir_core = z_core + factor * dir_core
                dir_non = z_non + factor * dir_non
            else:
                mapped, dir_core, dir_non = z_mapped, z_core, z_non
            rz_old = rz
            mapped_full = gather(mapped)
            scaled = m_row * (dir_non - times_rows(mapped_full, block))
            pushed = scatter(
                jnp.dot(scaled.astype(jnp.bfloat16), block, preferred_element_type=jnp.float32), width
            )
            remainder = mine(dir_core) - pushed
            image_non = rec_non * dir_non + mix(trait_inverse, scaled)
            curve_part = (
                jnp.sum(dir_non * image_non)
                + jnp.sum(mine(rec_core * dir_core * dir_core))
                + jnp.sum(mapped * mix(trait_inverse, remainder))
            )
            rem_full, (curve,) = gather(remainder, (curve_part,))
            core_out = times_rows(rem_full, core_inverse)
            image_core = rec_core * dir_core + mix(trait_inverse, core_out)
            step = rz / curve
            sol_core = sol_core + step * dir_core
            sol_non = sol_non + step * dir_non
            res_core = res_core - step * image_core
            res_non = res_non - step * image_non
            z_core, z_non = prec_core * res_core, prec_non * res_non
        return sol_core, sol_non, res_core, res_non

    return body

LANES = 128
F32 = jnp.float32
BF16 = jnp.bfloat16
VMEM_SPEC = pl.BlockSpec(memory_space=pltpu.VMEM)
FAR_SPEC = pl.BlockSpec(memory_space=pltpu.HBM)
GRANT = 20 * 2**20
WORK = 10**8


def lane_sum(x):
    row = jnp.sum(x, axis=0, keepdims=True)
    out = row[:, :LANES]
    for k in range(LANES, row.shape[1], LANES):
        out = out + row[:, k : k + LANES]
    return out


def all_lanes(x):
    shift = LANES // 2
    while shift:
        x = x + pltpu.roll(x, shift, 1)
        shift //= 2
    return x


def wide(x, lanes):
    return jnp.concatenate([x] * (lanes // LANES), axis=1) if lanes > LANES else x


def trait_mix(tb_ref, x):
    out = None
    for s in range(x.shape[0]):
        term = wide(tb_ref[:, s * LANES : (s + 1) * LANES], x.shape[1]) * x[s : s + 1, :]
        out = term if out is None else out + term
    return out


def rows_times(full_ref, rows):
    dims = (((1,), (1,)), ((), ()))
    piece = 2 * LANES
    if full_ref.shape[1] % piece or full_ref.shape[1] == piece:
        return lax.dot_general(full_ref[...], rows, dims, preferred_element_type=F32)
    left, right = [], []
    for n, k in enumerate(range(0, full_ref.shape[1], piece)):
        at = slice(k, k + piece)
        if n % 9 % 2 == 0:
            left.append(lax.dot_general(full_ref[:, at], rows[:, at], dims, preferred_element_type=F32))
        else:
            right.append(lax.dot_general(rows[:, at], full_ref[:, at], dims, preferred_element_type=F32))
    return sum(left[1:], left[0]) + sum(right[1:], right[0]).T


def put_full(full_ref, got_ref, first, width, places):
    traits = got_ref.shape[1]
    for r, place in enumerate(places):
        full_ref[first : first + traits, place * width : (place + 1) * width] = got_ref[r]


def put_products(sent_ref, left, rows_ref, at, width, places):
    for r, place in enumerate(places):
        rows = rows_ref[pl.ds(at, width), place * width : (place + 1) * width]
        sent_ref[r] = jnp.dot(left, rows, preferred_element_type=F32).astype(BF16)


def put_all(sent_ref, own, width):
    value = own.astype(BF16)
    sent_ref[:, :, :width] = jnp.broadcast_to(value[None], (sent_ref.shape[0],) + value.shape)


def tail_slot(shape, k):
    return lax.broadcasted_iota(jnp.int32, shape, 1) // (LANES // 4) == k


def put_sums(sent_ref, sums):
    width = sent_ref.shape[2] - LANES
    shape = (2, LANES)
    row = lax.broadcasted_iota(jnp.int32, shape, 0)
    tail = jnp.zeros(shape, F32)
    for k, value in enumerate(sums):
        value = value + pltpu.roll(value, LANES // 2, 1)
        value = value + pltpu.roll(value, LANES // 4, 1)
        high = value.astype(BF16).astype(F32)
        tail = jnp.where(tail_slot(shape, k), jnp.where(row == 0, high, value - high), tail)
    tail = tail.astype(BF16)
    sent_ref[:, :, width:] = jnp.broadcast_to(tail[None], (sent_ref.shape[0],) + shape)


def put_folded(sent_ref, left, rows_ref, width, places):
    for r, place in enumerate(places):
        part = jnp.dot(
            left, rows_ref[:, place * width : (place + 1) * width], preferred_element_type=F32
        ).astype(BF16)
        for k in range(part.shape[0] // 2):
            sent_ref[r, :, k * width : (k + 1) * width] = part[2 * k : 2 * k + 2]


def get_folded(got_ref, width):
    both = jnp.sum(got_ref[...].astype(F32), axis=0)
    pairs = (both.shape[1] - LANES) // width
    block = jnp.concatenate([both[:, k * width : (k + 1) * width] for k in range(pairs)], axis=0)
    return block, both[:, pairs * width : pairs * width + LANES]


def get_sums(tail, count):
    out = []
    for k in range(count):
        rows = all_lanes(jnp.where(tail_slot(tail.shape, k), tail, 0.0))
        out.append(rows[0:1] + rows[1:2])
    return out


def own_part(x, groups, width):
    part = x[:, :width]
    for k in range(1, groups):
        part = jnp.where(lax.axis_index("grp") == k, x[:, k * width : (k + 1) * width], part)
    return part


def early_kernel(out):
    out[...] = jnp.zeros_like(out)


def begin_kernel(
    groups, width, rhs_c, rhs_n, rec_c, rec_n, m_ref, t_ref, early, sent, dir_c, dir_n, rz, prec_c, prec_n, tb
):
    traits = t_ref.shape[0]
    row = lax.broadcasted_iota(jnp.int32, (traits, LANES), 0)
    diag = early[...]
    for s in range(traits):
        column = jnp.broadcast_to(t_ref[:, s : s + 1], (traits, LANES))
        tb[:, s * LANES : (s + 1) * LANES] = column
        diag = jnp.where(row == s, column, diag)
    part_c = 1.0 / (rec_c[...] + wide(diag, rec_c.shape[1]))
    z_c = part_c * rhs_c[...]
    put_all(sent, own_part(z_c, groups, width), width)
    part_n = 1.0 / (rec_n[...] + wide(diag, rec_n.shape[1]) * m_ref[...])
    z_n = part_n * rhs_n[...]
    prec_c[...] = part_c
    prec_n[...] = part_n
    dir_c[...] = z_c
    dir_n[...] = z_n
    rz[...] = lane_sum(rhs_n[...] * z_n) + lane_sum(own_part(rhs_c[...] * z_c, groups, width))


def own_rows(width):
    return pl.multiple_of(lax.axis_index("grp") * width, LANES)


def core_form(mapped, own, record, tb):
    return lane_sum(mapped * trait_mix(tb, own) + record * own * own)


def map_first_kernel(groups, width, places, got, c_ref, dir_c, rec_c, tb, sent, form, full):
    put_full(full, got, 0, width, places)
    out = rows_times(full, c_ref[pl.ds(own_rows(width), width), :])
    put_all(sent, out, width)
    form[...] = core_form(out, own_part(dir_c[...], groups, width), own_part(rec_c[...], groups, width), tb)


def map_next_kernel(groups, width, got, z_own, rec_c, tb, sent, form):
    out = jnp.sum(got[...].astype(F32), axis=0)
    put_all(sent, out, width)
    form[...] = core_form(out, z_own[...], own_part(rec_c[...], groups, width), tb)


def pull_kernel(width, places, got, g_ref, m_ref, vec_n, rec_n, form, tb, image_n, left, curve, full):
    put_full(full, got, 0, width, places)
    differ = vec_n[...] - rows_times(full, g_ref[...])
    scaled = m_ref[...] * differ
    left[...] = scaled.astype(BF16)
    mixed = trait_mix(tb, scaled)
    weighted = rec_n[...] * vec_n[...]
    image_n[...] = weighted + mixed
    curve[...] = form[...] + lane_sum(vec_n[...] * weighted + differ * mixed)


def push_kernel(width, places, left, g_ref, *others):
    sent, sums = others[-1], others[:-1]
    put_sums(sent, [one[...] for one in sums])
    put_folded(sent, left[...], g_ref, width, places)


def rest_first_kernel(
    groups, width, places, got, dir_c, c_ref, rhs_n, image_n, prec_n,
    sent, step_out, rz_out, curve_out, res_n_out, z_n_out, rz_part, cross_part,
):
    pushed, tail = get_folded(got, width)
    left = (own_part(dir_c[...], groups, width) - pushed).astype(BF16)
    put_products(sent, left, c_ref, own_rows(width), width, places)
    curve, rz = get_sums(tail, 2)
    step = rz / curve
    step_out[...] = step
    rz_out[...] = rz
    curve_out[...] = curve
    res_n = rhs_n[...] - wide(step, rhs_n.shape[1]) * image_n[...]
    z_n = prec_n[...] * res_n
    res_n_out[...] = res_n
    z_n_out[...] = z_n
    rz_part[...] = lane_sum(res_n * z_n)
    cross_part[...] = lane_sum(z_n * image_n[...])


def step_kernel(
    groups, width, places, got, c_ref, dir_c, rec_c, rhs_c, prec_c, tb, step, rz_in, cross_in,
    sent, core_own, z_own, rz_part, cross_part,
):
    def mine(ref):
        return own_part(ref[...], groups, width)

    core_out = jnp.sum(got[...].astype(F32), axis=0)
    image = mine(rec_c) * mine(dir_c) + trait_mix(tb, core_out)
    res = mine(rhs_c) - wide(step[...], width) * image
    z = mine(prec_c) * res
    put_products(sent, z.astype(BF16), c_ref, own_rows(width), width, places)
    core_own[...] = core_out
    z_own[...] = z
    rz_part[...] = rz_in[...] + lane_sum(res * z)
    cross_part[...] = cross_in[...] + lane_sum(z * image)


def rest_next_kernel(
    width, places, got, z_own, c_ref, z_n, dir_n, res_n, image_n, image_z, old_step, old_rz, old_curve,
    sent, step_out, factor_out, sol_n, res_n_out,
):
    pushed, tail = get_folded(got, width)
    put_products(sent, (z_own[...] - pushed).astype(BF16), c_ref, own_rows(width), width, places)
    curve_z, rz, cross = get_sums(tail, 3)
    factor = rz / old_rz[...]
    step = rz / (curve_z + factor * (2.0 * cross + factor * old_curve[...]))
    step_out[...] = step
    factor_out[...] = factor
    many = z_n.shape[1]
    sol_n[...] = wide(old_step[...] + step * factor, many) * dir_n[...] + wide(step, many) * z_n[...]
    res_n_out[...] = res_n[...] - wide(step, many) * (image_z[...] + wide(factor, many) * image_n[...])


def pair_kernel(got, core_own, both):
    traits = core_own.shape[0]
    both[:traits] = core_own[...]
    both[traits:] = jnp.sum(got[...].astype(F32), axis=0)


def final_kernel(
    groups, width, dir_c, rec_c, rhs_c, prec_c, tb, first, second, ratio, sol_n, res_n, *refs
):
    pieces, (sol_c_far, sol_n_far, res_c_far, res_n_far, sol_c, res_c, sems) = refs[:groups], refs[groups:]
    pairs = ((sol_n, sol_n_far), (res_n, res_n_far), (sol_c, sol_c_far), (res_c, res_c_far))
    copies = [pltpu.make_async_copy(near, far, sems.at[k]) for k, (near, far) in enumerate(pairs)]
    copies[0].start()
    copies[1].start()
    traits = dir_c.shape[0]
    early = wide(first[...] + second[...] * ratio[...], width)
    old, new, mixed = wide(first[...], width), wide(second[...], width), wide(ratio[...], width)
    here = lax.axis_index("grp")
    for block in range(groups):
        both = pieces[0][...]
        for k in range(1, groups):
            both = jnp.where(here == (block + k) % groups, pieces[k][...], both)
        at = slice(block * width, (block + 1) * width)
        image = rec_c[:, at] * dir_c[:, at] + trait_mix(tb, both[:traits])
        res = rhs_c[:, at] - old * image
        z = prec_c[:, at] * res
        sol_c[:, at] = early * dir_c[:, at] + new * z
        res_c[:, at] = res - new * (rec_c[:, at] * z + trait_mix(tb, both[traits:]) + mixed * image)
    copies[2].start()
    copies[3].start()
    for copy in copies:
        copy.wait()


def call(kernel, outs, scratch=(), out_spec=VMEM_SPEC):
    def run(*args):
        return pl.pallas_call(
            kernel,
            out_shape=[jax.ShapeDtypeStruct(shape, dtype) for shape, dtype in outs],
            in_specs=[VMEM_SPEC] * len(args),
            out_specs=[out_spec] * len(outs),
            scratch_shapes=list(scratch),
            compiler_params=pltpu.CompilerParams(vmem_limit_bytes=GRANT),
            cost_estimate=pl.CostEstimate(flops=WORK, transcendentals=WORK, bytes_accessed=2**20),
        )(*args)

    return run


def make_kernel_body(groups, cores):
    parts = groups * cores

    def exchange(blocks):
        return lax.all_to_all(blocks, ("y", "grp", "z", "x"), 0, 0, tiled=False)

    def body(rhs_c, rhs_n, rec_c, rec_n, core_inverse, block, m_inverse, t):
        traits, held = rhs_c.shape
        width = held // groups
        many = rhs_n.shape[1]
        m_row = m_inverse[None, :]
        core, non, own = ((traits, held), F32), ((traits, many), F32), ((traits, width), F32)
        lanes, mixer = ((1, LANES), F32), ((traits, traits * LANES), F32)
        plain = ((parts, traits, width), BF16)
        tailed = ((parts, 2, traits // 2 * width + LANES), BF16)
        near = ((traits, many), BF16)
        full = [pltpu.VMEM((traits, parts * width), BF16)]
        places = [
            ((z * 2 + y) * 2 + x) * groups + g
            for y in range(2) for g in range(groups) for z in range(cores // 4) for x in range(2)
        ]
        part = functools.partial

        (early,) = call(early_kernel, [((traits, LANES), F32)])()
        sent, dir_c, dir_n, rz, prec_c, prec_n, tb = call(
            part(begin_kernel, groups, width), [plain, core, non, lanes, core, non, mixer]
        )(rhs_c, rhs_n, rec_c, rec_n, m_row, t, early)
        pull = call(part(pull_kernel, width, places), [non, near, lanes], full)
        push = call(part(push_kernel, width, places), [tailed])

        sent, form = call(part(map_first_kernel, groups, width, places), [plain, lanes], full)(
            exchange(sent), core_inverse, dir_c, rec_c, tb
        )
        image_n, left, curve = pull(exchange(sent), block, m_row, dir_n, rec_n, form, tb)
        (sent,) = push(left, block, curve, rz)
        sent, step, rz, curve, res_n, z_n, rz_part, cross = call(
            part(rest_first_kernel, groups, width, places), [plain, lanes, lanes, lanes, non, non, lanes, lanes]
        )(exchange(sent), dir_c, core_inverse, rhs_n, image_n, prec_n)
        sent, core_own, z_own, rz_part, cross = call(
            part(step_kernel, groups, width, places), [plain, own, own, lanes, lanes]
        )(exchange(sent), core_inverse, dir_c, rec_c, rhs_c, prec_c, tb, step, rz_part, cross)

        sent, form = call(part(map_next_kernel, groups, width), [plain, lanes])(exchange(sent), z_own, rec_c, tb)
        image_z, left, curve_z = pull(exchange(sent), block, m_row, z_n, rec_n, form, tb)
        (sent,) = push(left, block, curve_z, rz_part, cross)
        sent, next_step, factor, sol_n, res_n = call(
            part(rest_next_kernel, width, places), [plain, lanes, lanes, non, non]
        )(exchange(sent), z_own, core_inverse, z_n, dir_n, res_n, image_n, image_z, step, rz, curve)
        (both,) = call(pair_kernel, [((2 * traits, width), F32)])(exchange(sent), core_own)
        pieces = [both]
        for k in range(1, groups):
            pieces.append(lax.ppermute(both, "grp", [(g, (g + k) % groups) for g in range(groups)]))
        scratch = [pltpu.VMEM(*core), pltpu.VMEM(*core), pltpu.SemaphoreType.DMA((4,))]
        return tuple(
            call(part(final_kernel, groups, width), [core, non, core, non], scratch, FAR_SPEC)(
                dir_c, rec_c, rhs_c, prec_c, tb, step, next_step, factor, sol_n, res_n, *pieces
            )
        )

    return body


def solution(mesh):
    groups, cores = mesh.shape["grp"], mesh.shape["cores"]
    fine = cores % 4 == 0
    if fine:
        mesh = jax.sharding.Mesh(mesh.devices.reshape(groups, cores // 4, 2, 2), ("grp", "z", "y", "x"))
        c = ("z", "y", "x")
    else:
        c = ("cores",)
    gc = ("grp",) + c
    in_specs = (P(None, c), P(None, gc), P(None, c), P(None, gc), P(c, None), P(gc, None), P(gc), P())
    out_specs = (P(None, c), P(None, gc), P(None, c), P(None, gc))

    def body(rhs_core, *rest):
        fits = fine and rhs_core.shape[1] % (groups * LANES) == 0 and rhs_core.shape[0] % 2 == 0
        make = make_kernel_body if fits else make_plain_body
        return make(groups, cores)(rhs_core, *rest)

    return jax.shard_map(body, mesh=mesh, in_specs=in_specs, out_specs=out_specs, check_vma=False)
```

```python
import functools

import jax
import jax.numpy as jnp
from jax import lax
from jax.experimental import pallas as pl
from jax.experimental.pallas import tpu as pltpu
from jax.sharding import PartitionSpec as P

ITERS = 2
AXES = ("z", "y", "x", "grp")


def split3(value):
    hi = lax.reduce_precision(value, 8, 7)
    mid = lax.reduce_precision(value - hi, 8, 7)
    low = value - hi - mid
    return jnp.stack([hi, mid, low]).astype(jnp.bfloat16)


def mix(trait_inverse, x):
    return sum(trait_inverse[:, s : s + 1] * x[s : s + 1, :] for s in range(x.shape[0]))


def make_plain_body(groups, cores):
    parts = groups * cores

    def exchange(blocks):
        return lax.all_to_all(blocks, AXES, 0, 0, tiled=False)

    def gather(own, scalars=()):
        traits, width = own.shape
        sent = own.astype(jnp.bfloat16)
        if scalars:
            row = jnp.concatenate([split3(s) for s in scalars])
            row = jnp.pad(row, (0, 128 - row.shape[0]))[None]
            sent = jnp.concatenate([sent, jnp.pad(row, ((0, traits - 1), (0, 0)))], axis=1)
        got = exchange(jnp.broadcast_to(sent[None], (parts,) + sent.shape))
        full = got[:, :, :width].transpose(1, 0, 2).reshape(traits, parts * width)
        if not scalars:
            return full
        tail = got[:, 0, width : width + 3 * len(scalars)].astype(jnp.float32)
        sums = tail.reshape(parts, len(scalars), 3).sum((0, 2))
        return full, sums

    def scatter(partial, width):
        traits = partial.shape[0]
        blocks = partial.astype(jnp.bfloat16).reshape(traits, parts, width).transpose(1, 0, 2)
        return exchange(blocks).astype(jnp.float32).sum(0)

    def times_rows(full, rows):
        return lax.dot_general(full, rows, (((1,), (1,)), ((), ())), preferred_element_type=jnp.float32)

    def body(rhs_core, rhs_non, rec_core, rec_non, core_inverse, block, m_inverse, trait_inverse):
        traits, held = rhs_core.shape
        width = held // groups
        at = lax.axis_index("grp") * width

        def mine(x):
            return lax.dynamic_slice_in_dim(x, at, width, axis=1)

        rows_mine = lax.dynamic_slice_in_dim(core_inverse, at, width, axis=0)
        m_row = m_inverse[None, :]
        trait_diag = jnp.diagonal(trait_inverse)[:, None]
        prec_core = 1.0 / (rec_core + trait_diag)
        prec_non = 1.0 / (rec_non + trait_diag * m_row)
        sol_core, sol_non = jnp.zeros_like(rhs_core), jnp.zeros_like(rhs_non)
        res_core, res_non = rhs_core, rhs_non
        z_core, z_non = prec_core * res_core, prec_non * res_non
        dir_core, dir_non = jnp.zeros_like(z_core), jnp.zeros_like(z_non)
        mapped = jnp.zeros((traits, width), jnp.float32)
        rz_old = None
        for iteration in range(ITERS):
            rz_part = jnp.sum(res_non * z_non) + jnp.sum(mine(res_core * z_core))
            z_full, (rz,) = gather(mine(z_core), (rz_part,))
            z_mapped = times_rows(z_full, rows_mine)
            if iteration:
                factor = rz / rz_old
                mapped = z_mapped + factor * mapped
                dir_core = z_core + factor * dir_core
                dir_non = z_non + factor * dir_non
            else:
                mapped, dir_core, dir_non = z_mapped, z_core, z_non
            rz_old = rz
            mapped_full = gather(mapped)
            scaled = m_row * (dir_non - times_rows(mapped_full, block))
            pushed = scatter(
                jnp.dot(scaled.astype(jnp.bfloat16), block, preferred_element_type=jnp.float32), width
            )
            remainder = mine(dir_core) - pushed
            image_non = rec_non * dir_non + mix(trait_inverse, scaled)
            curve_part = (
                jnp.sum(dir_non * image_non)
                + jnp.sum(mine(rec_core * dir_core * dir_core))
                + jnp.sum(mapped * mix(trait_inverse, remainder))
            )
            rem_full, (curve,) = gather(remainder, (curve_part,))
            core_out = times_rows(rem_full, core_inverse)
            image_core = rec_core * dir_core + mix(trait_inverse, core_out)
            step = rz / curve
            sol_core = sol_core + step * dir_core
            sol_non = sol_non + step * dir_non
            res_core = res_core - step * image_core
            res_non = res_non - step * image_non
            z_core, z_non = prec_core * res_core, prec_non * res_non
        return sol_core, sol_non, res_core, res_non

    return body

LANES = 128
F32 = jnp.float32
BF16 = jnp.bfloat16
VMEM_SPEC = pl.BlockSpec(memory_space=pltpu.VMEM)
FAR_SPEC = pl.BlockSpec(memory_space=pltpu.HBM)
GRANT = 20 * 2**20
WORK = 10**8


def lane_sum(x):
    row = jnp.sum(x, axis=0, keepdims=True)
    out = row[:, :LANES]
    for k in range(LANES, row.shape[1], LANES):
        out = out + row[:, k : k + LANES]
    return out


def all_lanes(x):
    shift = LANES // 2
    while shift:
        x = x + pltpu.roll(x, shift, 1)
        shift //= 2
    return x


def wide(x, lanes):
    return jnp.concatenate([x] * (lanes // LANES), axis=1) if lanes > LANES else x


def trait_mix(tb_ref, x):
    out = None
    for s in range(x.shape[0]):
        term = wide(tb_ref[:, s * LANES : (s + 1) * LANES], x.shape[1]) * x[s : s + 1, :]
        out = term if out is None else out + term
    return out


def rows_times(full_ref, rows):
    dims = (((1,), (1,)), ((), ()))
    piece = 2 * LANES
    if full_ref.shape[1] % piece or full_ref.shape[1] == piece:
        return lax.dot_general(full_ref[...], rows, dims, preferred_element_type=F32)
    left, right = [], []
    for n, k in enumerate(range(0, full_ref.shape[1], piece)):
        at = slice(k, k + piece)
        if n % 11 % 2 == 0:
            left.append(lax.dot_general(full_ref[:, at], rows[:, at], dims, preferred_element_type=F32))
        else:
            right.append(lax.dot_general(rows[:, at], full_ref[:, at], dims, preferred_element_type=F32))
    return sum(left[1:], left[0]) + sum(right[1:], right[0]).T


def put_full(full_ref, got_ref, first, width, places):
    traits = got_ref.shape[1]
    for r, place in enumerate(places):
        full_ref[first : first + traits, place * width : (place + 1) * width] = got_ref[r]


def put_products(sent_ref, left, rows_ref, at, width, places):
    for r, place in enumerate(places):
        rows = rows_ref[pl.ds(at, width), place * width : (place + 1) * width]
        sent_ref[r] = jnp.dot(left, rows, preferred_element_type=F32).astype(BF16)


def put_all(sent_ref, own, width):
    value = own.astype(BF16)
    sent_ref[:, :, :width] = jnp.broadcast_to(value[None], (sent_ref.shape[0],) + value.shape)


def tail_slot(shape, k):
    return lax.broadcasted_iota(jnp.int32, shape, 1) // (LANES // 4) == k


def put_sums(sent_ref, sums):
    width = sent_ref.shape[2] - LANES
    shape = (2, LANES)
    row = lax.broadcasted_iota(jnp.int32, shape, 0)
    tail = jnp.zeros(shape, F32)
    for k, value in enumerate(sums):
        value = value + pltpu.roll(value, LANES // 2, 1)
        value = value + pltpu.roll(value, LANES // 4, 1)
        high = value.astype(BF16).astype(F32)
        tail = jnp.where(tail_slot(shape, k), jnp.where(row == 0, high, value - high), tail)
    tail = tail.astype(BF16)
    sent_ref[:, :, width:] = jnp.broadcast_to(tail[None], (sent_ref.shape[0],) + shape)


def put_folded(sent_ref, left, rows_ref, width, places):
    for r, place in enumerate(places):
        part = jnp.dot(
            left, rows_ref[:, place * width : (place + 1) * width], preferred_element_type=F32
        ).astype(BF16)
        for k in range(part.shape[0] // 2):
            sent_ref[r, :, k * width : (k + 1) * width] = part[2 * k : 2 * k + 2]


def get_folded(got_ref, width):
    both = jnp.sum(got_ref[...].astype(F32), axis=0)
    pairs = (both.shape[1] - LANES) // width
    block = jnp.concatenate([both[:, k * width : (k + 1) * width] for k in range(pairs)], axis=0)
    return block, both[:, pairs * width : pairs * width + LANES]


def get_sums(tail, count):
    out = []
    for k in range(count):
        rows = all_lanes(jnp.where(tail_slot(tail.shape, k), tail, 0.0))
        out.append(rows[0:1] + rows[1:2])
    return out


def own_part(x, groups, width):
    part = x[:, :width]
    for k in range(1, groups):
        part = jnp.where(lax.axis_index("grp") == k, x[:, k * width : (k + 1) * width], part)
    return part


def early_kernel(out):
    out[...] = jnp.zeros_like(out)


def begin_kernel(
    groups, width, rhs_c, rhs_n, rec_c, rec_n, m_ref, t_ref, early, sent, dir_c, dir_n, rz, prec_c, prec_n, tb
):
    traits = t_ref.shape[0]
    row = lax.broadcasted_iota(jnp.int32, (traits, LANES), 0)
    diag = early[...]
    for s in range(traits):
        column = jnp.broadcast_to(t_ref[:, s : s + 1], (traits, LANES))
        tb[:, s * LANES : (s + 1) * LANES] = column
        diag = jnp.where(row == s, column, diag)
    part_c = 1.0 / (rec_c[...] + wide(diag, rec_c.shape[1]))
    z_c = part_c * rhs_c[...]
    put_all(sent, own_part(z_c, groups, width), width)
    part_n = 1.0 / (rec_n[...] + wide(diag, rec_n.shape[1]) * m_ref[...])
    z_n = part_n * rhs_n[...]
    prec_c[...] = part_c
    prec_n[...] = part_n
    dir_c[...] = z_c
    dir_n[...] = z_n
    rz[...] = lane_sum(rhs_n[...] * z_n) + lane_sum(own_part(rhs_c[...] * z_c, groups, width))


def own_rows(width):
    return pl.multiple_of(lax.axis_index("grp") * width, LANES)


def core_form(mapped, own, record, tb):
    return lane_sum(mapped * trait_mix(tb, own) + record * own * own)


def map_first_kernel(groups, width, places, got, c_ref, dir_c, rec_c, tb, sent, form, full):
    put_full(full, got, 0, width, places)
    out = rows_times(full, c_ref[pl.ds(own_rows(width), width), :])
    put_all(sent, out, width)
    form[...] = core_form(out, own_part(dir_c[...], groups, width), own_part(rec_c[...], groups, width), tb)


def map_next_kernel(groups, width, got, z_own, rec_c, tb, sent, form):
    out = jnp.sum(got[...].astype(F32), axis=0)
    put_all(sent, out, width)
    form[...] = core_form(out, z_own[...], own_part(rec_c[...], groups, width), tb)


def pull_kernel(width, places, got, g_ref, m_ref, vec_n, rec_n, form, tb, image_n, left, curve, full):
    put_full(full, got, 0, width, places)
    differ = vec_n[...] - rows_times(full, g_ref[...])
    scaled = m_ref[...] * differ
    left[...] = scaled.astype(BF16)
    mixed = trait_mix(tb, scaled)
    weighted = rec_n[...] * vec_n[...]
    image_n[...] = weighted + mixed
    curve[...] = form[...] + lane_sum(vec_n[...] * weighted + differ * mixed)


def push_kernel(width, places, left, g_ref, *others):
    sent, sums = others[-1], others[:-1]
    put_sums(sent, [one[...] for one in sums])
    put_folded(sent, left[...], g_ref, width, places)


def rest_first_kernel(
    groups, width, places, got, dir_c, c_ref, rhs_n, image_n, prec_n,
    sent, step_out, rz_out, curve_out, res_n_out, z_n_out, rz_part, cross_part,
):
    pushed, tail = get_folded(got, width)
    left = (own_part(dir_c[...], groups, width) - pushed).astype(BF16)
    put_products(sent, left, c_ref, own_rows(width), width, places)
    curve, rz = get_sums(tail, 2)
    step = rz / curve
    step_out[...] = step
    rz_out[...] = rz
    curve_out[...] = curve
    res_n = rhs_n[...] - wide(step, rhs_n.shape[1]) * image_n[...]
    z_n = prec_n[...] * res_n
    res_n_out[...] = res_n
    z_n_out[...] = z_n
    rz_part[...] = lane_sum(res_n * z_n)
    cross_part[...] = lane_sum(z_n * image_n[...])


def step_kernel(
    groups, width, places, got, c_ref, dir_c, rec_c, rhs_c, prec_c, tb, step, rz_in, cross_in,
    sent, core_own, z_own, rz_part, cross_part,
):
    def mine(ref):
        return own_part(ref[...], groups, width)

    core_out = jnp.sum(got[...].astype(F32), axis=0)
    image = mine(rec_c) * mine(dir_c) + trait_mix(tb, core_out)
    res = mine(rhs_c) - wide(step[...], width) * image
    z = mine(prec_c) * res
    put_products(sent, z.astype(BF16), c_ref, own_rows(width), width, places)
    core_own[...] = core_out
    z_own[...] = z
    rz_part[...] = rz_in[...] + lane_sum(res * z)
    cross_part[...] = cross_in[...] + lane_sum(z * image)


def rest_next_kernel(
    width, places, got, z_own, c_ref, z_n, dir_n, res_n, image_n, image_z, old_step, old_rz, old_curve,
    sent, step_out, factor_out, sol_n, res_n_out,
):
    pushed, tail = get_folded(got, width)
    put_products(sent, (z_own[...] - pushed).astype(BF16), c_ref, own_rows(width), width, places)
    curve_z, rz, cross = get_sums(tail, 3)
    factor = rz / old_rz[...]
    step = rz / (curve_z + factor * (2.0 * cross + factor * old_curve[...]))
    step_out[...] = step
    factor_out[...] = factor
    many = z_n.shape[1]
    sol_n[...] = wide(old_step[...] + step * factor, many) * dir_n[...] + wide(step, many) * z_n[...]
    res_n_out[...] = res_n[...] - wide(step, many) * (image_z[...] + wide(factor, many) * image_n[...])


def pair_kernel(got, core_own, both):
    traits = core_own.shape[0]
    both[:traits] = core_own[...]
    both[traits:] = jnp.sum(got[...].astype(F32), axis=0)


def final_kernel(
    groups, width, dir_c, rec_c, rhs_c, prec_c, tb, first, second, ratio, sol_n, res_n, *refs
):
    pieces, (sol_c_far, sol_n_far, res_c_far, res_n_far, sol_c, res_c, sems) = refs[:groups], refs[groups:]
    pairs = ((sol_n, sol_n_far), (res_n, res_n_far), (sol_c, sol_c_far), (res_c, res_c_far))
    copies = [pltpu.make_async_copy(near, far, sems.at[k]) for k, (near, far) in enumerate(pairs)]
    copies[0].start()
    copies[1].start()
    traits = dir_c.shape[0]
    early = wide(first[...] + second[...] * ratio[...], width)
    old, new, mixed = wide(first[...], width), wide(second[...], width), wide(ratio[...], width)
    here = lax.axis_index("grp")
    for block in range(groups):
        both = pieces[0][...]
        for k in range(1, groups):
            both = jnp.where(here == (block + k) % groups, pieces[k][...], both)
        at = slice(block * width, (block + 1) * width)
        image = rec_c[:, at] * dir_c[:, at] + trait_mix(tb, both[:traits])
        res = rhs_c[:, at] - old * image
        z = prec_c[:, at] * res
        sol_c[:, at] = early * dir_c[:, at] + new * z
        res_c[:, at] = res - new * (rec_c[:, at] * z + trait_mix(tb, both[traits:]) + mixed * image)
    copies[2].start()
    copies[3].start()
    for copy in copies:
        copy.wait()


def call(kernel, outs, scratch=(), out_spec=VMEM_SPEC):
    def run(*args):
        return pl.pallas_call(
            kernel,
            out_shape=[jax.ShapeDtypeStruct(shape, dtype) for shape, dtype in outs],
            in_specs=[VMEM_SPEC] * len(args),
            out_specs=[out_spec] * len(outs),
            scratch_shapes=list(scratch),
            compiler_params=pltpu.CompilerParams(vmem_limit_bytes=GRANT),
            cost_estimate=pl.CostEstimate(flops=WORK, transcendentals=WORK, bytes_accessed=2**20),
        )(*args)

    return run


def make_kernel_body(groups, cores):
    parts = groups * cores

    def exchange(blocks):
        return lax.all_to_all(blocks, ("y", "grp", "z", "x"), 0, 0, tiled=False)

    def body(rhs_c, rhs_n, rec_c, rec_n, core_inverse, block, m_inverse, t):
        traits, held = rhs_c.shape
        width = held // groups
        many = rhs_n.shape[1]
        m_row = m_inverse[None, :]
        core, non, own = ((traits, held), F32), ((traits, many), F32), ((traits, width), F32)
        lanes, mixer = ((1, LANES), F32), ((traits, traits * LANES), F32)
        plain = ((parts, traits, width), BF16)
        tailed = ((parts, 2, traits // 2 * width + LANES), BF16)
        near = ((traits, many), BF16)
        full = [pltpu.VMEM((traits, parts * width), BF16)]
        places = [
            ((z * 2 + y) * 2 + x) * groups + g
            for y in range(2) for g in range(groups) for z in range(cores // 4) for x in range(2)
        ]
        part = functools.partial

        (early,) = call(early_kernel, [((traits, LANES), F32)])()
        sent, dir_c, dir_n, rz, prec_c, prec_n, tb = call(
            part(begin_kernel, groups, width), [plain, core, non, lanes, core, non, mixer]
        )(rhs_c, rhs_n, rec_c, rec_n, m_row, t, early)
        pull = call(part(pull_kernel, width, places), [non, near, lanes], full)
        push = call(part(push_kernel, width, places), [tailed])

        sent, form = call(part(map_first_kernel, groups, width, places), [plain, lanes], full)(
            exchange(sent), core_inverse, dir_c, rec_c, tb
        )
        image_n, left, curve = pull(exchange(sent), block, m_row, dir_n, rec_n, form, tb)
        (sent,) = push(left, block, curve, rz)
        sent, step, rz, curve, res_n, z_n, rz_part, cross = call(
            part(rest_first_kernel, groups, width, places), [plain, lanes, lanes, lanes, non, non, lanes, lanes]
        )(exchange(sent), dir_c, core_inverse, rhs_n, image_n, prec_n)
        sent, core_own, z_own, rz_part, cross = call(
            part(step_kernel, groups, width, places), [plain, own, own, lanes, lanes]
        )(exchange(sent), core_inverse, dir_c, rec_c, rhs_c, prec_c, tb, step, rz_part, cross)

        sent, form = call(part(map_next_kernel, groups, width), [plain, lanes])(exchange(sent), z_own, rec_c, tb)
        image_z, left, curve_z = pull(exchange(sent), block, m_row, z_n, rec_n, form, tb)
        (sent,) = push(left, block, curve_z, rz_part, cross)
        sent, next_step, factor, sol_n, res_n = call(
            part(rest_next_kernel, width, places), [plain, lanes, lanes, non, non]
        )(exchange(sent), z_own, core_inverse, z_n, dir_n, res_n, image_n, image_z, step, rz, curve)
        (both,) = call(pair_kernel, [((2 * traits, width), F32)])(exchange(sent), core_own)
        pieces = [both]
        for k in range(1, groups):
            pieces.append(lax.ppermute(both, "grp", [(g, (g + k) % groups) for g in range(groups)]))
        scratch = [pltpu.VMEM(*core), pltpu.VMEM(*core), pltpu.SemaphoreType.DMA((4,))]
        return tuple(
            call(part(final_kernel, groups, width), [core, non, core, non], scratch, FAR_SPEC)(
                dir_c, rec_c, rhs_c, prec_c, tb, step, next_step, factor, sol_n, res_n, *pieces
            )
        )

    return body


def solution(mesh):
    groups, cores = mesh.shape["grp"], mesh.shape["cores"]
    fine = cores % 4 == 0
    if fine:
        mesh = jax.sharding.Mesh(mesh.devices.reshape(groups, cores // 4, 2, 2), ("grp", "z", "y", "x"))
        c = ("z", "y", "x")
    else:
        c = ("cores",)
    gc = ("grp",) + c
    in_specs = (P(None, c), P(None, gc), P(None, c), P(None, gc), P(c, None), P(gc, None), P(gc), P())
    out_specs = (P(None, c), P(None, gc), P(None, c), P(None, gc))

    def body(rhs_core, *rest):
        fits = fine and rhs_core.shape[1] % (groups * LANES) == 0 and rhs_core.shape[0] % 2 == 0
        make = make_kernel_body if fits else make_plain_body
        return make(groups, cores)(rhs_core, *rest)

    return jax.shard_map(body, mesh=mesh, in_specs=in_specs, out_specs=out_specs, check_vma=False)
```
